32 devices in a mesh: rep: 8 (over y, x, core), shard: 4 (over z).
Axes of the slice: x: 2, y: 2, z: 4, core: 2. Of those that a mesh axis runs over, the one named last changes fastest.
Arguments:
- inputs: bfloat16 [8, 4, 1104, 1024], P('rep', 'shard'), may hold values from -6 to 6
- counts: int32 [8], P('rep'), may hold values from 1 to 4, as said below
- ln1_gain: bfloat16 [1024], P('shard'), may hold values from 0.5 to 1.5
- ln1_shift: bfloat16 [1024], P('shard'), may hold values from -4 to 4
- w_qkv: bfloat16 [1024, 3072], P('shard'), may hold values from -0.1875 to 0.1875
- qv_bias: bfloat16 [2048], P('shard'), may hold values from -4 to 4
- w_out: bfloat16 [1024, 1024], P('shard'), may hold values from -0.75 to 0.75
- out_bias: bfloat16 [1024], P('shard'), may hold values from -4 to 4
- ln2_gain: bfloat16 [1024], P('shard'), may hold values from 0.5 to 1.5
- ln2_shift: bfloat16 [1024], P('shard'), may hold values from -4 to 4
- w_up: bfloat16 [1024, 4096], P('shard'), may hold values from -0.1875 to 0.1875
- up_bias: bfloat16 [4096], P('shard'), may hold values from -4 to 4
- w_down: bfloat16 [4096, 1024], P('shard'), may hold values from -0.09375 to 0.09375
- down_bias: bfloat16 [1024], P('shard'), may hold values from -4 to 4
- cotangent: bfloat16 [8, 4, 1104, 1024], P('rep', 'shard'), may hold values from -6 to 6
Outputs:
- output: bfloat16 [8, 4, 1104, 1024], P('rep', 'shard')
- input_grad: float32 [8, 4, 1104, 1024], P('rep', 'shard')
- grad_ln1_gain: float32 [1024], P('shard')
- grad_ln1_shift: float32 [1024], P('shard')
- grad_w_qkv: float32 [1024, 3072], P('shard')
- grad_qv_bias: float32 [2048], P('shard')
- grad_w_out: float32 [1024, 1024], P('shard')
- grad_out_bias: float32 [1024], P('shard')
- grad_ln2_gain: float32 [1024], P('shard')
- grad_ln2_shift: float32 [1024], P('shard')
- grad_w_up: float32 [1024, 4096], P('shard')
- grad_up_bias: float32 [4096], P('shard')
- grad_w_down: float32 [4096, 1024], P('shard')
- grad_down_bias: float32 [1024], P('shard')
The draws below stay inside these ranges and needn't reach their ends.
Inputs may be any that keep to these rules, and one draw needn't show every extreme that they name: A group's live sequences occupy its slots 0 to counts - 1; some group has exactly 4 and some exactly 1.
All inputs are finite; a program needn't handle non-finite values.
Results may differ from the reference program's by a relative error of at most 0.018.
Values may be sent and summed in bfloat16 or wider, within the bound.
No kernel may reach another device: no remote copies, remote signals or barrier semaphores. Data moves between devices by JAX's collectives and lax.ppermute only.
A program may use at most 256 MiB of HBM per device.

```python
import jax
import jax.numpy as jnp
from jax import lax

D = 1024
HEADS = 16
HDIM = 64
FF = 4096
SEQ = 1104
CAP = 4
GROUPS = 8


def draw_counts(key, part):
    key = jax.random.fold_in(key, 7)
    first_key, second_key = jax.random.split(key)
    drawn = jax.random.randint(first_key, (GROUPS,), 1, CAP + 1)
    order = jax.random.permutation(second_key, GROUPS)
    drawn = drawn.at[order[0]].set(CAP)
    drawn = drawn.at[order[1]].set(1)
    return drawn.astype(jnp.int32)


def steps_of(rng, dims, cuts, low, top_value):
    def one(dim, parts):
        heights = jax.random.uniform(jax.random.fold_in(jax.random.fold_in(rng, 6), dim), (parts,), jnp.float32, low / len(cuts), top_value / len(cuts))
        return jnp.repeat(jnp.exp(heights), dims[dim] // parts).reshape((-1,) + (1,) * (len(dims) - dim - 1))

    factor_of = one(*cuts[0])
    for cut in cuts[1:]:
        factor_of = factor_of * one(*cut)
    return factor_of


def centred(rng, extent, scale, reach, cuts=(), kind=jnp.bfloat16):
    level = steps_of(rng, extent, cuts, -0.22, 0.18) if cuts else 1.0
    values = jax.random.normal(rng, extent, jnp.float32) * scale * level
    return jnp.minimum(jnp.maximum(values, -reach), reach).astype(kind)


def setup_inputs(seed: int = 0) -> dict:
    key_list = jax.random.split(jax.random.key(seed), 16)
    inputs = centred(key_list[0], (GROUPS, CAP, SEQ, D), 1.0, 6.0, ((0, 8), (1, 4)))
    counts = draw_counts(jax.random.fold_in(key_list[15], 71), 0)
    ln1_gain = jnp.clip(1.0 + 0.1 * jax.random.normal(key_list[2], (D,), jnp.float32), 0.5, 1.5).astype(jnp.bfloat16)
    ln1_shift = centred(key_list[3], (D,), 0.3, 4.0, ((0, 4),))
    w_qkv = centred(key_list[4], (D, 3 * D), D ** -0.5, 0.1875, ((0, 4),))
    qv_bias = centred(key_list[5], (2 * D,), 0.3, 4.0, ((0, 4),))
    w_out = centred(key_list[6], (D, D), (D // 16) ** -0.5, 0.75, ((0, 4),))
    out_bias = centred(key_list[7], (D,), 0.3, 4.0, ((0, 4),))
    ln2_gain = jnp.clip(1.0 + 0.1 * jax.random.normal(key_list[8], (D,), jnp.float32), 0.5, 1.5).astype(jnp.bfloat16)
    ln2_shift = centred(key_list[9], (D,), 0.3, 4.0, ((0, 4),))
    w_up = centred(key_list[10], (D, FF), D ** -0.5, 0.1875, ((0, 4),))
    up_bias = centred(key_list[11], (FF,), 0.3, 4.0, ((0, 4),))
    w_down = centred(key_list[12], (FF, D), FF ** -0.5, 0.09375, ((0, 4),))
    down_bias = centred(key_list[13], (D,), 0.3, 4.0, ((0, 4),))
    cotangent = centred(key_list[14], (GROUPS, CAP, SEQ, D), 1.0, 6.0, ((0, 8), (1, 4)))
    return {"inputs": inputs, "counts": counts, "ln1_gain": ln1_gain, "ln1_shift": ln1_shift, "w_qkv": w_qkv, "qv_bias": qv_bias, "w_out": w_out, "out_bias": out_bias, "ln2_gain": ln2_gain, "ln2_shift": ln2_shift, "w_up": w_up, "up_bias": up_bias, "w_down": w_down, "down_bias": down_bias, "cotangent": cotangent}


@jax.custom_vjp
def low(v):
    return lax.optimization_barrier(v.astype(jnp.bfloat16)).astype(jnp.float32)

@jax.custom_vjp
def low_back(v):
    return v

def low_keep(v):
    return (low(v), None)

def low_pass(kept, grad):
    return (grad,)

def back_keep(v):
    return (v, None)

def back_low(kept, grad):
    return (low(grad),)
low.defvjp(low_keep, low_pass)
low_back.defvjp(back_keep, back_low)

def layer_norm(values, gain, shift):
    centre = values - lax.optimization_barrier(jnp.mean(values, -1, keepdims=True))
    spread = lax.optimization_barrier(jnp.mean(centre * centre, -1, keepdims=True))
    return centre * lax.rsqrt(spread + 1e-06) * gain + shift

def matmul(left, right):
    return jnp.dot(left, right, precision=lax.Precision.HIGHEST)

def attend(queries, keys, values):
    query_heads = queries.reshape(SEQ, HEADS, HDIM)
    key_heads = keys.reshape(SEQ, HEADS, HDIM)
    value_heads = values.reshape(SEQ, HEADS, HDIM)
    scores = jnp.einsum('qhd,khd->hqk', query_heads, key_heads, precision=lax.Precision.HIGHEST) * HDIM ** (-0.5)
    scores = low_back(scores)
    largest = lax.optimization_barrier(jnp.max(scores, -1, keepdims=True))
    exponent = jnp.exp(scores - largest)
    attn_probs = low(exponent / lax.optimization_barrier(jnp.sum(exponent, -1, keepdims=True)))
    mixed = jnp.einsum('hqk,khd->qhd', attn_probs, value_heads, precision=lax.Precision.HIGHEST)
    return mixed.reshape(SEQ, D)
attend_saved = jax.checkpoint(attend)

def block(tokens, params):
    ln1_gain, ln1_shift, w_qkv, qv_bias, w_out, out_bias, ln2_gain, ln2_shift, w_up, up_bias, w_down, down_bias = params
    hidden_one = low(layer_norm(tokens, ln1_gain, ln1_shift))
    full_bias = jnp.concatenate([qv_bias[:D], jnp.zeros((D,), jnp.float32), qv_bias[D:]])
    projected = low(low_back(matmul(hidden_one, w_qkv) + full_bias))
    attended = low(low_back(attend_saved(projected[:, :D], projected[:, D:2 * D], projected[:, 2 * D:])))
    middle = tokens + low_back(matmul(attended, w_out) + out_bias)
    hidden_two = low(layer_norm(middle, ln2_gain, ln2_shift))
    pre_act = low_back(matmul(hidden_two, w_up) + up_bias)
    activated = low(jax.nn.gelu(pre_act, approximate=False))
    return middle + matmul(activated, w_down) + down_bias

def reference(inputs, counts, ln1_gain, ln1_shift, w_qkv, qv_bias, w_out, out_bias, ln2_gain, ln2_shift, w_up, up_bias, w_down, down_bias, cotangent):
    params = tuple((p.astype(jnp.float32) for p in (ln1_gain, ln1_shift, w_qkv, qv_bias, w_out, out_bias, ln2_gain, ln2_shift, w_up, up_bias, w_down, down_bias)))
    sequences = inputs.reshape(GROUPS * CAP, SEQ, D)
    cot_seqs = cotangent.reshape(GROUPS * CAP, SEQ, D)
    alive = (jnp.arange(CAP, dtype=jnp.int32)[None, :] < counts[:, None]).reshape(GROUPS * CAP)
    zero_grads = tuple((jnp.zeros(p.shape, jnp.float32) for p in params))

    def one_sequence(running, sequence_item):
        seq_in, seq_cot, seq_alive = sequence_item

        def run_block(unused):
            result, backward = jax.vjp(block, seq_in.astype(jnp.float32), params)
            grad_in, grad_params = backward(seq_cot.astype(jnp.float32))
            return (result, grad_in, grad_params)

        def skip_block(unused):
            return (jnp.zeros((SEQ, D), jnp.float32), jnp.zeros((SEQ, D), jnp.float32), zero_grads)
        result, grad_in, grad_params = lax.cond(seq_alive, run_block, skip_block, 0)
        running = tuple((a + b for a, b in zip(running, grad_params)))
        return (running, (result, grad_in))
    grads, (results, input_grads) = lax.scan(one_sequence, zero_grads, (sequences, cot_seqs, alive))
    output = results.astype(jnp.bfloat16).reshape(GROUPS, CAP, SEQ, D)
    input_grad = input_grads.reshape(GROUPS, CAP, SEQ, D)
    return (output, input_grad, grads[0], grads[1], grads[2], grads[3], grads[4], grads[5], grads[6], grads[7], grads[8], grads[9], grads[10], grads[11])
```

```python
import functools

import jax
import jax.numpy as jnp
from jax import lax
from jax.experimental import pallas as pl
from jax.experimental.pallas import tpu as pltpu
from jax.sharding import PartitionSpec as P

HEADS = 16
HDIM = 64

eps = 1e-06
head_block = 4
bf16 = jnp.bfloat16
f32 = jnp.float32


def layer_norm(values, gain, shift):
    centre = values - jnp.mean(values, -1, keepdims=True)
    spread = jnp.mean(centre * centre, -1, keepdims=True)
    return centre * lax.rsqrt(spread + eps) * gain + shift


def gelu_exact(values):
    return jax.nn.gelu(values, approximate=False)


def matmul(left, right):
    return jnp.dot(left, right, preferred_element_type=f32)


def left_trans(left, right):
    return lax.dot_general(left, right, (((0,), (0,)), ((), ())), preferred_element_type=f32)


def right_trans(left, right):
    return lax.dot_general(left, right, (((1,), (1,)), ((), ())), preferred_element_type=f32)


class Links:
    def __init__(self, mesh):
        self.ns = mesh.shape["shard"]
        self.nr = mesh.shape["rep"]
        self.nq = self.nr // 2

    def here(self):
        rep = lax.axis_index("rep")
        return lax.axis_index("shard"), rep // 2, rep % 2

    def along(self, values, step):
        return lax.ppermute(values, "shard", [(i, (i + step) % self.ns) for i in range(self.ns)])

    def chip(self, values, k):
        return lax.ppermute(values, "rep", [(i, i ^ (2 * k)) for i in range(self.nr)])

    def core(self, values):
        return lax.ppermute(values, "rep", [(i, i ^ 1) for i in range(self.nr)])


def piece_of(links, weight):
    rows, cols = weight.shape
    _, q, c = links.here()
    rq, half = rows // links.nq, cols // 2
    return lax.dynamic_slice(weight, (q * rq, c * half), (rq, half))


def assemble(links, weights, own, crossed, mate):
    ns, nq = links.ns, links.nq
    rows = [w.shape[0] for w in weights]
    cols = [w.shape[1] for w in weights]
    rq = [r // nq for r in rows]

    def kernel(*refs):
        n = len(weights)
        w_refs = refs[:n]
        part_refs = refs[n : n + nq]
        mate_ref = refs[n + nq]
        out_refs = refs[n + nq + 1 : n + nq + 1 + n]
        sem = refs[-1]
        z = lax.axis_index("shard")
        rep = lax.axis_index("rep")
        q, c = rep // 2, rep % 2
        copies = []

        def go(src, dst):
            copy = pltpu.make_async_copy(src, dst, sem.at[len(copies)])
            copy.start()
            copies.append(copy)

        base = 0
        for i in range(n):
            half = cols[i] // 2
            go(w_refs[i], out_refs[i].at[pl.ds(pl.multiple_of(z * rows[i], rows[i]), rows[i]), :])
            mine = pl.ds(pl.multiple_of(c * half, half), half)
            other = pl.ds(pl.multiple_of((1 - c) * half, half), half)
            for s in range(1, ns):
                zs = lax.rem(z + (ns - s), ns)
                for k in range(nq):
                    at = pl.ds(pl.multiple_of(zs * rows[i] + (q ^ k) * rq[i], rq[i]), rq[i])
                    lanes = pl.ds(base, half)
                    go(part_refs[k].at[s - 1, :, lanes], out_refs[i].at[at, mine])
                    go(mate_ref.at[k, s - 1, :, lanes], out_refs[i].at[at, other])
            base += half
        for copy in copies:
            copy.wait()

    count = len(weights) * (1 + 2 * (ns - 1) * nq)
    anywhere = pl.BlockSpec(memory_space=pl.ANY)
    return pl.pallas_call(
        kernel,
        out_shape=[jax.ShapeDtypeStruct((ns * r, n), bf16) for r, n in zip(rows, cols)],
        in_specs=[anywhere] * (len(weights) + nq + 1),
        out_specs=[anywhere] * len(weights),
        scratch_shapes=[pltpu.SemaphoreType.DMA((count,))],
        name="assemble",
    )(*weights, own, *crossed, mate)


def gather(links, weights, extra=None):
    piece = jnp.concatenate([piece_of(links, w) for w in weights], 1)
    n = piece.shape[0]
    sent = piece if extra is None else jnp.concatenate([piece, extra], 0)
    got = [links.along(sent, s) for s in range(1, links.ns)]
    own = jnp.stack([g[:n] for g in got])
    crossed = [links.chip(own, k) for k in range(1, links.nq)]
    mate = links.core(jnp.stack([own] + crossed))
    full = assemble(links, weights, own, crossed, mate)
    if extra is None:
        return full
    return full, [g[n:] for g in got]


def scatter(links, sent, kept):
    ns, nq = links.ns, links.nq
    z, q, c = links.here()
    got = [links.core(s) for s in sent]
    rq = sent[0].shape[0] // (ns * nq)

    def view(values):
        return values.reshape(ns, nq, rq, values.shape[1])

    def part(k):
        pairs = [
            lax.dynamic_index_in_dim(view(a), q ^ k, 1, False).astype(f32)
            + lax.dynamic_index_in_dim(view(b), q ^ k, 1, False).astype(f32)
            for a, b in zip(kept, got)
        ]
        return jnp.concatenate(pairs, -1) if len(pairs) > 1 else pairs[0]

    crossed = [links.chip(part(k).astype(bf16), k) for k in range(1, nq)]
    total = part(0)
    for x in crossed:
        total = total + x.astype(f32)
    total = total.astype(bf16)
    moved = [
        links.along(lax.dynamic_index_in_dim(total, (z + s) % ns, 0, False), s)
        for s in range(1, ns)
    ]
    final = lax.dynamic_index_in_dim(total, z, 0, False).astype(f32)
    for x in moved:
        final = final + x.astype(f32)
    final = final.astype(bf16)
    mine = jnp.stack([final] + [links.chip(final, k) for k in range(1, nq)])
    mate = links.core(mine)
    first = jnp.where(c == 0, mine, mate)
    second = jnp.where(c == 0, mate, mine)
    outs = []
    base = 0
    for s in sent:
        half = s.shape[1]
        both = jnp.concatenate(
            [first[:, :, base : base + half], second[:, :, base : base + half]], -1
        )
        ordered = [lax.dynamic_index_in_dim(both, q ^ j, 0, False) for j in range(nq)]
        outs.append(jnp.concatenate(ordered).astype(f32))
        base += half
    return outs


def halves(links, left, right):
    _, _, c = links.here()
    half = right.shape[1] // 2
    away = lax.dynamic_slice_in_dim(right, (1 - c) * half, half, 1)
    home = lax.dynamic_slice_in_dim(right, c * half, half, 1)
    return left_trans(left, away).astype(bf16), left_trans(left, home).astype(bf16)


def body(
    links,
    inputs,
    counts,
    ln1_gain,
    ln1_shift,
    w_qkv,
    qv_bias,
    w_out,
    out_bias,
    ln2_gain,
    ln2_shift,
    w_up,
    up_bias,
    w_down,
    down_bias,
    cotangent,
):
    ns = links.ns
    slots = inputs.shape[1]
    seq_len = inputs.shape[2]
    width = inputs.shape[3]
    n_rows = slots * seq_len
    groups = HEADS // head_block
    scale = HDIM ** (-0.5)
    z = lax.axis_index("shard")

    small = (ln1_gain, ln1_shift, qv_bias, out_bias, ln2_gain, ln2_shift, up_bias, down_bias)
    sizes = [v.shape[0] for v in small]
    line = w_qkv.shape[1] // 2
    total_small = sum(sizes)
    n_lines = -(-total_small // line)
    packed = jnp.concatenate(small + (jnp.zeros((n_lines * line - total_small,), bf16),))
    packed = packed.reshape(n_lines, line)
    extra = jnp.concatenate([packed, jnp.zeros((16 - n_lines, line), bf16)])

    (full_qkv,), got_small = gather(links, [w_qkv], extra)
    all_small = jnp.stack([packed] + [g[:n_lines] for g in got_small]).reshape(ns, -1)
    all_small = jnp.concatenate(
        [lax.dynamic_index_in_dim(all_small, (z - j) % ns, 0) for j in range(ns)]
    )
    full_small = []
    base = 0
    for n in sizes:
        full_small.append(all_small[:, base : base + n].reshape(-1).astype(f32))
        base += n
    full_g1, full_s1, bias_f, full_bout, full_g2, full_s2, full_bup, full_bdown = full_small
    full_wout, full_wup = gather(links, [w_out, w_up])
    (full_wdown,) = gather(links, [w_down])

    first_slot = z * slots
    alive = (jnp.arange(slots, dtype=jnp.int32) + first_slot < counts[0]).astype(f32)
    alive_rows = jnp.broadcast_to(alive[:, None], (slots, seq_len)).reshape(n_rows, 1)
    tokens = inputs.reshape(n_rows, width).astype(f32)
    hidden_one, norm_one_back = jax.vjp(layer_norm, tokens, full_g1, full_s1)
    hidden_one_b = hidden_one.astype(bf16)
    projected = matmul(hidden_one_b, full_qkv)
    queries_b = (projected[:, :width] + bias_f[:width]).astype(bf16)
    keys_b = projected[:, width : 2 * width].astype(bf16)
    values_b = (projected[:, 2 * width :] + bias_f[width:]).astype(bf16)

    def arrange(values):
        return values.reshape(slots, seq_len, groups, head_block, HDIM).transpose(2, 0, 1, 3, 4)

    def restore(values):
        return values.transpose(1, 2, 0, 3, 4).reshape(n_rows, width)

    query_groups = arrange(queries_b)
    key_groups = arrange(keys_b)
    value_groups = arrange(values_b)

    def forward_group(operands):
        query_part, key_part, value_part = operands
        scores = (
            jnp.einsum("cqhd,ckhd->chqk", query_part, key_part, preferred_element_type=f32) * scale
        )
        largest = jnp.max(scores, -1, keepdims=True)
        exponent = jnp.exp(scores - largest)
        denominator = jnp.sum(exponent, -1, keepdims=True)
        probs_b = (exponent / denominator).astype(bf16)
        mixed = jnp.einsum("chqk,ckhd->cqhd", probs_b, value_part, preferred_element_type=f32)
        return (mixed, (largest + jnp.log(denominator))[..., 0])

    mixed_groups, log_totals = lax.map(forward_group, (query_groups, key_groups, value_groups))
    attended_b = restore(mixed_groups).astype(bf16)
    middle = tokens + matmul(attended_b, full_wout) + full_bout
    hidden_two, norm_two_back = jax.vjp(layer_norm, middle, full_g2, full_s2)
    hidden_two_b = hidden_two.astype(bf16)
    pre_act = matmul(hidden_two_b, full_wup) + full_bup
    activated, gelu_back = jax.vjp(gelu_exact, pre_act)
    activated_b = activated.astype(bf16)
    d_out = alive_rows * cotangent.reshape(n_rows, width).astype(f32)
    d_out_b = d_out.astype(bf16)
    grad_wdown = halves(links, activated_b, d_out_b)
    (o_wdown,) = scatter(links, [grad_wdown[0]], [grad_wdown[1]])
    result = middle + matmul(activated_b, full_wdown) + full_bdown
    output = (alive_rows * result).astype(bf16).reshape(inputs.shape)
    grad_bdown = jnp.sum(d_out, 0)
    d_act = right_trans(d_out_b, full_wdown)
    d_pre_b = gelu_back(d_act)[0].astype(bf16)
    grad_wup = halves(links, hidden_two_b, d_pre_b)
    grad_bup = jnp.sum(d_pre_b.astype(f32), 0)
    d_hidden_two = right_trans(d_pre_b, full_wup)
    d_mid_norm, grad_g2, grad_s2 = norm_two_back(d_hidden_two)
    d_mid = d_out + d_mid_norm
    d_proj_b = d_mid.astype(bf16)
    grad_wout = halves(links, attended_b, d_proj_b)
    o_wout, o_wup = scatter(links, [grad_wout[0], grad_wup[0]], [grad_wout[1], grad_wup[1]])
    grad_bout = jnp.sum(d_proj_b.astype(f32), 0)
    d_att_b = right_trans(d_proj_b, full_wout).astype(bf16)
    d_att_groups = arrange(d_att_b)

    def backward_group(operands):
        query_part, key_part, value_part, log_total, grad_part = operands
        scores = (
            jnp.einsum("cqhd,ckhd->chqk", query_part, key_part, preferred_element_type=f32) * scale
        )
        attn_probs = jnp.exp(scores - log_total[..., None])
        probs_b = attn_probs.astype(bf16)
        d_probs = jnp.einsum("cqhd,ckhd->chqk", grad_part, value_part, preferred_element_type=f32)
        row_inner = jnp.sum(d_probs * attn_probs, -1, keepdims=True)
        d_scores_b = (attn_probs * (d_probs - row_inner)).astype(bf16)
        d_query = (
            jnp.einsum("chqk,ckhd->cqhd", d_scores_b, key_part, preferred_element_type=f32) * scale
        )
        d_key = (
            jnp.einsum("chqk,cqhd->ckhd", d_scores_b, query_part, preferred_element_type=f32)
            * scale
        )
        d_value = jnp.einsum("chqk,cqhd->ckhd", probs_b, grad_part, preferred_element_type=f32)
        return (d_query, d_key, d_value)

    d_query_groups, d_key_groups, d_value_groups = lax.map(
        backward_group, (query_groups, key_groups, value_groups, log_totals, d_att_groups)
    )
    d_qkv_b = jnp.concatenate(
        [restore(d_query_groups), restore(d_key_groups), restore(d_value_groups)], 1
    ).astype(bf16)
    grad_qkv = halves(links, hidden_one_b, d_qkv_b)
    (o_qkv,) = scatter(links, [grad_qkv[0]], [grad_qkv[1]])
    column_sums = jnp.sum(d_qkv_b.astype(f32), 0)
    grad_qvb = jnp.concatenate([column_sums[:width], column_sums[2 * width :]])
    d_hidden_one = right_trans(d_qkv_b, full_qkv)
    d_in_norm, grad_g1, grad_s1 = norm_one_back(d_hidden_one)
    input_grad = (d_mid + d_in_norm).reshape(inputs.shape)
    small_grads = (grad_g1, grad_s1, grad_qvb, grad_bout, grad_g2, grad_s2, grad_bup, grad_bdown)
    joined = jnp.concatenate([g.reshape(ns, -1) for g in small_grads], 1)
    joined = lax.psum(joined, ("rep", "shard"))
    joined = lax.dynamic_index_in_dim(joined, z, 0, False)
    owned = []
    base = 0
    for n in sizes:
        owned.append(joined[base : base + n])
        base += n
    o_g1, o_s1, o_qvb, o_bout, o_g2, o_s2, o_bup, o_bdown = owned
    return (
        output,
        input_grad,
        o_g1,
        o_s1,
        o_qkv,
        o_qvb,
        o_wout,
        o_bout,
        o_g2,
        o_s2,
        o_wup,
        o_bup,
        o_wdown,
        o_bdown,
    )


def solution(mesh):
    tokens = P("rep", "shard", None, None)
    vector = P("shard")
    matrix = P("shard", None)
    return jax.shard_map(
        functools.partial(body, Links(mesh)),
        mesh=mesh,
        in_specs=(
            tokens,
            P("rep"),
            vector,
            vector,
            matrix,
            vector,
            matrix,
            vector,
            vector,
            vector,
            matrix,
            vector,
            matrix,
            vector,
            tokens,
        ),
        out_specs=(
            tokens,
            tokens,
            vector,
            vector,
            matrix,
            vector,
            matrix,
            vector,
            vector,
            vector,
            matrix,
            vector,
            matrix,
            vector,
        ),
        check_vma=False,
    )
```

```python
import functools

import jax
import jax.numpy as jnp
from jax import lax
from jax.experimental import pallas as pl
from jax.experimental.pallas import tpu as pltpu
from jax.sharding import PartitionSpec as P

HDIM = 64

eps = 1e-06
bf16 = jnp.bfloat16
f32 = jnp.float32


def layer_norm(values, gain, shift):
    centre = values - jnp.mean(values, -1, keepdims=True)
    spread = jnp.mean(centre * centre, -1, keepdims=True)
    return centre * lax.rsqrt(spread + eps) * gain + shift


def gelu_exact(values):
    return jax.nn.gelu(values, approximate=False)


def matmul(left, right):
    return jnp.dot(left, right, preferred_element_type=f32)


def left_trans(left, right):
    return lax.dot_general(left, right, (((0,), (0,)), ((), ())), preferred_element_type=f32)


def right_trans(left, right):
    return lax.dot_general(left, right, (((1,), (1,)), ((), ())), preferred_element_type=f32)


LOG2E = 1.4426950408889634


def contract(left, right, left_dim, right_dim):
    return lax.dot_general(
        left, right, (((left_dim,), (right_dim,)), ((), ())), preferred_element_type=f32
    )


def query_blocks(rows, tile=256):
    return [(i, min(tile, rows - i)) for i in range(0, rows, tile)]


def head_mask(head, rows, dtype):
    lane = lax.broadcasted_iota(jnp.int32, (rows, 2 * HDIM), 1)
    return (lane // HDIM == head).astype(dtype)


def attend_kernel(q_ref, k_ref, v_ref, o_ref, inv_ref, p_ref):
    rows = q_ref.shape[0]
    factor = HDIM ** (-0.5) * LOG2E
    keys = k_ref[...]
    values = v_ref[...]
    ones = jnp.ones(values.shape, bf16)
    for start, n in query_blocks(rows):
        queries = q_ref[start : start + n, :]
        mixed = inverse = None
        for head in range(2):
            mask = head_mask(head, rows, bf16)
            scores = contract(keys * mask, queries, 1, 1)
            largest = jnp.max(scores, axis=0, keepdims=True)
            probs = jnp.exp2((scores - largest) * factor).astype(bf16)
            p_ref[head, :, start : start + n] = probs
            both = contract(probs, jnp.concatenate([values * mask, ones], 1), 0, 0)
            inv = 1.0 / both[:, 2 * HDIM :]
            part = both[:, : 2 * HDIM] * inv
            share = head_mask(head, n, f32) * inv
            mixed = part if mixed is None else mixed + part
            inverse = share if inverse is None else inverse + share
        o_ref[start : start + n, :] = mixed.astype(bf16)
        inv_ref[start : start + n, :] = inverse


def attend(qkv):
    rows, wide = qkv.shape
    width = wide // 3
    pairs = width // (2 * HDIM)

    def column(offset):
        return pl.BlockSpec((rows, 2 * HDIM), lambda j: (0, offset + j))

    return pl.pallas_call(
        attend_kernel,
        grid=(pairs,),
        in_specs=[column(0), column(pairs), column(2 * pairs)],
        out_specs=[column(0), column(0), pl.BlockSpec((2, rows, rows), lambda j: (j, 0, 0))],
        out_shape=[
            jax.ShapeDtypeStruct((rows, width), bf16),
            jax.ShapeDtypeStruct((rows, width), f32),
            jax.ShapeDtypeStruct((2 * pairs, rows, rows), bf16),
        ],
        compiler_params=pltpu.CompilerParams(vmem_limit_bytes=56 * 1024 * 1024),
        cost_estimate=pl.CostEstimate(
            flops=16 * rows * rows * width, transcendentals=2 * pairs * rows * rows,
            bytes_accessed=4 * pairs * rows * rows + 12 * rows * width,
        ),
        name="attend",
    )(qkv, qkv, qkv)


def attend_back_kernel(
    q_ref, k_ref, v_ref, d_ref, o_ref, inv_ref, p_ref, dq_ref, dk_ref, dv_ref
):
    rows = q_ref.shape[0]
    scale = HDIM ** (-0.5)
    queries = q_ref[...]
    keys = k_ref[...]
    values = v_ref[...]
    grads = (d_ref[...].astype(f32) * inv_ref[...]).astype(bf16)
    product = grads.astype(f32) * o_ref[...].astype(f32)
    lane = lax.broadcasted_iota(jnp.int32, (rows, 2 * HDIM), 1)
    blocks = query_blocks(rows)
    d_queries = [None] * len(blocks)
    d_keys = d_values = None
    for head in range(2):
        mask = head_mask(head, rows, bf16)
        inner = -jnp.sum(jnp.where(lane // HDIM == head, product, 0.0), 1, keepdims=True)
        high = inner.astype(bf16)
        low = (inner - high.astype(f32)).astype(bf16)
        tail = jnp.where(lane == 0, high, jnp.where(lane == 1, low, jnp.zeros_like(low)))
        grads_wide = jnp.concatenate([grads, tail], 1)
        values_wide = jnp.concatenate([values * mask, (lane < 2).astype(bf16)], 1)
        keys_h, queries_h, grads_h = keys * mask, queries * mask, grads * mask
        for b, (start, n) in enumerate(blocks):
            d_probs = contract(values_wide, grads_wide[start : start + n, :], 1, 1)
            probs = p_ref[head, :, start : start + n]
            d_scores = probs * d_probs.astype(bf16)
            to_values = contract(probs, grads_h[start : start + n, :], 1, 0)
            to_keys = contract(d_scores, queries_h[start : start + n, :], 1, 0)
            to_queries = contract(d_scores, keys_h, 0, 0)
            d_values = to_values if d_values is None else d_values + to_values
            d_keys = to_keys if d_keys is None else d_keys + to_keys
            d_queries[b] = to_queries if d_queries[b] is None else d_queries[b] + to_queries
    dk_ref[...] = (d_keys * scale).astype(bf16)
    dv_ref[...] = d_values.astype(bf16)
    for b, (start, n) in enumerate(blocks):
        dq_ref[start : start + n, :] = (d_queries[b] * scale).astype(bf16)


def attend_back(qkv, grad, attended, inverse, probs):
    rows, wide = qkv.shape
    width = wide // 3
    pairs = width // (2 * HDIM)

    def column(offset):
        return pl.BlockSpec((rows, 2 * HDIM), lambda j: (0, offset + j))

    return pl.pallas_call(
        attend_back_kernel,
        grid=(pairs,),
        in_specs=[column(0), column(pairs), column(2 * pairs)]
        + [column(0)] * 3
        + [pl.BlockSpec((2, rows, rows), lambda j: (j, 0, 0))],
        out_specs=[column(0)] * 3,
        out_shape=[jax.ShapeDtypeStruct((rows, width), bf16)] * 3,
        compiler_params=pltpu.CompilerParams(vmem_limit_bytes=56 * 1024 * 1024),
        cost_estimate=pl.CostEstimate(
            flops=32 * rows * rows * width, transcendentals=0,
            bytes_accessed=4 * pairs * rows * rows + 24 * rows * width,
        ),
        name="attend_back",
    )(qkv, qkv, qkv, grad, attended, inverse, probs)


class Links:
    def __init__(self, mesh):
        self.ns = mesh.shape["shard"]
        self.nr = mesh.shape["rep"]
        self.nq = self.nr // 2

    def here(self):
        rep = lax.axis_index("rep")
        return lax.axis_index("shard"), rep // 2, rep % 2

    def along(self, values, step):
        return lax.ppermute(values, "shard", [(i, (i + step) % self.ns) for i in range(self.ns)])

    def chip(self, values, k):
        return lax.ppermute(values, "rep", [(i, i ^ (2 * k)) for i in range(self.nr)])

    def core(self, values):
        return lax.ppermute(values, "rep", [(i, i ^ 1) for i in range(self.nr)])


def piece_of(links, weight):
    rows, cols = weight.shape
    _, q, c = links.here()
    rq, half = rows // links.nq, cols // 2
    return lax.dynamic_slice(weight, (q * rq, c * half), (rq, half))


def assemble(links, weights, own, crossed, mate):
    ns, nq = links.ns, links.nq
    rows = [w.shape[0] for w in weights]
    cols = [w.shape[1] for w in weights]
    rq = [r // nq for r in rows]

    def kernel(*refs):
        n = len(weights)
        w_refs = refs[:n]
        part_refs = refs[n : n + nq]
        mate_ref = refs[n + nq]
        out_refs = refs[n + nq + 1 : n + nq + 1 + n]
        sem = refs[-1]
        z = lax.axis_index("shard")
        rep = lax.axis_index("rep")
        q, c = rep // 2, rep % 2
        copies = []

        def go(src, dst):
            copy = pltpu.make_async_copy(src, dst, sem.at[len(copies)])
            copy.start()
            copies.append(copy)

        base = 0
        for i in range(n):
            half = cols[i] // 2
            go(w_refs[i], out_refs[i].at[pl.ds(pl.multiple_of(z * rows[i], rows[i]), rows[i]), :])
            mine = pl.ds(pl.multiple_of(c * half, half), half)
            other = pl.ds(pl.multiple_of((1 - c) * half, half), half)
            for s in range(1, ns):
                zs = lax.rem(z + (ns - s), ns)
                for k in range(nq):
                    at = pl.ds(pl.multiple_of(zs * rows[i] + (q ^ k) * rq[i], rq[i]), rq[i])
                    lanes = pl.ds(base, half)
                    go(part_refs[k].at[s - 1, :, lanes], out_refs[i].at[at, mine])
                    go(mate_ref.at[k, s - 1, :, lanes], out_refs[i].at[at, other])
            base += half
        for copy in copies:
            copy.wait()

    count = len(weights) * (1 + 2 * (ns - 1) * nq)
    anywhere = pl.BlockSpec(memory_space=pl.ANY)
    return pl.pallas_call(
        kernel,
        out_shape=[jax.ShapeDtypeStruct((ns * r, n), bf16) for r, n in zip(rows, cols)],
        in_specs=[anywhere] * (len(weights) + nq + 1),
        out_specs=[pl.BlockSpec(memory_space=pltpu.VMEM)] * len(weights),
        scratch_shapes=[pltpu.SemaphoreType.DMA((count,))],
        compiler_params=pltpu.CompilerParams(vmem_limit_bytes=32 * 1024 * 1024),
        name="assemble",
    )(*weights, own, *crossed, mate)


def gather(links, weights, extra=None):
    piece = jnp.concatenate([piece_of(links, w) for w in weights], 1)
    n = piece.shape[0]
    sent = piece if extra is None else jnp.concatenate([piece, extra], 0)
    got = [links.along(sent, s) for s in range(1, links.ns)]
    own = jnp.stack([g[:n] for g in got])
    crossed = [links.chip(own, k) for k in range(1, links.nq)]
    mate = links.core(jnp.stack([own] + crossed))
    full = assemble(links, weights, own, crossed, mate)
    if extra is None:
        return full
    return full, [g[n:] for g in got]


def scatter(links, sent, kept):
    ns, nq = links.ns, links.nq
    z, q, c = links.here()
    got = [links.core(s) for s in sent]
    rq = sent[0].shape[0] // (ns * nq)

    def view(values):
        return values.reshape(ns, nq, rq, values.shape[1])

    def part(k):
        pairs = [
            lax.dynamic_index_in_dim(view(a), q ^ k, 1, False).astype(f32)
            + lax.dynamic_index_in_dim(view(b), q ^ k, 1, False).astype(f32)
            for a, b in zip(kept, got)
        ]
        return jnp.concatenate(pairs, -1) if len(pairs) > 1 else pairs[0]

    crossed = [links.chip(part(k).astype(bf16), k) for k in range(1, nq)]
    total = part(0)
    for x in crossed:
        total = total + x.astype(f32)
    total = total.astype(bf16)
    moved = [
        links.along(lax.dynamic_index_in_dim(total, (z + s) % ns, 0, False), s)
        for s in range(1, ns)
    ]
    final = lax.dynamic_index_in_dim(total, z, 0, False).astype(f32)
    for x in moved:
        final = final + x.astype(f32)
    final = final.astype(bf16)
    mine = jnp.stack([final] + [links.chip(final, k) for k in range(1, nq)])
    mate = links.core(mine)
    first = jnp.where(c == 0, mine, mate)
    second = jnp.where(c == 0, mate, mine)
    outs = []
    base = 0
    for s in sent:
        half = s.shape[1]
        both = jnp.concatenate(
            [first[:, :, base : base + half], second[:, :, base : base + half]], -1
        )
        ordered = [lax.dynamic_index_in_dim(both, q ^ j, 0, False) for j in range(nq)]
        outs.append(jnp.concatenate(ordered).astype(f32))
        base += half
    return outs


def total_of(links, lines):
    z, _, _ = links.here()
    lines = lines + links.core(lines)
    crossed = [links.chip(lines, k) for k in range(1, links.nq)]
    for x in crossed:
        lines = lines + x
    moved = [
        links.along(lax.dynamic_index_in_dim(lines, (z + s) % links.ns, 0, False), s)
        for s in range(1, links.ns)
    ]
    line = lax.dynamic_index_in_dim(lines, z, 0, False)
    for x in moved:
        line = line + x
    return line


def halves(links, left, right):
    _, _, c = links.here()
    half = right.shape[1] // 2
    away = lax.dynamic_slice_in_dim(right, (1 - c) * half, half, 1)
    home = lax.dynamic_slice_in_dim(right, c * half, half, 1)
    return left_trans(left, away).astype(bf16), left_trans(left, home).astype(bf16)


def body(
    links,
    inputs,
    counts,
    ln1_gain,
    ln1_shift,
    w_qkv,
    qv_bias,
    w_out,
    out_bias,
    ln2_gain,
    ln2_shift,
    w_up,
    up_bias,
    w_down,
    down_bias,
    cotangent,
):
    ns = links.ns
    slots = inputs.shape[1]
    seq_len = inputs.shape[2]
    width = inputs.shape[3]
    n_rows = slots * seq_len
    z = lax.axis_index("shard")

    small = (ln1_gain, ln1_shift, qv_bias, out_bias, ln2_gain, ln2_shift, up_bias, down_bias)
    sizes = [v.shape[0] for v in small]
    line = w_qkv.shape[1] // 2
    total_small = sum(sizes)
    n_lines = -(-total_small // line)
    packed = jnp.concatenate(small + (jnp.zeros((n_lines * line - total_small,), bf16),))
    packed = packed.reshape(n_lines, line)
    extra = jnp.concatenate([packed, jnp.zeros((16 - n_lines, line), bf16)])

    (full_qkv,), got_small = gather(links, [w_qkv], extra)
    all_small = jnp.stack([packed] + [g[:n_lines] for g in got_small]).reshape(ns, -1)
    all_small = jnp.concatenate(
        [lax.dynamic_index_in_dim(all_small, (z - j) % ns, 0) for j in range(ns)]
    )
    full_small = []
    base = 0
    for n in sizes:
        full_small.append(all_small[:, base : base + n].reshape(-1).astype(f32))
        base += n
    full_g1, full_s1, bias_f, full_bout, full_g2, full_s2, full_bup, full_bdown = full_small
    full_wout, full_wup = gather(links, [w_out, w_up])
    (full_wdown,) = gather(links, [w_down])

    first_slot = z * slots
    alive = (jnp.arange(slots, dtype=jnp.int32) + first_slot < counts[0]).astype(f32)
    alive_rows = jnp.broadcast_to(alive[:, None], (slots, seq_len)).reshape(n_rows, 1)
    tokens = inputs.reshape(n_rows, width).astype(f32)
    hidden_one, norm_one_back = jax.vjp(layer_norm, tokens, full_g1, full_s1)
    hidden_one_b = hidden_one.astype(bf16)
    projected = matmul(hidden_one_b, full_qkv)
    none = jnp.zeros((width,), f32)
    qkv_bias = jnp.concatenate([bias_f[:width], none, bias_f[width:]])
    qkv_b = (projected + qkv_bias).astype(bf16)
    attended_b, inverse, probs_b = attend(qkv_b)
    middle = tokens + matmul(attended_b, full_wout) + full_bout
    hidden_two, norm_two_back = jax.vjp(layer_norm, middle, full_g2, full_s2)
    hidden_two_b = hidden_two.astype(bf16)
    pre_act = matmul(hidden_two_b, full_wup) + full_bup
    activated, gelu_back = jax.vjp(gelu_exact, pre_act)
    activated_b = activated.astype(bf16)
    d_out = alive_rows * cotangent.reshape(n_rows, width).astype(f32)
    d_out_b = d_out.astype(bf16)
    grad_wdown = halves(links, activated_b, d_out_b)
    (o_wdown,) = scatter(links, [grad_wdown[0]], [grad_wdown[1]])
    result = middle + matmul(activated_b, full_wdown) + full_bdown
    output = (alive_rows * result).astype(bf16).reshape(inputs.shape)
    grad_bdown = jnp.sum(d_out, 0)
    d_act = right_trans(d_out_b, full_wdown)
    d_pre_b = gelu_back(d_act)[0].astype(bf16)
    grad_wup = halves(links, hidden_two_b, d_pre_b)
    grad_bup = jnp.sum(d_pre_b.astype(f32), 0)
    d_hidden_two = right_trans(d_pre_b, full_wup)
    d_mid_norm, grad_g2, grad_s2 = norm_two_back(d_hidden_two)
    d_mid = d_out + d_mid_norm
    d_proj_b = d_mid.astype(bf16)
    grad_wout = halves(links, attended_b, d_proj_b)
    o_wout, o_wup = scatter(links, [grad_wout[0], grad_wup[0]], [grad_wout[1], grad_wup[1]])
    grad_bout = jnp.sum(d_proj_b.astype(f32), 0)
    d_att_b = right_trans(d_proj_b, full_wout).astype(bf16)
    d_qkv_b = jnp.concatenate(attend_back(qkv_b, d_att_b, attended_b, inverse, probs_b), 1)
    grad_qkv = halves(links, hidden_one_b, d_qkv_b)
    (o_qkv,) = scatter(links, [grad_qkv[0]], [grad_qkv[1]])
    column_sums = jnp.sum(d_qkv_b.astype(f32), 0)
    grad_qvb = jnp.concatenate([column_sums[:width], column_sums[2 * width :]])
    d_hidden_one = right_trans(d_qkv_b, full_qkv)
    d_in_norm, grad_g1, grad_s1 = norm_one_back(d_hidden_one)
    input_grad = (d_mid + d_in_norm).reshape(inputs.shape)
    small_grads = (grad_g1, grad_s1, grad_qvb, grad_bout, grad_g2, grad_s2, grad_bup, grad_bdown)
    joined = jnp.concatenate([g.reshape(ns, -1) for g in small_grads], 1)
    joined = total_of(links, joined)
    owned = []
    base = 0
    for n in sizes:
        owned.append(joined[base : base + n])
        base += n
    o_g1, o_s1, o_qvb, o_bout, o_g2, o_s2, o_bup, o_bdown = owned
    return (
        output,
        input_grad,
        o_g1,
        o_s1,
        o_qkv,
        o_qvb,
        o_wout,
        o_bout,
        o_g2,
        o_s2,
        o_wup,
        o_bup,
        o_wdown,
        o_bdown,
    )


def solution(mesh):
    tokens = P("rep", "shard", None, None)
    vector = P("shard")
    matrix = P("shard", None)
    return jax.shard_map(
        functools.partial(body, Links(mesh)),
        mesh=mesh,
        in_specs=(
            tokens,
            P("rep"),
            vector,
            vector,
            matrix,
            vector,
            matrix,
            vector,
            vector,
            vector,
            matrix,
            vector,
            matrix,
            vector,
            tokens,
        ),
        out_specs=(
            tokens,
            tokens,
            vector,
            vector,
            matrix,
            vector,
            matrix,
            vector,
            vector,
            vector,
            matrix,
            vector,
            matrix,
            vector,
        ),
        check_vma=False,
    )
```

```python
import functools

import jax
import jax.numpy as jnp
from jax import lax
from jax.experimental import pallas as pl
from jax.experimental.pallas import tpu as pltpu
from jax.sharding import PartitionSpec as P

HDIM = 64

eps = 1e-06
bf16 = jnp.bfloat16
HINT = pl.CostEstimate(flops=1, transcendentals=0, bytes_accessed=1)
f32 = jnp.float32


def layer_norm(values, gain, shift):
    centre = values - jnp.mean(values, -1, keepdims=True)
    spread = jnp.mean(centre * centre, -1, keepdims=True)
    return centre * lax.rsqrt(spread + eps) * gain + shift


def matmul(left, right):
    return jnp.dot(left, right, preferred_element_type=f32)


LOG2E = 1.4426950408889634


def contract(left, right, left_dim, right_dim):
    return lax.dot_general(
        left, right, (((left_dim,), (right_dim,)), ((), ())), preferred_element_type=f32
    )


def query_blocks(rows, tile=256):
    return [(i, min(tile, rows - i)) for i in range(0, rows, tile)]


def head_mask(head, rows, dtype):
    lane = lax.broadcasted_iota(jnp.int32, (rows, 2 * HDIM), 1)
    return (lane // HDIM == head).astype(dtype)


def attend_kernel(q_ref, k_ref, v_ref, o_ref, inv_ref, p_ref):
    rows = q_ref.shape[0]
    factor = HDIM ** (-0.5) * LOG2E
    keys = k_ref[...]
    values = v_ref[...]
    ones = jnp.ones(values.shape, bf16)
    for start, n in query_blocks(rows):
        queries = q_ref[start : start + n, :]
        mixed = inverse = None
        for head in range(2):
            mask = head_mask(head, rows, bf16)
            scores = contract(keys * mask, queries, 1, 1)
            largest = jnp.max(scores, axis=0, keepdims=True)
            probs = jnp.exp2((scores - largest) * factor).astype(bf16)
            p_ref[head, :, start : start + n] = probs
            both = contract(probs, jnp.concatenate([values * mask, ones], 1), 0, 0)
            inv = 1.0 / both[:, 2 * HDIM :]
            part = both[:, : 2 * HDIM] * inv
            share = head_mask(head, n, f32) * inv
            mixed = part if mixed is None else mixed + part
            inverse = share if inverse is None else inverse + share
        o_ref[start : start + n, :] = mixed.astype(bf16)
        inv_ref[start : start + n, :] = inverse


def whole(count):
    return [pl.BlockSpec(memory_space=pl.ANY)] * count


def attend(qkv, first, last, before=None):
    rows, wide = qkv.shape
    width = wide // 3
    pairs = width // (2 * HDIM)
    count = last - first

    def column(offset):
        return pl.BlockSpec((rows, 2 * HDIM), lambda j: (0, offset + first + j))

    def kernel(*refs):
        attend_kernel(*refs[:3], *refs[-3:])

    given = () if before is None else tuple(before)
    return pl.pallas_call(
        kernel,
        grid=(count,),
        in_specs=[column(0), column(pairs), column(2 * pairs)] + whole(len(given)),
        out_specs=[
            column(0),
            column(0),
            pl.BlockSpec((2, rows, rows), lambda j: (first + j, 0, 0)),
        ],
        out_shape=[
            jax.ShapeDtypeStruct((rows, width), bf16),
            jax.ShapeDtypeStruct((rows, width), f32),
            jax.ShapeDtypeStruct((2 * pairs, rows, rows), bf16),
        ],
        input_output_aliases={3 + i: i for i in range(len(given))},
        compiler_params=pltpu.CompilerParams(vmem_limit_bytes=56 * 1024 * 1024),
        cost_estimate=HINT,
        name="attend",
    )(qkv, qkv, qkv, *given)


def attend_back_kernel(
    q_ref, k_ref, v_ref, d_ref, o_ref, inv_ref, p_ref, out_ref, sum_ref
):
    rows = q_ref.shape[0]
    scale = HDIM ** (-0.5)
    queries = q_ref[...]
    keys = k_ref[...]
    values = v_ref[...]
    grads = (d_ref[...].astype(f32) * inv_ref[...]).astype(bf16)
    product = grads.astype(f32) * o_ref[...].astype(f32)
    lane = lax.broadcasted_iota(jnp.int32, (rows, 2 * HDIM), 1)
    blocks = query_blocks(rows)
    d_queries = [None] * len(blocks)
    d_keys = d_values = None
    for head in range(2):
        mask = head_mask(head, rows, bf16)
        inner = -jnp.sum(jnp.where(lane // HDIM == head, product, 0.0), 1, keepdims=True)
        high = inner.astype(bf16)
        low = (inner - high.astype(f32)).astype(bf16)
        tail = jnp.where(lane == 0, high, jnp.where(lane == 1, low, jnp.zeros_like(low)))
        grads_wide = jnp.concatenate([grads, tail], 1)
        values_wide = jnp.concatenate([values * mask, (lane < 2).astype(bf16)], 1)
        keys_h, queries_h, grads_h = keys * mask, queries * mask, grads * mask
        for b, (start, n) in enumerate(blocks):
            d_probs = contract(values_wide, grads_wide[start : start + n, :], 1, 1)
            probs = p_ref[head, :, start : start + n]
            d_scores = probs * d_probs.astype(bf16)
            to_values = contract(probs, grads_h[start : start + n, :], 1, 0)
            to_keys = contract(d_scores, queries_h[start : start + n, :], 1, 0)
            to_queries = contract(d_scores, keys_h, 0, 0)
            d_values = to_values if d_values is None else d_values + to_values
            d_keys = to_keys if d_keys is None else d_keys + to_keys
            d_queries[b] = to_queries if d_queries[b] is None else d_queries[b] + to_queries
    d_values = d_values.astype(bf16)
    out_ref[1] = (d_keys * scale).astype(bf16)
    out_ref[2] = d_values
    sums = jnp.zeros((1, 2 * HDIM), f32)
    for b, (start, n) in enumerate(blocks):
        block = (d_queries[b] * scale).astype(bf16)
        out_ref[0, start : start + n, :] = block
        sums = sums + jnp.sum(block.astype(f32), 0, keepdims=True)
    sum_ref[0] = sums
    sum_ref[1] = jnp.sum(d_values.astype(f32), 0, keepdims=True)


def attend_back(qkv, grad, attended, inverse, probs, first, last, before=None):
    rows, wide = qkv.shape
    width = wide // 3
    pairs = width // (2 * HDIM)
    count = last - first

    def column(offset):
        return pl.BlockSpec((rows, 2 * HDIM), lambda j: (0, offset + first + j))

    def kernel(*refs):
        attend_back_kernel(*refs[:7], *refs[-2:])

    given = () if before is None else tuple(before)
    return pl.pallas_call(
        kernel,
        grid=(count,),
        in_specs=[column(0), column(pairs), column(2 * pairs)]
        + [column(0)] * 3
        + [pl.BlockSpec((2, rows, rows), lambda j: (first + j, 0, 0))]
        + whole(len(given)),
        out_specs=[
            pl.BlockSpec((3, rows, 2 * HDIM), lambda j: (0, 0, first + j)),
            pl.BlockSpec((2, 1, 2 * HDIM), lambda j: (0, 0, first + j)),
        ],
        out_shape=[
            jax.ShapeDtypeStruct((3, rows, width), bf16),
            jax.ShapeDtypeStruct((2, 1, width), f32),
        ],
        input_output_aliases={7 + i: i for i in range(len(given))},
        compiler_params=pltpu.CompilerParams(vmem_limit_bytes=56 * 1024 * 1024),
        cost_estimate=HINT,
        name="attend_back",
    )(qkv, qkv, qkv, grad, attended, inverse, probs, *given)


def gelu_pair(values):
    bell = jnp.exp2(values * values * (-0.5 * LOG2E))
    t = 1.0 / (1.0 + 0.23164189 * jnp.abs(values))
    poly = 0.5307027145 * t - 0.7265760135
    poly = poly * t + 0.7107068705
    poly = poly * t - 0.142248368
    poly = poly * t + 0.127414796
    tail = poly * t * bell
    area = jnp.where(values >= 0, 1.0 - tail, tail)
    return values * area, area + values * bell * 0.3989422804014327


def feed_forward_kernel(
    h_ref, dm_ref, up_ref, bias_ref, down_ref, alive_ref, last_ref, y0_ref, g0_ref,
    y_ref, g_ref, down_away, down_home, up_away, up_home, gb_ref,
    act_ref, dp_ref, y_acc, g_acc,
):
    j = pl.program_id(0)

    @pl.when(j == 0)
    def _():
        if g0_ref is None:
            y_acc[...] = y0_ref[...] + last_ref[...]
            g_acc[...] = jnp.zeros_like(g_acc)
        else:
            y_acc[...] = y0_ref[...]
            g_acc[...] = g0_ref[...]

    rows = h_ref.shape[0]
    up, down = up_ref[...], down_ref[...]
    bias = bias_ref[...]
    chunk = 368
    for start in range(0, rows, chunk):
        r = slice(start, min(start + chunk, rows))
        act, slope = gelu_pair(contract(h_ref[r, :], up, 1, 0) + bias)
        act = act.astype(bf16)
        act_ref[r, :] = act
        d_pre = (contract(dm_ref[r, :], down, 1, 1) * slope).astype(bf16)
        dp_ref[r, :] = d_pre
        y_acc[r, :] += contract(act, down, 1, 0)
        g_acc[r, :] += contract(d_pre, up, 1, 1)
    gb_ref[...] = jnp.sum(dp_ref[...].astype(f32), 0, keepdims=True)[None]
    first_core = lax.axis_index("rep") % 2 == 0
    for left, right, away, home in (
        (act_ref, dm_ref, down_away, down_home),
        (h_ref, dp_ref, up_away, up_home),
    ):
        grad = contract(left[...], right[...], 0, 0)
        half = grad.shape[1] // 2
        low, high = grad[:, :half], grad[:, half:]
        away[...] = jnp.where(first_core, high, low).reshape(away.shape).astype(bf16)
        home[...] = jnp.where(first_core, low, high).reshape(home.shape).astype(bf16)

    @pl.when(j == pl.num_programs(0) - 1)
    def _():
        y = y_acc[...]
        y_ref[...] = y if g0_ref is None else (alive_ref[0] * y).astype(bf16)
        g_ref[...] = g_acc[...]


def feed_forward(links, hidden, d_out, up, bias, down, alive, last_bias, y0, g0, part):
    ns, nq = links.ns, links.nq
    rows, width = hidden.shape
    block = up.shape[1] // (2 * ns)
    rq = width // (ns * nq)
    per = width // block
    wide = dict(pipeline_mode=pl.Buffered(1))

    def full():
        return pl.BlockSpec((rows, width), lambda j: (0, 0), **wide)

    def kernel(*refs):
        refs = list(refs)
        if g0 is None:
            refs.insert(8, None)
        feed_forward_kernel(*refs)

    down_spec = pl.BlockSpec((1, block, width // 2), lambda j: (j, 0, 0))
    up_spec = pl.BlockSpec((ns, nq, 1, rq, block // 2), lambda j: (0, 0, j // per, 0, j % per))
    down_shape = jax.ShapeDtypeStruct((ns, block, width // 2), bf16)
    up_shape = jax.ShapeDtypeStruct((ns, nq, ns // per, rq, width // 2), bf16)
    sums = jax.ShapeDtypeStruct((rows, width), f32)
    given = (y0,) if g0 is None else (y0, g0)
    y, g, d_away, d_home, u_away, u_home, gb = pl.pallas_call(
        kernel,
        grid=(ns,),
        in_specs=[
            full(),
            full(),
            pl.BlockSpec((width, block), lambda j: (0, 2 * j + part)),
            pl.BlockSpec((1, block), lambda j: (0, 2 * j + part)),
            pl.BlockSpec((block, width), lambda j: (2 * j + part, 0)),
            pl.BlockSpec(memory_space=pltpu.SMEM),
            pl.BlockSpec((1, width), lambda j: (0, 0)),
        ]
        + [full() for _ in given],
        out_specs=[
            full(),
            full(),
            down_spec,
            down_spec,
            up_spec,
            up_spec,
            pl.BlockSpec((1, 1, block), lambda j: (j, 0, 0)),
        ],
        out_shape=[
            sums if g0 is None else jax.ShapeDtypeStruct((rows, width), bf16),
            sums,
            down_shape,
            down_shape,
            up_shape,
            up_shape,
            jax.ShapeDtypeStruct((ns, 1, block), f32),
        ],
        scratch_shapes=[
            pltpu.VMEM((rows, block), bf16),
            pltpu.VMEM((rows, block), bf16),
            pltpu.VMEM((rows, width), f32),
            pltpu.VMEM((rows, width), f32),
        ],
        compiler_params=pltpu.CompilerParams(vmem_limit_bytes=58 * 1024 * 1024),
        cost_estimate=HINT,
        name="feed_forward",
    )(hidden, d_out, up, bias, down, alive, last_bias, *given)

    def pieces(down_grad, up_grad):
        lanes = width // 2
        return [
            down_grad.reshape(ns, nq, block // nq, lanes),
            up_grad.reshape(ns, nq, ns // per * rq, lanes),
        ]

    return y, g, pieces(d_away, u_away), pieces(d_home, u_home), gb.reshape(ns, block)


def grad_kernel(left_ref, right_ref, away_ref, home_ref):
    grad = contract(left_ref[...], right_ref[0], 0, 0)
    half = grad.shape[1] // 2
    low, high = grad[:, :half], grad[:, half:]
    first_core = lax.axis_index("rep") % 2 == 0
    away_ref[...] = jnp.where(first_core, high, low).reshape(away_ref.shape).astype(bf16)
    home_ref[...] = jnp.where(first_core, low, high).reshape(home_ref.shape).astype(bf16)


def weight_grads(links, left, rights):
    ns, nq = links.ns, links.nq
    rows, width = left.shape
    count, _, wide = rights.shape
    rq = width // (ns * nq)
    spec = pl.BlockSpec((ns, nq, 1, rq, wide // 2), lambda i: (0, 0, i, 0, 0))
    shape = jax.ShapeDtypeStruct((ns, nq, count, rq, wide // 2), bf16)
    away, home = pl.pallas_call(
        grad_kernel,
        grid=(count,),
        in_specs=[
            pl.BlockSpec((rows, width), lambda i: (0, 0)),
            pl.BlockSpec((1, rows, wide), lambda i: (i, 0, 0)),
        ],
        out_specs=[spec, spec],
        out_shape=[shape, shape],
        compiler_params=pltpu.CompilerParams(vmem_limit_bytes=48 * 1024 * 1024),
        cost_estimate=HINT,
        name="weight_grads",
    )(left, rights)
    flat = (ns, nq, count * rq, wide // 2)
    return [away.reshape(flat)], [home.reshape(flat)]


def row_block(rows):
    return 368 if rows % 368 == 0 else rows


def normal(values):
    centre = values - jnp.mean(values, -1, keepdims=True)
    scale = lax.rsqrt(jnp.mean(centre * centre, -1, keepdims=True) + eps)
    return centre * scale, scale


def normal_back(unit, scale, grad):
    inner = jnp.mean(grad * unit, -1, keepdims=True)
    return scale * (grad - jnp.mean(grad, -1, keepdims=True) - unit * inner)


def column_sum(values):
    return jnp.sum(values, 0, keepdims=True)


def middle_kernel(x_ref, att_ref, w_ref, bias_ref, gain_ref, shift_ref, mid_ref, h_ref):
    mid = x_ref[...].astype(f32) + contract(att_ref[...], w_ref[...], 1, 0) + bias_ref[...]
    mid_ref[...] = mid
    unit, _ = normal(mid)
    h_ref[...] = (unit * gain_ref[...] + shift_ref[...]).astype(bf16)


def middle_of(tokens, attended, weight, bias, gain, shift):
    rows, width = tokens.shape
    n = row_block(rows)
    block = pl.BlockSpec((n, width), lambda i: (i, 0))
    line = pl.BlockSpec((1, width), lambda i: (0, 0))
    return pl.pallas_call(
        middle_kernel,
        grid=(rows // n,),
        in_specs=[block, block, pl.BlockSpec(weight.shape, lambda i: (0, 0)), line, line, line],
        out_specs=[block, block],
        out_shape=[
            jax.ShapeDtypeStruct((rows, width), f32),
            jax.ShapeDtypeStruct((rows, width), bf16),
        ],
        compiler_params=pltpu.CompilerParams(vmem_limit_bytes=48 * 1024 * 1024),
        cost_estimate=HINT,
        name="middle",
    )(tokens, attended, weight, bias, gain, shift)


def middle_back_kernel(
    g_ref, mid_ref, dm_ref, att_ref, w_ref, gain_ref,
    d_mid_ref, d_att_ref, away_ref, home_ref, sum_ref, acc_ref,
):
    i = pl.program_id(0)

    @pl.when(i == 0)
    def _():
        acc_ref[...] = jnp.zeros_like(acc_ref)
        sum_ref[...] = jnp.zeros_like(sum_ref)

    unit, scale = normal(mid_ref[...])
    g = g_ref[...]
    d_out = dm_ref[...].astype(f32)
    d_mid = d_out + normal_back(unit, scale, g * gain_ref[...])
    d_mid_ref[...] = d_mid
    d_proj = d_mid.astype(bf16)
    d_att_ref[...] = contract(d_proj, w_ref[...], 1, 1).astype(bf16)
    acc_ref[...] += contract(att_ref[...], d_proj, 0, 0)
    sum_ref[0:1, :] += column_sum(g * unit)
    sum_ref[1:2, :] += column_sum(g)
    sum_ref[2:3, :] += column_sum(d_proj.astype(f32))
    sum_ref[3:4, :] += column_sum(d_out)

    @pl.when(i == pl.num_programs(0) - 1)
    def _():
        grad = acc_ref[...]
        half = grad.shape[1] // 2
        low, high = grad[:, :half], grad[:, half:]
        first_core = lax.axis_index("rep") % 2 == 0
        away_ref[...] = jnp.where(first_core, high, low).reshape(away_ref.shape).astype(bf16)
        home_ref[...] = jnp.where(first_core, low, high).reshape(home_ref.shape).astype(bf16)


def middle_back(links, grad, middle, d_out, attended, weight, gain):
    ns, nq = links.ns, links.nq
    rows, width = middle.shape
    n = row_block(rows)
    block = pl.BlockSpec((n, width), lambda i: (i, 0))
    pieces = (ns, nq, width // (ns * nq), width // 2)
    whole_piece = pl.BlockSpec(pieces, lambda i: (0, 0, 0, 0))
    return pl.pallas_call(
        middle_back_kernel,
        grid=(rows // n,),
        in_specs=[block] * 4
        + [
            pl.BlockSpec(weight.shape, lambda i: (0, 0)),
            pl.BlockSpec((1, width), lambda i: (0, 0)),
        ],
        out_specs=[
            block,
            block,
            whole_piece,
            whole_piece,
            pl.BlockSpec((8, width), lambda i: (0, 0)),
        ],
        out_shape=[
            jax.ShapeDtypeStruct((rows, width), f32),
            jax.ShapeDtypeStruct((rows, width), bf16),
            jax.ShapeDtypeStruct(pieces, bf16),
            jax.ShapeDtypeStruct(pieces, bf16),
            jax.ShapeDtypeStruct((8, width), f32),
        ],
        scratch_shapes=[pltpu.VMEM((width, width), f32)],
        compiler_params=pltpu.CompilerParams(vmem_limit_bytes=48 * 1024 * 1024),
        cost_estimate=HINT,
        name="middle_back",
    )(grad, middle, d_out, attended, weight, gain)


def entry_back_kernel(d_ref, w_ref, x_ref, d_mid_ref, gain_ref, out_ref, sum_ref):
    @pl.when(pl.program_id(0) == 0)
    def _():
        sum_ref[...] = jnp.zeros_like(sum_ref)

    width = x_ref.shape[1]
    g = contract(d_ref[0], w_ref[:, :width], 1, 1)
    for t in range(1, 3):
        g = g + contract(d_ref[t], w_ref[:, t * width : (t + 1) * width], 1, 1)
    unit, scale = normal(x_ref[...].astype(f32))
    out_ref[...] = d_mid_ref[...] + normal_back(unit, scale, g * gain_ref[...])
    sum_ref[0:1, :] += column_sum(g * unit)
    sum_ref[1:2, :] += column_sum(g)


def entry_back(grads, weight, tokens, d_mid, gain):
    rows, width = tokens.shape
    n = row_block(rows)
    block = pl.BlockSpec((n, width), lambda i: (i, 0))
    return pl.pallas_call(
        entry_back_kernel,
        grid=(rows // n,),
        in_specs=[
            pl.BlockSpec((3, n, width), lambda i: (0, i, 0)),
            pl.BlockSpec(weight.shape, lambda i: (0, 0), pipeline_mode=pl.Buffered(1)),
            block,
            block,
            pl.BlockSpec((1, width), lambda i: (0, 0)),
        ],
        out_specs=[block, pl.BlockSpec((8, width), lambda i: (0, 0))],
        out_shape=[
            jax.ShapeDtypeStruct((rows, width), f32),
            jax.ShapeDtypeStruct((8, width), f32),
        ],
        compiler_params=pltpu.CompilerParams(vmem_limit_bytes=48 * 1024 * 1024),
        cost_estimate=HINT,
        name="entry_back",
    )(grads, weight, tokens, d_mid, gain)


class Links:
    def __init__(self, mesh):
        self.ns = mesh.shape["shard"]
        self.nr = mesh.shape["rep"]
        self.nq = self.nr // 2
        self.bits = self.nq.bit_length() - 1
        assert 1 << self.bits == self.nq

    def here(self):
        rep = lax.axis_index("rep")
        return lax.axis_index("shard"), rep // 2, rep % 2

    def along(self, values, step):
        return lax.ppermute(values, "shard", [(i, (i + step) % self.ns) for i in range(self.ns)])

    def chip(self, values, k):
        return lax.ppermute(values, "rep", [(i, i ^ (2 * k)) for i in range(self.nr)])

    def core(self, values):
        return lax.ppermute(values, "rep", [(i, i ^ 1) for i in range(self.nr)])


def meet(*values):
    return lax.optimization_barrier(values)


def tie(values, others):
    return lax.optimization_barrier((values, others))[0]


def piece_of(links, weights):
    _, q, c = links.here()
    parts = []
    for w in weights:
        rq, half = w.shape[0] // links.nq, w.shape[1] // 2
        parts.append(lax.dynamic_slice(w, (q * rq, c * half), (rq, half)))
    return jnp.concatenate(parts, 1)


def pack(links, weight, small, line):
    rq = weight.shape[0] // links.nq
    total = sum(v.shape[0] for v in small)
    fits = all(sum(v.shape[0] for v in part) == line for part in (small[:6], small[6:]))
    if rq % 16 or line % 128 or not fits:
        filled = jnp.concatenate(small + (jnp.zeros((-total % line,), bf16),)).reshape(-1, line)
        filler = jnp.zeros((16 - filled.shape[0], line), bf16)
        return jnp.concatenate([piece_of(links, [weight]), filled, filler])

    def kernel(w_ref, *refs):
        *vectors, out_ref, sem = refs
        rep = lax.axis_index("rep")
        q, c = rep // 2, rep % 2
        rows = pl.ds(pl.multiple_of(q * rq, rq), rq)
        copy = pltpu.make_async_copy(
            w_ref.at[rows, pl.ds(pl.multiple_of(c * line, line), line)], out_ref.at[:rq], sem
        )
        copy.start()
        lines = [[], []]
        for at, ref in enumerate(vectors):
            lines[at // 6].append(ref[...].astype(f32).reshape(1, -1))
        block = [jnp.concatenate(x, 1) for x in lines]
        row = lax.broadcasted_iota(jnp.int32, (16, line), 0)
        filled = jnp.where(row == 0, block[0], jnp.where(row == 1, block[1], 0.0))
        out_ref[rq:, :] = filled.astype(bf16)
        copy.wait()

    return pl.pallas_call(
        kernel,
        in_specs=whole(1) + [pl.BlockSpec(memory_space=pltpu.VMEM)] * len(small),
        out_specs=pl.BlockSpec(memory_space=pltpu.VMEM),
        out_shape=jax.ShapeDtypeStruct((rq + 16, line), bf16),
        scratch_shapes=[pltpu.SemaphoreType.DMA(())],
        cost_estimate=HINT,
        name="pack",
    )(weight, *small)


def gather_along(links, piece):
    return [links.along(piece, s) for s in range(1, links.ns)]


def lanes_of(links, values, part):
    n = values.shape[-1] // links.bits
    return values[..., part * n : (part + 1) * n]


def gather_step(links, held, step):
    out = []
    for part, pieces in enumerate(held):
        bit = 1 << ((part + step) % links.bits)
        known = sorted(pieces)
        sent = jnp.stack([pieces[k] for k in known])
        got = links.chip(sent, bit)
        out.append((bit, known, got))
    return out


def gather_merge(links, held, got):
    merged = []
    for pieces, (bit, known, values) in zip(held, got):
        more = dict(pieces)
        for i, k in enumerate(known):
            more[k ^ bit] = values[i]
        merged.append(more)
    return merged


def assemble(links, weights, got_mine, got_mate):
    ns, nq, bits = links.ns, links.nq, links.bits
    rows = [w.shape[0] for w in weights]
    cols = [w.shape[1] for w in weights]
    rq = [r // nq for r in rows]
    total = sum(cols) // 2
    lanes = total // bits
    n = len(weights)
    per_side = len(got_mine)

    def kernel(*refs):
        w_refs = refs[:n]
        sides = (refs[n : n + per_side], refs[n + per_side : n + 2 * per_side])
        out_refs = refs[n + 2 * per_side : n + 2 * per_side + n]
        sem = refs[-1]
        z = lax.axis_index("shard")
        rep = lax.axis_index("rep")
        q, c = rep // 2, rep % 2
        copies = []

        def go(src, dst):
            copy = pltpu.make_async_copy(src, dst, sem.at[len(copies)])
            copy.start()
            copies.append(copy)

        for i in range(n):
            go(w_refs[i], out_refs[i].at[pl.ds(pl.multiple_of(z * rows[i], rows[i]), rows[i]), :])
        for side, parts in enumerate(sides):
            core = c if side == 0 else 1 - c
            base = 0
            for i in range(n):
                half = cols[i] // 2

                def place(source, k, s, low, high):
                    zs = lax.rem(z + (ns - s), ns)
                    at = pl.ds(pl.multiple_of(zs * rows[i] + (q ^ k) * rq[i], rq[i]), rq[i])
                    to = pl.ds(pl.multiple_of(core * half + (low - base), 128), high - low)
                    go(source, out_refs[i].at[at, to])

                for s in range(1, ns):
                    own = parts[0].at[s - 1, :, pl.ds(base, half)]
                    place(own, 0, s, base, base + half)
                    at = 1
                    for step in range(bits):
                        for part in range(bits):
                            known = [0]
                            for t in range(step):
                                bit = 1 << ((part + t) % bits)
                                known = known + [k ^ bit for k in known]
                            known = sorted(known)
                            bit = 1 << ((part + step) % bits)
                            low = max(base, part * lanes)
                            high = min(base + half, (part + 1) * lanes)
                            if low < high:
                                cut = pl.ds(low - part * lanes, high - low)
                                for j, k in enumerate(known):
                                    source = parts[at].at[j, s - 1, :, cut]
                                    place(source, k ^ bit, s, low, high)
                            at += 1
                base += half
        for copy in copies:
            copy.wait()

    pieces = 0
    base = 0
    for i in range(n):
        half = cols[i] // 2
        for part in range(bits):
            if max(base, part * lanes) < min(base + half, (part + 1) * lanes):
                pieces += nq - 1
        pieces += 1
        base += half
    count = n + 2 * (ns - 1) * pieces
    return pl.pallas_call(
        kernel,
        out_shape=[jax.ShapeDtypeStruct((ns * r, c), bf16) for r, c in zip(rows, cols)],
        in_specs=whole(n + 2 * per_side),
        out_specs=[pl.BlockSpec(memory_space=pltpu.VMEM)] * n,
        scratch_shapes=[pltpu.SemaphoreType.DMA((count,))],
        compiler_params=pltpu.CompilerParams(vmem_limit_bytes=32 * 1024 * 1024),
        cost_estimate=HINT,
        name="assemble",
    )(*weights, *got_mine, *got_mate)


class Gather:
    def __init__(self, links, weights):
        self.links, self.weights = links, weights

    def start(self, own):
        self.own = own
        self.held = [{0: lanes_of(self.links, own, p)} for p in range(self.links.bits)]
        self.mine = [own]
        self.mate = [self.links.core(own)]
        self.done = 0
        return own

    def step(self, after=None):
        held = self.held if after is None else tie(self.held, after)
        got = gather_step(self.links, held, self.done)
        self.held = gather_merge(self.links, held, got)
        self.done += 1
        for _, _, values in got:
            self.mine.append(values)
            self.mate.append(self.links.core(values))
        return self.mine[-1]

    def full(self):
        while self.done < self.links.bits:
            self.step()
        return assemble(self.links, self.weights, self.mine, self.mate)


class Scatter:
    def __init__(self, links, sent, kept):
        self.links = links
        self.rows = [s.shape[2] for s in sent]
        self.lanes = sent[0].shape[3]
        self.got = [links.core(s) for s in sent]
        self.kept = kept
        self.done = 0
        total = sum(self.rows)
        if links.bits == 2 and all(n % 32 == 0 for n in self.rows):
            first = []
            second = []
            taken = 0
            for i, n in enumerate(self.rows):
                cut = min(n, total // 2 - taken)
                if len(self.rows) == 3:
                    cut = (n, 0, n // 2)[i]
                taken += cut
                if cut:
                    first.append((i, 0, cut))
                if cut < n:
                    second.append((i, cut, n))
            self.parts = [first, second]
        else:
            self.parts = None

    def plan(self):
        if self.parts is None:
            return [(i, 0, n) for i, n in enumerate(self.rows)]
        return self.parts[0] + self.parts[1]

    def blocks(self):
        links = self.links
        ns, nq, lanes = links.ns, links.nq, self.lanes
        n = len(self.rows)
        sizes = [sum(high - low for _, low, high in part) for part in self.parts]

        def kernel(*refs):
            kept, got, outs = refs[:n], refs[n : 2 * n], refs[2 * n :]
            q = lax.axis_index("rep") // 2
            for p, part in enumerate(self.parts):
                bit = 1 << p
                for at, k in enumerate([k for k in range(nq) if not k & bit]):
                    for out, chip in ((outs[2 * p], k ^ bit), (outs[2 * p + 1], k)):
                        base = 0
                        for i, low, high in part:
                            a = kept[i][0, q ^ chip, low:high, :].astype(f32)
                            b = got[i][0, q ^ chip, low:high, :].astype(f32)
                            out[at, 0, base : base + high - low, :] = (a + b).astype(bf16)
                            base += high - low

        return pl.pallas_call(
            kernel,
            grid=(ns,),
            in_specs=[pl.BlockSpec((1, nq, r, lanes), lambda j: (j, 0, 0, 0)) for r in self.rows] * 2,
            out_specs=[
                pl.BlockSpec((nq // 2, 1, r, lanes), lambda j: (0, j, 0, 0))
                for r in sizes
                for _ in range(2)
            ],
            out_shape=[
                jax.ShapeDtypeStruct((nq // 2, ns, r, lanes), bf16) for r in sizes for _ in range(2)
            ],
            compiler_params=pltpu.CompilerParams(vmem_limit_bytes=32 * 1024 * 1024),
            cost_estimate=HINT,
            name="core_sums",
        )(*self.kept, *self.got)

    def prepare(self):
        links = self.links
        if self.done == 0 and self.parts is not None:
            s0, k0, s1, k1 = self.blocks()
            self.buffers = [s0, s1]
            self.stay = [[0, 2], [0, 1]]
            self.held = [{0: k0[0], 2: k0[1]}, {0: k1[0], 1: k1[1]}]
            return self.buffers
        if self.done == 0:
            _, q, _ = links.here()
            total = sum(self.rows)
            size = total // links.bits
            self.held = []
            both = [a.astype(f32) + b.astype(f32) for a, b in zip(self.kept, self.got)]
            both = jnp.concatenate(both, 2).astype(bf16)
            for p in range(links.bits):
                high = (p + 1) * size if p < links.bits - 1 else total
                cut = both[:, :, p * size : high]
                self.held.append(
                    {k: lax.dynamic_index_in_dim(cut, q ^ k, 1, False) for k in range(links.nq)}
                )
        self.buffers = []
        self.stay = []
        for part, pieces in enumerate(self.held):
            bit = 1 << ((part + self.done) % links.bits)
            stay = [k for k in sorted(pieces) if not k & bit]
            self.stay.append(stay)
            self.buffers.append(jnp.stack([pieces[k ^ bit] for k in stay]))
        return self.buffers

    def send(self):
        links = self.links
        last = self.done == links.bits - 1 and self.parts is not None
        out = []
        for part, (pieces, buffer, stay) in enumerate(zip(self.held, self.buffers, self.stay)):
            got = links.chip(buffer, 1 << ((part + self.done) % links.bits))
            if last:
                out.append((pieces[0], got[0]))
                continue
            out.append(
                {
                    k: (pieces[k].astype(f32) + got[i].astype(f32)).astype(bf16)
                    for i, k in enumerate(stay)
                }
            )
        self.held = out
        self.done += 1

    def prepare_along(self):
        links = self.links
        ns = links.ns
        if self.parts is not None:
            lanes = self.lanes
            total = sum(self.rows)

            def kernel(a0, b0, a1, b1, *outs):
                z = lax.axis_index("shard")
                for s, out in enumerate(outs):
                    at = lax.rem(z + s, ns)
                    base = 0
                    for a, b in ((a0, b0), (a1, b1)):
                        n = a.shape[1]
                        out[base : base + n, :] = (a[at].astype(f32) + b[at].astype(f32)).astype(bf16)
                        base += n

            pairs = [x for pair in self.held for x in pair]
            self.buffers = pl.pallas_call(
                kernel,
                in_specs=[pl.BlockSpec(memory_space=pltpu.VMEM)] * 4,
                out_specs=[pl.BlockSpec(memory_space=pltpu.VMEM)] * ns,
                out_shape=[jax.ShapeDtypeStruct((total, lanes), bf16)] * ns,
                compiler_params=pltpu.CompilerParams(vmem_limit_bytes=32 * 1024 * 1024),
                cost_estimate=HINT,
                name="chip_sums",
            )(*pairs)
            return self.buffers
        z, _, _ = links.here()
        total = jnp.concatenate([p[0] for p in self.held], 1)
        self.buffers = [
            lax.dynamic_index_in_dim(total, (z + s) % ns, 0, False) for s in range(ns)
        ]
        return self.buffers

    def send_along(self):
        final = self.buffers[0].astype(f32)
        for s in range(1, self.links.ns):
            final = final + self.links.along(self.buffers[s], s).astype(f32)
        self.final = final.astype(bf16)
        return self.final

    def spread(self, after=None):
        links = self.links
        final = self.final if after is None else tie(self.final, after)
        others = [links.chip(final, k) for k in range(1, links.nq)]
        self.mine = [final] + others
        self.mate = [links.core(v) for v in self.mine]
        return self.mate

    def owned(self):
        links = self.links
        _, q, c = links.here()
        mine, mate = jnp.stack(self.mine), jnp.stack(self.mate)
        both = jnp.stack([jnp.where(c == 0, mine, mate), jnp.where(c == 0, mate, mine)])
        ordered = [lax.dynamic_index_in_dim(both, q ^ j, 1) for j in range(links.nq)]
        full = jnp.concatenate(ordered, 1).astype(f32)
        outs = []
        base = 0
        for n in self.rows:
            outs.append(full[:, :, base : base + n])
            base += n
        return outs


def owned_by_kernel(links, scatters, shapes, place):
    sides = [x for s in scatters for x in s.mine + s.mate]
    nq = links.nq

    def kernel(*refs):
        ins, outs = refs[: len(sides)], refs[len(sides) :]
        rep = lax.axis_index("rep")
        q, first_core = rep // 2, rep % 2 == 0
        for at, scatter in enumerate(scatters):
            refs_here = ins[2 * nq * at : 2 * nq * (at + 1)]
            for k in range(nq):
                mine, mate = refs_here[k], refs_here[nq + k]
                chip = q ^ k
                base = 0
                for i, low, high in scatter.plan():
                    for lo, hi, left, right, out, factor, offset, zero, one in place(at, i):
                        a, b = max(lo, low), min(hi, high)
                        if a >= b:
                            continue
                        r = slice(base + a - low, base + b - low)
                        x, y = mine[r, left:right].astype(f32), mate[r, left:right].astype(f32)
                        row = pl.multiple_of(chip * factor + (offset + a - lo), 8)
                        rows = pl.ds(row, b - a)
                        wide = right - left
                        outs[out][rows, zero : zero + wide] = jnp.where(first_core, x, y)
                        outs[out][rows, one : one + wide] = jnp.where(first_core, y, x)
                    base += high - low

    return pl.pallas_call(
        kernel,
        in_specs=[pl.BlockSpec(memory_space=pltpu.VMEM)] * len(sides),
        out_specs=[pl.BlockSpec(memory_space=pltpu.VMEM)] * len(shapes),
        out_shape=[jax.ShapeDtypeStruct(s, f32) for s in shapes],
        compiler_params=pltpu.CompilerParams(vmem_limit_bytes=48 * 1024 * 1024),
        cost_estimate=HINT,
        name="owned",
    )(*sides)


def owned_feed_forward(links, scatter_1, scatter_2, w_up, w_down, w_out):
    lanes = scatter_1.lanes
    block = w_down.shape[0] // 2
    if scatter_1.parts is None or scatter_2.parts is None:
        down_first, up_first = scatter_1.owned()
        down_second, up_second, o_wout = scatter_2.owned()
        o_wdown = jnp.concatenate([side_by_side(down_first, 1), side_by_side(down_second, 1)])
        return o_wdown, up_columns(links, up_first, up_second), side_by_side(o_wout, 1)
    down_rows, up_rows = scatter_1.rows
    rq = w_up.shape[0] // links.nq
    half = block // 2

    def place(at, i):
        if i == 0:
            return [(0, down_rows, 0, lanes, 0, down_rows, at * block, 0, lanes)]
        if i == 2:
            return [(0, rq, 0, lanes, 2, rq, 0, 0, lanes)]
        out = []
        per = lanes // half
        for g in range(up_rows // rq):
            for p in range(per):
                column = (g * per + p) * 2 * block + at * block
                out.append(
                    (g * rq, (g + 1) * rq, p * half, (p + 1) * half, 1, rq, 0, column, column + half)
                )
        return out

    return owned_by_kernel(
        links, [scatter_1, scatter_2], [w_down.shape, w_up.shape, w_out.shape], place
    )


def owned_qkv(links, scatter, w_qkv):
    if scatter.parts is None:
        (grad,) = scatter.owned()
        return side_by_side(grad, 3)
    lanes = scatter.lanes
    rq = w_qkv.shape[0] // links.nq

    def place(at, i):
        return [
            (t * rq, (t + 1) * rq, 0, lanes, 0, rq, 0, 2 * t * lanes, (2 * t + 1) * lanes)
            for t in range(3)
        ]

    return owned_by_kernel(links, [scatter], [w_qkv.shape], place)[0]


def up_columns(links, first, second):
    cores, chips, _, lanes = first.shape
    both = jnp.stack([first, second])
    groups = first.shape[2] * chips * links.ns // (2 * lanes)
    rows = first.shape[2] // groups
    per = links.ns // groups
    both = both.reshape(2, cores, chips, groups, rows, per, lanes // per)
    return both.transpose(2, 4, 3, 5, 0, 1, 6).reshape(chips * rows, -1)


def side_by_side(grad, groups):
    cores, chips, rows, lanes = grad.shape
    grad = grad.reshape(cores, chips, groups, rows // groups, lanes)
    return grad.transpose(1, 3, 2, 0, 4).reshape(chips * rows // groups, groups * cores * lanes)


def total_of(links, lines):
    z, _, _ = links.here()
    lines = lines + links.core(lines)
    crossed = [links.chip(lines, k) for k in range(1, links.nq)]
    for x in crossed:
        lines = lines + x
    moved = [
        links.along(lax.dynamic_index_in_dim(lines, (z + s) % links.ns, 0, False), s)
        for s in range(1, links.ns)
    ]
    line = lax.dynamic_index_in_dim(lines, z, 0, False)
    for x in moved:
        line = line + x
    return line


def body(
    links,
    inputs,
    counts,
    ln1_gain,
    ln1_shift,
    w_qkv,
    qv_bias,
    w_out,
    out_bias,
    ln2_gain,
    ln2_shift,
    w_up,
    up_bias,
    w_down,
    down_bias,
    cotangent,
):
    ns = links.ns
    slots = inputs.shape[1]
    seq_len = inputs.shape[2]
    width = inputs.shape[3]
    n_rows = slots * seq_len
    z = lax.axis_index("shard")

    small = (ln1_gain, ln1_shift, out_bias, ln2_gain, ln2_shift, down_bias, qv_bias, up_bias)
    sizes = [v.shape[0] for v in small]
    line = w_qkv.shape[1] // 2
    n_lines = -(-sum(sizes) // line)

    gather_a, gather_b, gather_c = (
        Gather(links, [w_qkv]),
        Gather(links, [w_out, w_up]),
        Gather(links, [w_down]),
    )
    n = w_qkv.shape[0] // links.nq
    packed_a = pack(links, w_qkv, small, line)
    got = gather_along(links, packed_a)
    got_small = [g[n : n + n_lines] for g in got]
    own_a = gather_a.start(jnp.stack([g[:n] for g in got]))
    got_b = gather_along(links, tie(piece_of(links, [w_out, w_up]), own_a))
    while gather_a.done < links.bits:
        last_a = gather_a.step()
    (full_qkv,) = gather_a.full()
    all_small = jnp.stack([packed_a[n : n + n_lines]] + got_small).reshape(ns, -1)
    all_small = jnp.concatenate(
        [lax.dynamic_index_in_dim(all_small, (z - j) % ns, 0) for j in range(ns)]
    )
    full_small = []
    base = 0
    for n in sizes:
        full_small.append(all_small[:, base : base + n].reshape(-1).astype(f32))
        base += n
    full_g1, full_s1, full_bout, full_g2, full_s2, full_bdown, bias_f, full_bup = full_small
    first_slot = z * slots
    alive = (jnp.arange(slots, dtype=jnp.int32) + first_slot < counts[0]).astype(f32)
    assert slots == 1
    d_out_b = jnp.where(alive[0] > 0, cotangent, jnp.zeros_like(cotangent)).reshape(n_rows, width)
    tokens_b = inputs.reshape(n_rows, width)
    hidden_one_b = layer_norm(tokens_b.astype(f32), full_g1, full_s1).astype(bf16)
    projected = matmul(hidden_one_b, full_qkv)
    none = jnp.zeros((width,), f32)
    qkv_bias = jnp.concatenate([bias_f[:width], none, bias_f[width:]])
    qkv_b = (projected + qkv_bias).astype(bf16)
    pairs = width // (2 * HDIM)
    cuts = (0, pairs // 4, pairs * 3 // 4, pairs)
    qkv_b, got_b = meet(qkv_b, got_b)
    got_c = gather_along(links, tie(piece_of(links, [w_down]), got_b))
    gather_b.start(jnp.stack(got_b))
    gather_b.step()
    kept = attend(qkv_b, cuts[0], cuts[1])
    kept, gather_b.held = meet(kept, gather_b.held)
    while gather_b.done < links.bits:
        gather_b.step()
    kept = attend(qkv_b, cuts[1], cuts[2], kept)
    kept, gather_b.mine, got_c = meet(kept, gather_b.mine, got_c)
    gather_c.start(jnp.stack(got_c))
    while gather_c.done < links.bits - 1:
        gather_c.step()
    kept = attend(qkv_b, cuts[2], cuts[3], kept)
    kept, gather_c.held = meet(kept, gather_c.held)
    gather_c.step()
    attended_b, inverse, probs_b = kept
    full_wout, full_wup = gather_b.full()
    gain_two = full_g2[None]
    middle, hidden_two_b = middle_of(
        tokens_b, attended_b, full_wout, full_bout[None], gain_two, full_s2[None]
    )
    middle, gather_c.mine = meet(middle, gather_c.mine)
    (full_wdown,) = gather_c.full()
    bias_up = full_bup[None]
    last_bias = full_bdown[None]
    y, g, away, home, gb_first = feed_forward(
        links, hidden_two_b, d_out_b, full_wup, bias_up, full_wdown, alive, last_bias, middle, None, 0
    )
    scatter_1 = Scatter(links, away, home)
    output, g, away, home, gb_second = feed_forward(
        links, hidden_two_b, d_out_b, full_wup, bias_up, full_wdown, alive, last_bias, y, g, 1
    )
    output = output.reshape(inputs.shape)
    grad_bup = jnp.concatenate([gb_first, gb_second], 1)
    g, scatter_1.kept = meet(g, scatter_1.kept)
    g, scatter_1.buffers = meet(g, scatter_1.prepare())
    scatter_1.send()
    d_mid, d_att_b, out_away, out_home, sums = middle_back(
        links, g, middle, d_out_b, attended_b, full_wout, gain_two
    )
    grad_g2, grad_s2, grad_bout, grad_bdown = (sums[i] for i in range(4))
    scatter_2 = Scatter(links, away + [out_away], home + [out_home])
    d_att_b, scatter_2.kept = meet(d_att_b, scatter_2.kept)
    d_att_b, scatter_2.buffers = meet(d_att_b, scatter_2.prepare())
    scatter_2.send()
    half = pairs // 2
    grads = attend_back(qkv_b, d_att_b, attended_b, inverse, probs_b, 0, half)
    grads, scatter_1.held, scatter_2.held = meet(grads, scatter_1.held, scatter_2.held)
    grads, scatter_1.buffers, scatter_2.buffers = meet(
        grads, scatter_1.prepare(), scatter_2.prepare()
    )
    scatter_1.send()
    scatter_2.send()
    grads = attend_back(qkv_b, d_att_b, attended_b, inverse, probs_b, half, pairs, grads)
    grads, scatter_1.held, scatter_2.held = meet(grads, scatter_1.held, scatter_2.held)
    grads, scatter_1.buffers, scatter_2.buffers = meet(
        grads, scatter_1.prepare_along(), scatter_2.prepare_along()
    )
    scatter_1.send_along()
    d_qkv, qv_sums = grads
    scatter_3 = Scatter(links, *weight_grads(links, hidden_one_b, d_qkv))
    scatter_3.kept, scatter_2.buffers = meet(scatter_3.kept, scatter_2.buffers)
    scatter_2.send_along()
    d_qkv, scatter_3.buffers = meet(d_qkv, scatter_3.prepare())
    scatter_3.send()
    input_grad, entry_sums = entry_back(d_qkv, full_qkv, tokens_b, d_mid, full_g1[None])
    grad_g1, grad_s1 = entry_sums[0], entry_sums[1]
    grad_qvb = qv_sums.reshape(-1)
    input_grad, scatter_1.final = meet(input_grad, scatter_1.final)
    scatter_1.spread()
    input_grad, scatter_3.held = meet(input_grad, scatter_3.held)
    input_grad = input_grad.reshape(inputs.shape)
    grad_g1, scatter_3.buffers, scatter_2.final = meet(
        grad_g1, scatter_3.prepare(), scatter_2.final
    )
    scatter_3.send()
    scatter_2.spread()
    scatter_3.buffers = scatter_3.prepare_along()
    scatter_3.send_along()
    scatter_3.final, scatter_1.mate, scatter_2.mate = meet(
        scatter_3.final, scatter_1.mate, scatter_2.mate
    )
    scatter_3.spread()
    o_wdown, o_wup, o_wout = owned_feed_forward(links, scatter_1, scatter_2, w_up, w_down, w_out)
    o_qkv = owned_qkv(links, scatter_3, w_qkv)
    small_grads = (grad_g1, grad_s1, grad_bout, grad_g2, grad_s2, grad_bdown, grad_qvb, grad_bup)
    joined = jnp.concatenate([g.reshape(ns, -1) for g in small_grads], 1)
    joined = total_of(links, joined)
    owned = []
    base = 0
    for n in sizes:
        owned.append(joined[base : base + n])
        base += n
    o_g1, o_s1, o_bout, o_g2, o_s2, o_bdown, o_qvb, o_bup = owned
    return (
        output,
        input_grad,
        o_g1,
        o_s1,
        o_qkv,
        o_qvb,
        o_wout,
        o_bout,
        o_g2,
        o_s2,
        o_wup,
        o_bup,
        o_wdown,
        o_bdown,
    )


def solution(mesh):
    tokens = P("rep", "shard", None, None)
    vector = P("shard")
    matrix = P("shard", None)
    return jax.shard_map(
        functools.partial(body, Links(mesh)),
        mesh=mesh,
        in_specs=(
            tokens,
            P("rep"),
            vector,
            vector,
            matrix,
            vector,
            matrix,
            vector,
            vector,
            vector,
            matrix,
            vector,
            matrix,
            vector,
            tokens,
        ),
        out_specs=(
            tokens,
            tokens,
            vector,
            vector,
            matrix,
            vector,
            matrix,
            vector,
            vector,
            vector,
            matrix,
            vector,
            matrix,
            vector,
        ),
        check_vma=False,
    )
```

```python
import functools

import jax
import jax.numpy as jnp
from jax import lax
from jax.experimental import pallas as pl
from jax.experimental.pallas import tpu as pltpu
from jax.sharding import PartitionSpec as P

HDIM = 64

eps = 1e-06
bf16 = jnp.bfloat16
LIGHT = pl.CostEstimate(flops=1, transcendentals=0, bytes_accessed=1)
HEAVY = pl.CostEstimate(flops=20_000_000_000, transcendentals=0, bytes_accessed=10_000_000)
f32 = jnp.float32


def layer_norm(values, gain, shift):
    centre = values - jnp.mean(values, -1, keepdims=True)
    spread = jnp.mean(centre * centre, -1, keepdims=True)
    return centre * lax.rsqrt(spread + eps) * gain + shift


def matmul(left, right):
    return jnp.dot(left, right, preferred_element_type=f32)


LOG2E = 1.4426950408889634


def contract(left, right, left_dim, right_dim):
    return lax.dot_general(
        left, right, (((left_dim,), (right_dim,)), ((), ())), preferred_element_type=f32
    )


def query_blocks(rows, tile=256):
    return [(i, min(tile, rows - i)) for i in range(0, rows, tile)]


def head_mask(head, rows, dtype):
    lane = lax.broadcasted_iota(jnp.int32, (rows, 2 * HDIM), 1)
    return (lane // HDIM == head).astype(dtype)


def attend_kernel(q_ref, k_ref, v_ref, o_ref, inv_ref, p_ref):
    rows = q_ref.shape[0]
    factor = HDIM ** (-0.5) * LOG2E
    keys = k_ref[...]
    values = v_ref[...]
    ones = jnp.ones(values.shape, bf16)
    for start, n in query_blocks(rows):
        queries = q_ref[start : start + n, :]
        mixed = inverse = None
        for head in range(2):
            mask = head_mask(head, rows, bf16)
            scores = contract(keys * mask, queries, 1, 1)
            largest = jnp.max(scores, axis=0, keepdims=True)
            probs = jnp.exp2((scores - largest) * factor).astype(bf16)
            p_ref[head, :, start : start + n] = probs
            both = contract(probs, jnp.concatenate([values * mask, ones], 1), 0, 0)
            inv = 1.0 / both[:, 2 * HDIM :]
            part = both[:, : 2 * HDIM] * inv
            share = head_mask(head, n, f32) * inv
            mixed = part if mixed is None else mixed + part
            inverse = share if inverse is None else inverse + share
        o_ref[start : start + n, :] = mixed.astype(bf16)
        inv_ref[start : start + n, :] = inverse


def whole(count):
    return [pl.BlockSpec(memory_space=pl.ANY)] * count


def attend(qkv, first, last, before=None):
    rows, wide = qkv.shape
    width = wide // 3
    pairs = width // (2 * HDIM)
    count = last - first

    def column(offset):
        return pl.BlockSpec((rows, 2 * HDIM), lambda j: (0, offset + first + j))

    def kernel(*refs):
        attend_kernel(*refs[:3], *refs[-3:])

    given = () if before is None else tuple(before)
    return pl.pallas_call(
        kernel,
        grid=(count,),
        in_specs=[column(0), column(pairs), column(2 * pairs)] + whole(len(given)),
        out_specs=[
            column(0),
            column(0),
            pl.BlockSpec((2, rows, rows), lambda j: (first + j, 0, 0)),
        ],
        out_shape=[
            jax.ShapeDtypeStruct((rows, width), bf16),
            jax.ShapeDtypeStruct((rows, width), f32),
            jax.ShapeDtypeStruct((2 * pairs, rows, rows), bf16),
        ],
        input_output_aliases={3 + i: i for i in range(len(given))},
        compiler_params=pltpu.CompilerParams(vmem_limit_bytes=56 * 1024 * 1024),
        cost_estimate=HEAVY,
        name="attend",
    )(qkv, qkv, qkv, *given)


def attend_back_kernel(
    q_ref, k_ref, v_ref, d_ref, o_ref, inv_ref, p_ref, out_ref, sum_ref
):
    rows = q_ref.shape[0]
    scale = HDIM ** (-0.5)
    queries = q_ref[...]
    keys = k_ref[...]
    values = v_ref[...]
    grads = (d_ref[...].astype(f32) * inv_ref[...]).astype(bf16)
    product = grads.astype(f32) * o_ref[...].astype(f32)
    lane = lax.broadcasted_iota(jnp.int32, (rows, 2 * HDIM), 1)
    blocks = query_blocks(rows)
    d_queries = [None] * len(blocks)
    d_keys = d_values = None
    for head in range(2):
        mask = head_mask(head, rows, bf16)
        inner = -jnp.sum(jnp.where(lane // HDIM == head, product, 0.0), 1, keepdims=True)
        high = inner.astype(bf16)
        low = (inner - high.astype(f32)).astype(bf16)
        tail = jnp.where(lane == 0, high, jnp.where(lane == 1, low, jnp.zeros_like(low)))
        grads_wide = jnp.concatenate([grads, tail], 1)
        values_wide = jnp.concatenate([values * mask, (lane < 2).astype(bf16)], 1)
        keys_h, queries_h, grads_h = keys * mask, queries * mask, grads * mask
        for b, (start, n) in enumerate(blocks):
            d_probs = contract(values_wide, grads_wide[start : start + n, :], 1, 1)
            probs = p_ref[head, :, start : start + n]
            d_scores = probs * d_probs.astype(bf16)
            to_values = contract(probs, grads_h[start : start + n, :], 1, 0)
            to_keys = contract(d_scores, queries_h[start : start + n, :], 1, 0)
            to_queries = contract(d_scores, keys_h, 0, 0)
            d_values = to_values if d_values is None else d_values + to_values
            d_keys = to_keys if d_keys is None else d_keys + to_keys
            d_queries[b] = to_queries if d_queries[b] is None else d_queries[b] + to_queries
    d_values = d_values.astype(bf16)
    out_ref[1] = (d_keys * scale).astype(bf16)
    out_ref[2] = d_values
    sums = jnp.zeros((1, 2 * HDIM), f32)
    for b, (start, n) in enumerate(blocks):
        block = (d_queries[b] * scale).astype(bf16)
        out_ref[0, start : start + n, :] = block
        sums = sums + jnp.sum(block.astype(f32), 0, keepdims=True)
    sum_ref[0] = sums
    sum_ref[1] = jnp.sum(d_values.astype(f32), 0, keepdims=True)


def attend_back(qkv, grad, attended, inverse, probs, first, last, before=None):
    rows, wide = qkv.shape
    width = wide // 3
    pairs = width // (2 * HDIM)
    count = last - first

    def column(offset):
        return pl.BlockSpec((rows, 2 * HDIM), lambda j: (0, offset + first + j))

    def kernel(*refs):
        attend_back_kernel(*refs[:7], *refs[-2:])

    given = () if before is None else tuple(before)
    return pl.pallas_call(
        kernel,
        grid=(count,),
        in_specs=[column(0), column(pairs), column(2 * pairs)]
        + [column(0)] * 3
        + [pl.BlockSpec((2, rows, rows), lambda j: (first + j, 0, 0))]
        + whole(len(given)),
        out_specs=[
            pl.BlockSpec((3, rows, 2 * HDIM), lambda j: (0, 0, first + j)),
            pl.BlockSpec((2, 1, 2 * HDIM), lambda j: (0, 0, first + j)),
        ],
        out_shape=[
            jax.ShapeDtypeStruct((3, rows, width), bf16),
            jax.ShapeDtypeStruct((2, 1, width), f32),
        ],
        input_output_aliases={7 + i: i for i in range(len(given))},
        compiler_params=pltpu.CompilerParams(vmem_limit_bytes=56 * 1024 * 1024),
        cost_estimate=HEAVY,
        name="attend_back",
    )(qkv, qkv, qkv, grad, attended, inverse, probs, *given)


def gelu_pair(values):
    bell = jnp.exp2(values * values * (-0.5 * LOG2E))
    t = 1.0 / (1.0 + 0.23164189 * jnp.abs(values))
    poly = 0.5307027145 * t - 0.7265760135
    poly = poly * t + 0.7107068705
    poly = poly * t - 0.142248368
    poly = poly * t + 0.127414796
    tail = poly * t * bell
    area = jnp.where(values >= 0, 1.0 - tail, tail)
    return values * area, area + values * bell * 0.3989422804014327


def feed_forward_kernel(
    h_ref, dm_ref, up_ref, bias_ref, down_ref, alive_ref, last_ref, y0_ref, g0_ref,
    y_ref, g_ref, down_away, down_home, up_away, up_home, gb_ref,
    act_ref, dp_ref, y_acc, g_acc,
):
    j = pl.program_id(0)

    @pl.when(j == 0)
    def _():
        if g0_ref is None:
            y_acc[...] = y0_ref[...] + last_ref[...]
            g_acc[...] = jnp.zeros_like(g_acc)
        else:
            y_acc[...] = y0_ref[...]
            g_acc[...] = g0_ref[...]

    rows = h_ref.shape[0]
    up, down = up_ref[...], down_ref[...]
    bias = bias_ref[...]
    chunk = 368
    for start in range(0, rows, chunk):
        r = slice(start, min(start + chunk, rows))
        act, slope = gelu_pair(contract(h_ref[r, :], up, 1, 0) + bias)
        act = act.astype(bf16)
        act_ref[r, :] = act
        d_pre = (contract(dm_ref[r, :], down, 1, 1) * slope).astype(bf16)
        dp_ref[r, :] = d_pre
        y_acc[r, :] += contract(act, down, 1, 0)
        g_acc[r, :] += contract(d_pre, up, 1, 1)
    gb_ref[...] = jnp.sum(dp_ref[...].astype(f32), 0, keepdims=True)[None]
    first_core = lax.axis_index("rep") % 2 == 0
    for left, right, away, home in (
        (act_ref, dm_ref, down_away, down_home),
        (h_ref, dp_ref, up_away, up_home),
    ):
        grad = contract(left[...], right[...], 0, 0)
        half = grad.shape[1] // 2
        low, high = grad[:, :half], grad[:, half:]
        away[...] = jnp.where(first_core, high, low).reshape(away.shape).astype(bf16)
        home[...] = jnp.where(first_core, low, high).reshape(home.shape).astype(bf16)

    @pl.when(j == pl.num_programs(0) - 1)
    def _():
        y = y_acc[...]
        y_ref[...] = y if g0_ref is None else (alive_ref[0] * y).astype(bf16)
        g_ref[...] = g_acc[...]


def feed_forward(links, hidden, d_out, up, bias, down, alive, last_bias, y0, g0, part):
    ns, nq = links.ns, links.nq
    rows, width = hidden.shape
    block = up.shape[1] // (2 * ns)
    rq = width // (ns * nq)
    per = width // block
    wide = dict(pipeline_mode=pl.Buffered(1))

    def full():
        return pl.BlockSpec((rows, width), lambda j: (0, 0), **wide)

    def kernel(*refs):
        refs = list(refs)
        if g0 is None:
            refs.insert(8, None)
        feed_forward_kernel(*refs)

    down_spec = pl.BlockSpec((1, block, width // 2), lambda j: (j, 0, 0))
    up_spec = pl.BlockSpec((ns, nq, 1, rq, block // 2), lambda j: (0, 0, j // per, 0, j % per))
    down_shape = jax.ShapeDtypeStruct((ns, block, width // 2), bf16)
    up_shape = jax.ShapeDtypeStruct((ns, nq, ns // per, rq, width // 2), bf16)
    sums = jax.ShapeDtypeStruct((rows, width), f32)
    given = (y0,) if g0 is None else (y0, g0)
    y, g, d_away, d_home, u_away, u_home, gb = pl.pallas_call(
        kernel,
        grid=(ns,),
        in_specs=[
            full(),
            full(),
            pl.BlockSpec((width, block), lambda j: (0, 2 * j + part)),
            pl.BlockSpec((1, block), lambda j: (0, 2 * j + part)),
            pl.BlockSpec((block, width), lambda j: (2 * j + part, 0)),
            pl.BlockSpec(memory_space=pltpu.SMEM),
            pl.BlockSpec((1, width), lambda j: (0, 0)),
        ]
        + [full() for _ in given],
        out_specs=[
            full(),
            full(),
            down_spec,
            down_spec,
            up_spec,
            up_spec,
            pl.BlockSpec((1, 1, block), lambda j: (j, 0, 0)),
        ],
        out_shape=[
            sums if g0 is None else jax.ShapeDtypeStruct((rows, width), bf16),
            sums,
            down_shape,
            down_shape,
            up_shape,
            up_shape,
            jax.ShapeDtypeStruct((ns, 1, block), f32),
        ],
        scratch_shapes=[
            pltpu.VMEM((rows, block), bf16),
            pltpu.VMEM((rows, block), bf16),
            pltpu.VMEM((rows, width), f32),
            pltpu.VMEM((rows, width), f32),
        ],
        compiler_params=pltpu.CompilerParams(vmem_limit_bytes=58 * 1024 * 1024),
        cost_estimate=HEAVY,
        name="feed_forward",
    )(hidden, d_out, up, bias, down, alive, last_bias, *given)

    def pieces(down_grad, up_grad):
        lanes = width // 2
        return [
            down_grad.reshape(ns, nq, block // nq, lanes),
            up_grad.reshape(ns, nq, ns // per * rq, lanes),
        ]

    return y, g, pieces(d_away, u_away), pieces(d_home, u_home), gb.reshape(ns, block)


def grad_kernel(left_ref, right_ref, away_ref, home_ref):
    grad = contract(left_ref[...], right_ref[0], 0, 0)
    half = grad.shape[1] // 2
    low, high = grad[:, :half], grad[:, half:]
    first_core = lax.axis_index("rep") % 2 == 0
    away_ref[...] = jnp.where(first_core, high, low).reshape(away_ref.shape).astype(bf16)
    home_ref[...] = jnp.where(first_core, low, high).reshape(home_ref.shape).astype(bf16)


def weight_grads(links, left, rights):
    ns, nq = links.ns, links.nq
    rows, width = left.shape
    count, _, wide = rights.shape
    rq = width // (ns * nq)
    spec = pl.BlockSpec((ns, nq, 1, rq, wide // 2), lambda i: (0, 0, i, 0, 0))
    shape = jax.ShapeDtypeStruct((ns, nq, count, rq, wide // 2), bf16)
    away, home = pl.pallas_call(
        grad_kernel,
        grid=(count,),
        in_specs=[
            pl.BlockSpec((rows, width), lambda i: (0, 0)),
            pl.BlockSpec((1, rows, wide), lambda i: (i, 0, 0)),
        ],
        out_specs=[spec, spec],
        out_shape=[shape, shape],
        compiler_params=pltpu.CompilerParams(vmem_limit_bytes=48 * 1024 * 1024),
        cost_estimate=HEAVY,
        name="weight_grads",
    )(left, rights)
    flat = (ns, nq, count * rq, wide // 2)
    return [away.reshape(flat)], [home.reshape(flat)]


def row_block(rows):
    return 368 if rows % 368 == 0 else rows


def normal(values):
    centre = values - jnp.mean(values, -1, keepdims=True)
    scale = lax.rsqrt(jnp.mean(centre * centre, -1, keepdims=True) + eps)
    return centre * scale, scale


def normal_back(unit, scale, grad):
    inner = jnp.mean(grad * unit, -1, keepdims=True)
    return scale * (grad - jnp.mean(grad, -1, keepdims=True) - unit * inner)


def column_sum(values):
    return jnp.sum(values, 0, keepdims=True)


def middle_kernel(x_ref, att_ref, w_ref, bias_ref, gain_ref, shift_ref, mid_ref, h_ref):
    mid = x_ref[...].astype(f32) + contract(att_ref[...], w_ref[...], 1, 0) + bias_ref[...]
    mid_ref[...] = mid
    unit, _ = normal(mid)
    h_ref[...] = (unit * gain_ref[...] + shift_ref[...]).astype(bf16)


def middle_of(tokens, attended, weight, bias, gain, shift):
    rows, width = tokens.shape
    n = row_block(rows)
    block = pl.BlockSpec((n, width), lambda i: (i, 0))
    line = pl.BlockSpec((1, width), lambda i: (0, 0))
    return pl.pallas_call(
        middle_kernel,
        grid=(rows // n,),
        in_specs=[block, block, pl.BlockSpec(weight.shape, lambda i: (0, 0)), line, line, line],
        out_specs=[block, block],
        out_shape=[
            jax.ShapeDtypeStruct((rows, width), f32),
            jax.ShapeDtypeStruct((rows, width), bf16),
        ],
        compiler_params=pltpu.CompilerParams(vmem_limit_bytes=48 * 1024 * 1024),
        cost_estimate=HEAVY,
        name="middle",
    )(tokens, attended, weight, bias, gain, shift)


def middle_back_kernel(
    g_ref, mid_ref, dm_ref, att_ref, w_ref, gain_ref,
    d_mid_ref, d_att_ref, away_ref, home_ref, sum_ref, acc_ref,
):
    i = pl.program_id(0)

    @pl.when(i == 0)
    def _():
        acc_ref[...] = jnp.zeros_like(acc_ref)
        sum_ref[...] = jnp.zeros_like(sum_ref)

    unit, scale = normal(mid_ref[...])
    g = g_ref[...]
    d_out = dm_ref[...].astype(f32)
    d_mid = d_out + normal_back(unit, scale, g * gain_ref[...])
    d_mid_ref[...] = d_mid
    d_proj = d_mid.astype(bf16)
    d_att_ref[...] = contract(d_proj, w_ref[...], 1, 1).astype(bf16)
    acc_ref[...] += contract(att_ref[...], d_proj, 0, 0)
    sum_ref[0:1, :] += column_sum(g * unit)
    sum_ref[1:2, :] += column_sum(g)
    sum_ref[2:3, :] += column_sum(d_proj.astype(f32))
    sum_ref[3:4, :] += column_sum(d_out)

    @pl.when(i == pl.num_programs(0) - 1)
    def _():
        grad = acc_ref[...]
        half = grad.shape[1] // 2
        low, high = grad[:, :half], grad[:, half:]
        first_core = lax.axis_index("rep") % 2 == 0
        away_ref[...] = jnp.where(first_core, high, low).reshape(away_ref.shape).astype(bf16)
        home_ref[...] = jnp.where(first_core, low, high).reshape(home_ref.shape).astype(bf16)


def middle_back(links, grad, middle, d_out, attended, weight, gain):
    ns, nq = links.ns, links.nq
    rows, width = middle.shape
    n = row_block(rows)
    block = pl.BlockSpec((n, width), lambda i: (i, 0))
    pieces = (ns, nq, width // (ns * nq), width // 2)
    whole_piece = pl.BlockSpec(pieces, lambda i: (0, 0, 0, 0))
    return pl.pallas_call(
        middle_back_kernel,
        grid=(rows // n,),
        in_specs=[block] * 4
        + [
            pl.BlockSpec(weight.shape, lambda i: (0, 0)),
            pl.BlockSpec((1, width), lambda i: (0, 0)),
        ],
        out_specs=[
            block,
            block,
            whole_piece,
            whole_piece,
            pl.BlockSpec((8, width), lambda i: (0, 0)),
        ],
        out_shape=[
            jax.ShapeDtypeStruct((rows, width), f32),
            jax.ShapeDtypeStruct((rows, width), bf16),
            jax.ShapeDtypeStruct(pieces, bf16),
            jax.ShapeDtypeStruct(pieces, bf16),
            jax.ShapeDtypeStruct((8, width), f32),
        ],
        scratch_shapes=[pltpu.VMEM((width, width), f32)],
        compiler_params=pltpu.CompilerParams(vmem_limit_bytes=48 * 1024 * 1024),
        cost_estimate=HEAVY,
        name="middle_back",
    )(grad, middle, d_out, attended, weight, gain)


def entry_back_kernel(d_ref, w_ref, x_ref, d_mid_ref, gain_ref, out_ref, sum_ref):
    @pl.when(pl.program_id(0) == 0)
    def _():
        sum_ref[...] = jnp.zeros_like(sum_ref)

    width = x_ref.shape[1]
    g = contract(d_ref[0], w_ref[:, :width], 1, 1)
    for t in range(1, 3):
        g = g + contract(d_ref[t], w_ref[:, t * width : (t + 1) * width], 1, 1)
    unit, scale = normal(x_ref[...].astype(f32))
    out_ref[...] = d_mid_ref[...] + normal_back(unit, scale, g * gain_ref[...])
    sum_ref[0:1, :] += column_sum(g * unit)
    sum_ref[1:2, :] += column_sum(g)


def entry_back(grads, weight, tokens, d_mid, gain):
    rows, width = tokens.shape
    n = row_block(rows)
    block = pl.BlockSpec((n, width), lambda i: (i, 0))
    return pl.pallas_call(
        entry_back_kernel,
        grid=(rows // n,),
        in_specs=[
            pl.BlockSpec((3, n, width), lambda i: (0, i, 0)),
            pl.BlockSpec(weight.shape, lambda i: (0, 0), pipeline_mode=pl.Buffered(1)),
            block,
            block,
            pl.BlockSpec((1, width), lambda i: (0, 0)),
        ],
        out_specs=[block, pl.BlockSpec((8, width), lambda i: (0, 0))],
        out_shape=[
            jax.ShapeDtypeStruct((rows, width), f32),
            jax.ShapeDtypeStruct((8, width), f32),
        ],
        compiler_params=pltpu.CompilerParams(vmem_limit_bytes=48 * 1024 * 1024),
        cost_estimate=HEAVY,
        name="entry_back",
    )(grads, weight, tokens, d_mid, gain)


class Links:
    def __init__(self, mesh):
        self.ns = mesh.shape["shard"]
        self.nr = mesh.shape["rep"]
        self.nq = self.nr // 2
        self.bits = self.nq.bit_length() - 1
        assert 1 << self.bits == self.nq

    def here(self):
        rep = lax.axis_index("rep")
        return lax.axis_index("shard"), rep // 2, rep % 2

    def along(self, values, step):
        return lax.ppermute(values, "shard", [(i, (i + step) % self.ns) for i in range(self.ns)])

    def chip(self, values, k):
        return lax.ppermute(values, "rep", [(i, i ^ (2 * k)) for i in range(self.nr)])

    def core(self, values):
        return lax.ppermute(values, "rep", [(i, i ^ 1) for i in range(self.nr)])


def meet(*values):
    return lax.optimization_barrier(values)


def tie(values, others):
    return lax.optimization_barrier((values, others))[0]


def piece_of(links, weights):
    _, q, c = links.here()
    parts = []
    for w in weights:
        rq, half = w.shape[0] // links.nq, w.shape[1] // 2
        parts.append(lax.dynamic_slice(w, (q * rq, c * half), (rq, half)))
    return jnp.concatenate(parts, 1)


def pack(links, weight, small, line):
    rq = weight.shape[0] // links.nq
    total = sum(v.shape[0] for v in small)
    fits = all(sum(v.shape[0] for v in part) == line for part in (small[:6], small[6:]))
    if rq % 16 or line % 128 or not fits:
        filled = jnp.concatenate(small + (jnp.zeros((-total % line,), bf16),)).reshape(-1, line)
        filler = jnp.zeros((16 - filled.shape[0], line), bf16)
        return jnp.concatenate([piece_of(links, [weight]), filled, filler])

    def kernel(w_ref, *refs):
        *vectors, out_ref, sem = refs
        rep = lax.axis_index("rep")
        q, c = rep // 2, rep % 2
        rows = pl.ds(pl.multiple_of(q * rq, rq), rq)
        copy = pltpu.make_async_copy(
            w_ref.at[rows, pl.ds(pl.multiple_of(c * line, line), line)], out_ref.at[:rq], sem
        )
        copy.start()
        lines = [[], []]
        for at, ref in enumerate(vectors):
            lines[at // 6].append(ref[...].astype(f32).reshape(1, -1))
        block = [jnp.concatenate(x, 1) for x in lines]
        row = lax.broadcasted_iota(jnp.int32, (16, line), 0)
        filled = jnp.where(row == 0, block[0], jnp.where(row == 1, block[1], 0.0))
        out_ref[rq:, :] = filled.astype(bf16)
        copy.wait()

    return pl.pallas_call(
        kernel,
        in_specs=whole(1) + [pl.BlockSpec(memory_space=pltpu.VMEM)] * len(small),
        out_specs=pl.BlockSpec(memory_space=pltpu.VMEM),
        out_shape=jax.ShapeDtypeStruct((rq + 16, line), bf16),
        scratch_shapes=[pltpu.SemaphoreType.DMA(())],
        cost_estimate=LIGHT,
        name="pack",
    )(weight, *small)


def gather_along(links, piece):
    return [links.along(piece, s) for s in range(1, links.ns)]


def lanes_of(links, values, part):
    n = values.shape[-1] // links.bits
    return values[..., part * n : (part + 1) * n]


def assemble(links, weights, got_mine, got_mate):
    ns, nq, bits = links.ns, links.nq, links.bits
    rows = [w.shape[0] for w in weights]
    cols = [w.shape[1] for w in weights]
    rq = [r // nq for r in rows]
    total = sum(cols) // 2
    lanes = total // bits
    n = len(weights)
    per_side = len(got_mine)

    def kernel(*refs):
        w_refs = refs[:n]
        sides = (refs[n : n + per_side], refs[n + per_side : n + 2 * per_side])
        out_refs = refs[n + 2 * per_side : n + 2 * per_side + n]
        sem = refs[-1]
        z = lax.axis_index("shard")
        rep = lax.axis_index("rep")
        q, c = rep // 2, rep % 2
        copies = []

        def go(src, dst):
            copy = pltpu.make_async_copy(src, dst, sem.at[len(copies)])
            copy.start()
            copies.append(copy)

        for i in range(n):
            go(w_refs[i], out_refs[i].at[pl.ds(pl.multiple_of(z * rows[i], rows[i]), rows[i]), :])
        for side, parts in enumerate(sides):
            core = c if side == 0 else 1 - c
            base = 0
            for i in range(n):
                half = cols[i] // 2

                def place(source, k, s, low, high):
                    zs = lax.rem(z + (ns - s), ns)
                    at = pl.ds(pl.multiple_of(zs * rows[i] + (q ^ k) * rq[i], rq[i]), rq[i])
                    to = pl.ds(pl.multiple_of(core * half + (low - base), 128), high - low)
                    go(source, out_refs[i].at[at, to])

                for s in range(1, ns):
                    own = parts[0].at[s - 1, :, pl.ds(base, half)]
                    place(own, 0, s, base, base + half)
                    at = 1
                    for step in range(bits):
                        for part in range(bits):
                            known = [0]
                            for t in range(step):
                                bit = 1 << ((part + t) % bits)
                                known = known + [k ^ bit for k in known]
                            known = sorted(known)
                            bit = 1 << ((part + step) % bits)
                            low = max(base, part * lanes)
                            high = min(base + half, (part + 1) * lanes)
                            if low < high:
                                cut = pl.ds(low - part * lanes, high - low)
                                for j, k in enumerate(known):
                                    source = parts[at].at[j, s - 1, :, cut]
                                    place(source, k ^ bit, s, low, high)
                            at += 1
                base += half
        for copy in copies:
            copy.wait()

    pieces = 0
    base = 0
    for i in range(n):
        half = cols[i] // 2
        for part in range(bits):
            if max(base, part * lanes) < min(base + half, (part + 1) * lanes):
                pieces += nq - 1
        pieces += 1
        base += half
    count = n + 2 * (ns - 1) * pieces
    return pl.pallas_call(
        kernel,
        out_shape=[jax.ShapeDtypeStruct((ns * r, c), bf16) for r, c in zip(rows, cols)],
        in_specs=whole(n + 2 * per_side),
        out_specs=[pl.BlockSpec(memory_space=pltpu.VMEM)] * n,
        scratch_shapes=[pltpu.SemaphoreType.DMA((count,))],
        compiler_params=pltpu.CompilerParams(vmem_limit_bytes=32 * 1024 * 1024),
        cost_estimate=LIGHT,
        name="assemble",
    )(*weights, *got_mine, *got_mate)


class Gather:
    def __init__(self, links, weights):
        self.links, self.weights = links, weights

    def start(self, own):
        self.own = own
        self.held = [{0: lanes_of(self.links, own, p)} for p in range(self.links.bits)]
        self.mine = [own]
        self.mate = [self.links.core(own)]
        self.done = 0
        return own

    def send(self):
        self.arrived = [
            self.links.chip(jnp.stack([pieces[k] for k in sorted(pieces)]), self.bit(part))
            for part, pieces in enumerate(self.held)
        ]

    def bit(self, part):
        return 1 << ((part + self.done) % self.links.bits)

    def absorb(self):
        for part, (pieces, values) in enumerate(zip(self.held, self.arrived)):
            for i, k in enumerate(sorted(pieces)):
                pieces[k ^ self.bit(part)] = values[i]
            self.mine.append(values)
            self.mate.append(self.links.core(values))
        self.done += 1

    def full(self):
        return assemble(self.links, self.weights, self.mine, self.mate)


class Scatter:
    def __init__(self, links, sent, kept):
        self.links = links
        self.rows = [s.shape[2] for s in sent]
        self.lanes = sent[0].shape[3]
        self.got = [links.core(s) for s in sent]
        self.kept = kept
        self.done = 0
        total = sum(self.rows)
        if links.bits == 2 and all(n % 32 == 0 for n in self.rows):
            first = []
            second = []
            taken = 0
            for i, n in enumerate(self.rows):
                cut = min(n, total // 2 - taken)
                if len(self.rows) == 3:
                    cut = (n, 0, n // 2)[i]
                taken += cut
                if cut:
                    first.append((i, 0, cut))
                if cut < n:
                    second.append((i, cut, n))
            self.parts = [first, second]
        else:
            self.parts = None

    def plan(self):
        if self.parts is None:
            return [(i, 0, n) for i, n in enumerate(self.rows)]
        return self.parts[0] + self.parts[1]

    def blocks(self):
        links = self.links
        ns, nq, lanes = links.ns, links.nq, self.lanes
        n = len(self.rows)
        sizes = [sum(high - low for _, low, high in part) for part in self.parts]

        def kernel(*refs):
            kept, got, outs = refs[:n], refs[n : 2 * n], refs[2 * n :]
            q = lax.axis_index("rep") // 2
            for p, part in enumerate(self.parts):
                bit = 1 << p
                for at, k in enumerate([k for k in range(nq) if not k & bit]):
                    for out, chip in ((outs[2 * p], k ^ bit), (outs[2 * p + 1], k)):
                        base = 0
                        for i, low, high in part:
                            a = kept[i][0, q ^ chip, low:high, :].astype(f32)
                            b = got[i][0, q ^ chip, low:high, :].astype(f32)
                            out[at, 0, base : base + high - low, :] = (a + b).astype(bf16)
                            base += high - low

        return pl.pallas_call(
            kernel,
            grid=(ns,),
            in_specs=[pl.BlockSpec((1, nq, r, lanes), lambda j: (j, 0, 0, 0)) for r in self.rows] * 2,
            out_specs=[
                pl.BlockSpec((nq // 2, 1, r, lanes), lambda j: (0, j, 0, 0))
                for r in sizes
                for _ in range(2)
            ],
            out_shape=[
                jax.ShapeDtypeStruct((nq // 2, ns, r, lanes), bf16) for r in sizes for _ in range(2)
            ],
            compiler_params=pltpu.CompilerParams(vmem_limit_bytes=32 * 1024 * 1024),
            cost_estimate=LIGHT,
            name="core_sums",
        )(*self.kept, *self.got)

    def prepare(self):
        links = self.links
        if self.done == 0 and self.parts is not None:
            s0, k0, s1, k1 = self.blocks()
            self.buffers = [s0, s1]
            self.stay = [[0, 2], [0, 1]]
            self.held = [{0: k0[0], 2: k0[1]}, {0: k1[0], 1: k1[1]}]
            return self.buffers
        if self.done == 0:
            _, q, _ = links.here()
            total = sum(self.rows)
            size = total // links.bits
            self.held = []
            both = [a.astype(f32) + b.astype(f32) for a, b in zip(self.kept, self.got)]
            both = jnp.concatenate(both, 2).astype(bf16)
            for p in range(links.bits):
                high = (p + 1) * size if p < links.bits - 1 else total
                cut = both[:, :, p * size : high]
                self.held.append(
                    {k: lax.dynamic_index_in_dim(cut, q ^ k, 1, False) for k in range(links.nq)}
                )
        self.buffers = []
        self.stay = []
        for part, pieces in enumerate(self.held):
            bit = 1 << ((part + self.done) % links.bits)
            stay = [k for k in sorted(pieces) if not k & bit]
            self.stay.append(stay)
            self.buffers.append(jnp.stack([pieces[k ^ bit] for k in stay]))
        return self.buffers

    def send(self):
        self.arrived = [
            self.links.chip(buffer, 1 << ((part + self.done) % self.links.bits))
            for part, buffer in enumerate(self.buffers)
        ]

    def absorb(self):
        last = self.done == self.links.bits - 1 and self.parts is not None
        out = []
        for pieces, got, stay in zip(self.held, self.arrived, self.stay):
            if last:
                out.append((pieces[0], got[0]))
                continue
            out.append(
                {
                    k: (pieces[k].astype(f32) + got[i].astype(f32)).astype(bf16)
                    for i, k in enumerate(stay)
                }
            )
        self.held = out
        self.done += 1

    def prepare_along(self, lines=None):
        links = self.links
        ns = links.ns
        if self.parts is not None:
            lanes = self.lanes
            total = sum(self.rows)
            more = 0 if lines is None else lines.shape[1]

            def kernel(a0, b0, a1, b1, *refs):
                outs = refs[-ns:]
                z = lax.axis_index("shard")
                for s, out in enumerate(outs):
                    at = lax.rem(z + s, ns)
                    base = 0
                    for a, b in ((a0, b0), (a1, b1)):
                        n = a.shape[1]
                        out[base : base + n, :] = (a[at].astype(f32) + b[at].astype(f32)).astype(bf16)
                        base += n
                    if more:
                        out[base : base + more, :] = refs[0][at].astype(bf16)

            pairs = [x for pair in self.held for x in pair]
            if more:
                pairs.append(lines)
            self.buffers = pl.pallas_call(
                kernel,
                in_specs=[pl.BlockSpec(memory_space=pltpu.VMEM)] * len(pairs),
                out_specs=[pl.BlockSpec(memory_space=pltpu.VMEM)] * ns,
                out_shape=[jax.ShapeDtypeStruct((total + more, lanes), bf16)] * ns,
                compiler_params=pltpu.CompilerParams(vmem_limit_bytes=32 * 1024 * 1024),
                cost_estimate=LIGHT,
                name="chip_sums",
            )(*pairs)
            return self.buffers
        z, _, _ = links.here()
        total = jnp.concatenate([p[0] for p in self.held], 1)
        self.buffers = [
            lax.dynamic_index_in_dim(total, (z + s) % ns, 0, False) for s in range(ns)
        ]
        return self.buffers

    def send_along(self):
        self.arrived = [
            self.links.along(self.buffers[s], s) for s in range(1, self.links.ns)
        ]

    def settle(self):
        final = self.buffers[0].astype(f32)
        for x in self.arrived:
            final = final + x.astype(f32)
        total = sum(self.rows)
        self.final = final[:total].astype(bf16)
        return final[total:]

    def owned(self):
        links = self.links
        _, q, c = links.here()
        rows = slice(self.base, self.base + sum(self.rows))
        mine = jnp.stack([v[rows] for v in self.mine])
        mate = jnp.stack([v[rows] for v in self.mate])
        both = jnp.stack([jnp.where(c == 0, mine, mate), jnp.where(c == 0, mate, mine)])
        ordered = [lax.dynamic_index_in_dim(both, q ^ j, 1) for j in range(links.nq)]
        full = jnp.concatenate(ordered, 1).astype(f32)
        outs = []
        base = 0
        for n in self.rows:
            outs.append(full[:, :, base : base + n])
            base += n
        return outs


class Spread:
    def __init__(self, links, scatters):
        self.links, self.scatters = links, scatters
        finals = [s.final for s in scatters]
        self.final = jnp.concatenate(finals) if len(finals) > 1 else finals[0]
        self.others = [links.chip(self.final, k) for k in range(1, links.nq)]

    def pair(self):
        mine = [self.final] + self.others
        self.mate = [self.links.core(v) for v in mine]
        base = 0
        for s in self.scatters:
            s.mine, s.mate, s.base = mine, self.mate, base
            base += sum(s.rows)


def owned_by_kernel(links, scatters, shapes, place):
    sides = scatters[0].mine + scatters[0].mate
    nq = links.nq

    def kernel(*refs):
        ins, outs = refs[: len(sides)], refs[len(sides) :]
        rep = lax.axis_index("rep")
        q, first_core = rep // 2, rep % 2 == 0
        for at, scatter in enumerate(scatters):
            for k in range(nq):
                mine, mate = ins[k], ins[nq + k]
                chip = q ^ k
                base = scatter.base
                for i, low, high in scatter.plan():
                    for lo, hi, left, right, out, factor, offset, zero, one in place(at, i):
                        a, b = max(lo, low), min(hi, high)
                        if a >= b:
                            continue
                        r = slice(base + a - low, base + b - low)
                        x, y = mine[r, left:right].astype(f32), mate[r, left:right].astype(f32)
                        row = pl.multiple_of(chip * factor + (offset + a - lo), 8)
                        rows = pl.ds(row, b - a)
                        wide = right - left
                        outs[out][rows, zero : zero + wide] = jnp.where(first_core, x, y)
                        outs[out][rows, one : one + wide] = jnp.where(first_core, y, x)
                    base += high - low

    return pl.pallas_call(
        kernel,
        in_specs=[pl.BlockSpec(memory_space=pltpu.VMEM)] * len(sides),
        out_specs=[pl.BlockSpec(memory_space=pltpu.VMEM)] * len(shapes),
        out_shape=[jax.ShapeDtypeStruct(s, f32) for s in shapes],
        compiler_params=pltpu.CompilerParams(vmem_limit_bytes=48 * 1024 * 1024),
        cost_estimate=LIGHT,
        name="owned",
    )(*sides)


def owned_feed_forward(links, scatter_1, scatter_2, w_up, w_down, w_out):
    lanes = scatter_1.lanes
    block = w_down.shape[0] // 2
    if scatter_1.parts is None or scatter_2.parts is None:
        down_first, up_first = scatter_1.owned()
        down_second, up_second, o_wout = scatter_2.owned()
        o_wdown = jnp.concatenate([side_by_side(down_first, 1), side_by_side(down_second, 1)])
        return o_wdown, up_columns(links, up_first, up_second), side_by_side(o_wout, 1)
    down_rows, up_rows = scatter_1.rows
    rq = w_up.shape[0] // links.nq
    half = block // 2

    def place(at, i):
        if i == 0:
            return [(0, down_rows, 0, lanes, 0, down_rows, at * block, 0, lanes)]
        if i == 2:
            return [(0, rq, 0, lanes, 2, rq, 0, 0, lanes)]
        out = []
        per = lanes // half
        for g in range(up_rows // rq):
            for p in range(per):
                column = (g * per + p) * 2 * block + at * block
                out.append(
                    (g * rq, (g + 1) * rq, p * half, (p + 1) * half, 1, rq, 0, column, column + half)
                )
        return out

    return owned_by_kernel(
        links, [scatter_1, scatter_2], [w_down.shape, w_up.shape, w_out.shape], place
    )


def owned_qkv(links, scatter, w_qkv):
    if scatter.parts is None:
        (grad,) = scatter.owned()
        return side_by_side(grad, 3)
    lanes = scatter.lanes
    rq = w_qkv.shape[0] // links.nq

    def place(at, i):
        return [
            (t * rq, (t + 1) * rq, 0, lanes, 0, rq, 0, 2 * t * lanes, (2 * t + 1) * lanes)
            for t in range(3)
        ]

    return owned_by_kernel(links, [scatter], [w_qkv.shape], place)[0]


def up_columns(links, first, second):
    cores, chips, _, lanes = first.shape
    both = jnp.stack([first, second])
    groups = first.shape[2] * chips * links.ns // (2 * lanes)
    rows = first.shape[2] // groups
    per = links.ns // groups
    both = both.reshape(2, cores, chips, groups, rows, per, lanes // per)
    return both.transpose(2, 4, 3, 5, 0, 1, 6).reshape(chips * rows, -1)


def side_by_side(grad, groups):
    cores, chips, rows, lanes = grad.shape
    grad = grad.reshape(cores, chips, groups, rows // groups, lanes)
    return grad.transpose(1, 3, 2, 0, 4).reshape(chips * rows // groups, groups * cores * lanes)


def total_over_rep(links, lines):
    lines = lines + links.core(lines)
    crossed = [links.chip(lines, k) for k in range(1, links.nq)]
    for x in crossed:
        lines = lines + x
    return lines


def total_over_shard(links, lines):
    z, _, _ = links.here()
    moved = [
        links.along(lax.dynamic_index_in_dim(lines, (z + s) % links.ns, 0, False), s)
        for s in range(1, links.ns)
    ]
    line = lax.dynamic_index_in_dim(lines, z, 0, False)
    for x in moved:
        line = line + x
    return line


def body(
    links,
    inputs,
    counts,
    ln1_gain,
    ln1_shift,
    w_qkv,
    qv_bias,
    w_out,
    out_bias,
    ln2_gain,
    ln2_shift,
    w_up,
    up_bias,
    w_down,
    down_bias,
    cotangent,
):
    ns = links.ns
    slots = inputs.shape[1]
    seq_len = inputs.shape[2]
    width = inputs.shape[3]
    n_rows = slots * seq_len
    z = lax.axis_index("shard")

    small = (ln1_gain, ln1_shift, out_bias, ln2_gain, ln2_shift, down_bias, qv_bias, up_bias)
    sizes = [v.shape[0] for v in small]
    line = w_qkv.shape[1] // 2
    n_lines = -(-sum(sizes) // line)

    gather_a, gather_b, gather_c = (
        Gather(links, [w_qkv]),
        Gather(links, [w_out, w_up]),
        Gather(links, [w_down]),
    )
    n = w_qkv.shape[0] // links.nq
    packed_a = pack(links, w_qkv, small, line)
    got = gather_along(links, packed_a)
    got_small = [g[n : n + n_lines] for g in got]
    own_a = gather_a.start(jnp.stack([g[:n] for g in got]))
    got_b = gather_along(links, tie(piece_of(links, [w_out, w_up]), own_a))
    while gather_a.done < links.bits:
        gather_a.send()
        gather_a.absorb()
    gather_a.mine, got_b = meet(gather_a.mine, got_b)
    (full_qkv,) = gather_a.full()
    got_c = gather_along(links, tie(piece_of(links, [w_down]), got_b))
    gather_b.start(jnp.stack(got_b))
    gather_b.send()
    all_small = jnp.stack([packed_a[n : n + n_lines]] + got_small).reshape(ns, -1)
    all_small = jnp.concatenate(
        [lax.dynamic_index_in_dim(all_small, (z - j) % ns, 0) for j in range(ns)]
    )
    full_small = []
    base = 0
    for n in sizes:
        full_small.append(all_small[:, base : base + n].reshape(-1).astype(f32))
        base += n
    full_g1, full_s1, full_bout, full_g2, full_s2, full_bdown, bias_f, full_bup = full_small
    first_slot = z * slots
    alive = (jnp.arange(slots, dtype=jnp.int32) + first_slot < counts[0]).astype(f32)
    assert slots == 1
    d_out_b = jnp.where(alive[0] > 0, cotangent, jnp.zeros_like(cotangent)).reshape(n_rows, width)
    tokens_b = inputs.reshape(n_rows, width)
    hidden_one_b = layer_norm(tokens_b.astype(f32), full_g1, full_s1).astype(bf16)
    projected = matmul(hidden_one_b, full_qkv)
    none = jnp.zeros((width,), f32)
    qkv_bias = jnp.concatenate([bias_f[:width], none, bias_f[width:]])
    qkv_b = (projected + qkv_bias).astype(bf16)
    pairs = width // (2 * HDIM)
    cuts = (0, pairs * 3 // 8, pairs * 5 // 8, pairs)
    qkv_b, gather_b.arrived = meet(qkv_b, gather_b.arrived)
    gather_b.absorb()
    while gather_b.done < links.bits - 1:
        gather_b.send()
        gather_b.absorb()
    gather_b.send()
    kept = attend(qkv_b, cuts[0], cuts[1])
    kept, gather_b.arrived, got_c = meet(kept, gather_b.arrived, got_c)
    gather_b.absorb()
    gather_c.start(jnp.stack(got_c))
    gather_c.send()
    kept = attend(qkv_b, cuts[1], cuts[2], kept)
    kept, gather_c.arrived = meet(kept, gather_c.arrived)
    gather_c.absorb()
    while gather_c.done < links.bits - 1:
        gather_c.send()
        gather_c.absorb()
    gather_c.send()
    kept = attend(qkv_b, cuts[2], cuts[3], kept)
    kept, gather_c.arrived = meet(kept, gather_c.arrived)
    gather_c.absorb()
    attended_b, inverse, probs_b = kept
    full_wout, full_wup = gather_b.full()
    gain_two = full_g2[None]
    middle, hidden_two_b = middle_of(
        tokens_b, attended_b, full_wout, full_bout[None], gain_two, full_s2[None]
    )
    middle, gather_c.mate = meet(middle, gather_c.mate)
    (full_wdown,) = gather_c.full()
    bias_up = full_bup[None]
    last_bias = full_bdown[None]
    y, g, away, home, gb_first = feed_forward(
        links, hidden_two_b, d_out_b, full_wup, bias_up, full_wdown, alive, last_bias, middle, None, 0
    )
    scatter_1 = Scatter(links, away, home)
    output, g, away, home, gb_second = feed_forward(
        links, hidden_two_b, d_out_b, full_wup, bias_up, full_wdown, alive, last_bias, y, g, 1
    )
    output = output.reshape(inputs.shape)
    grad_bup = jnp.concatenate([gb_first, gb_second], 1)
    g, scatter_1.kept = meet(g, scatter_1.kept)
    g, scatter_1.buffers = meet(g, scatter_1.prepare())
    scatter_1.send()
    d_mid, d_att_b, out_away, out_home, sums = middle_back(
        links, g, middle, d_out_b, attended_b, full_wout, gain_two
    )
    grad_g2, grad_s2, grad_bout, grad_bdown = (sums[i] for i in range(4))
    scatter_2 = Scatter(links, away + [out_away], home + [out_home])
    d_att_b, scatter_1.arrived = meet(d_att_b, scatter_1.arrived)
    scatter_1.absorb()
    d_att_b, scatter_1.buffers, scatter_2.buffers = meet(
        d_att_b, scatter_1.prepare(), scatter_2.prepare()
    )
    scatter_1.send()
    scatter_2.send()
    half = pairs * 5 // 8
    grads = attend_back(qkv_b, d_att_b, attended_b, inverse, probs_b, 0, half)
    for _ in range(links.bits - 2):
        scatter_1.absorb()
        scatter_1.prepare()
        scatter_1.send()
        scatter_2.absorb()
        scatter_2.prepare()
        scatter_2.send()
    grads, scatter_1.arrived, scatter_2.arrived = meet(
        grads, scatter_1.arrived, scatter_2.arrived
    )
    scatter_1.absorb()
    scatter_2.absorb()
    grads, scatter_1.buffers, scatter_2.buffers = meet(
        grads, scatter_1.prepare_along(), scatter_2.prepare()
    )
    scatter_1.send_along()
    scatter_2.send()
    grads = attend_back(qkv_b, d_att_b, attended_b, inverse, probs_b, half, pairs, grads)
    grads, scatter_1.arrived, scatter_2.arrived = meet(
        grads, scatter_1.arrived, scatter_2.arrived
    )
    scatter_1.settle()
    scatter_2.absorb()
    grads, scatter_1.final, scatter_2.buffers = meet(
        grads, scatter_1.final, scatter_2.prepare_along()
    )
    scatter_2.send_along()
    d_qkv, qv_sums = grads
    scatter_3 = Scatter(links, *weight_grads(links, hidden_one_b, d_qkv))
    d_qkv, scatter_3.buffers = meet(d_qkv, scatter_3.prepare())
    scatter_3.send()
    input_grad, entry_sums = entry_back(d_qkv, full_qkv, tokens_b, d_mid, full_g1[None])
    for _ in range(links.bits - 2):
        scatter_3.absorb()
        scatter_3.prepare()
        scatter_3.send()
    input_grad, entry_sums, scatter_3.arrived, scatter_2.arrived = meet(
        input_grad, entry_sums, scatter_3.arrived, scatter_2.arrived
    )
    scatter_3.absorb()
    scatter_3.prepare()
    scatter_3.send()
    scatter_2.settle()
    input_grad = input_grad.reshape(inputs.shape)
    grad_g1, grad_s1 = entry_sums[0], entry_sums[1]
    grad_qvb = qv_sums.reshape(-1)
    small_grads = (grad_g1, grad_s1, grad_bout, grad_g2, grad_s2, grad_bdown, grad_qvb, grad_bup)
    joined = jnp.concatenate([g.reshape(ns, -1) for g in small_grads], 1)
    joined = total_over_rep(links, joined)
    scatter_3.arrived, scatter_1.final, scatter_2.final = meet(
        scatter_3.arrived, scatter_1.final, scatter_2.final
    )
    scatter_3.absorb()
    n_small = joined.shape[1]
    ride = scatter_3.parts is not None and n_small % scatter_3.lanes == 0
    if ride:
        lines = joined.reshape(ns, -1, scatter_3.lanes)
        lines = jnp.pad(lines, ((0, 0), (0, -lines.shape[1] % 16), (0, 0)))
        scatter_3.buffers = scatter_3.prepare_along(lines)
    else:
        scatter_3.prepare_along()
        joined = total_over_shard(links, joined)
    scatter_3.send_along()
    spread_12 = Spread(links, [scatter_1, scatter_2])
    scatter_3.arrived, spread_12.others = meet(scatter_3.arrived, spread_12.others)
    spread_12.pair()
    arrived_lines = scatter_3.settle()
    spread_3 = Spread(links, [scatter_3])
    if ride:
        joined = arrived_lines.reshape(-1)[:n_small]
    o_wdown, o_wup, o_wout = owned_feed_forward(links, scatter_1, scatter_2, w_up, w_down, w_out)
    spread_3.pair()
    o_qkv = owned_qkv(links, scatter_3, w_qkv)
    owned = []
    base = 0
    for n in sizes:
        owned.append(joined[base : base + n])
        base += n
    o_g1, o_s1, o_bout, o_g2, o_s2, o_bdown, o_qvb, o_bup = owned
    return (
        output,
        input_grad,
        o_g1,
        o_s1,
        o_qkv,
        o_qvb,
        o_wout,
        o_bout,
        o_g2,
        o_s2,
        o_wup,
        o_bup,
        o_wdown,
        o_bdown,
    )


def solution(mesh):
    tokens = P("rep", "shard", None, None)
    vector = P("shard")
    matrix = P("shard", None)
    return jax.shard_map(
        functools.partial(body, Links(mesh)),
        mesh=mesh,
        in_specs=(
            tokens,
            P("rep"),
            vector,
            vector,
            matrix,
            vector,
            matrix,
            vector,
            vector,
            vector,
            matrix,
            vector,
            matrix,
            vector,
            tokens,
        ),
        out_specs=(
            tokens,
            tokens,
            vector,
            vector,
            matrix,
            vector,
            matrix,
            vector,
            vector,
            vector,
            matrix,
            vector,
            matrix,
            vector,
        ),
        check_vma=False,
    )
```

```python
import functools

import jax
import jax.numpy as jnp
from jax import lax
from jax.experimental import pallas as pl
from jax.experimental.pallas import tpu as pltpu
from jax.sharding import PartitionSpec as P

HDIM = 64

eps = 1e-06
bf16 = jnp.bfloat16
LIGHT = pl.CostEstimate(flops=1, transcendentals=0, bytes_accessed=1)
HEAVY = pl.CostEstimate(flops=20_000_000_000, transcendentals=0, bytes_accessed=10_000_000)
f32 = jnp.float32


def layer_norm(values, gain, shift):
    centre = values - jnp.mean(values, -1, keepdims=True)
    spread = jnp.mean(centre * centre, -1, keepdims=True)
    return centre * lax.rsqrt(spread + eps) * gain + shift


def matmul(left, right):
    return jnp.dot(left, right, preferred_element_type=f32)


LOG2E = 1.4426950408889634


def contract(left, right, left_dim, right_dim):
    return lax.dot_general(
        left, right, (((left_dim,), (right_dim,)), ((), ())), preferred_element_type=f32
    )


def query_blocks(rows, tile=256):
    return [(i, min(tile, rows - i)) for i in range(0, rows, tile)]


def head_mask(head, rows, dtype):
    lane = lax.broadcasted_iota(jnp.int32, (rows, 2 * HDIM), 1)
    return (lane // HDIM == head).astype(dtype)


def attend_kernel(q_ref, k_ref, v_ref, o_ref, inv_ref, p_ref):
    rows = q_ref.shape[0]
    factor = HDIM ** (-0.5) * LOG2E
    keys = k_ref[...]
    values = v_ref[...]
    ones = jnp.ones(values.shape, bf16)
    for start, n in query_blocks(rows):
        queries = q_ref[start : start + n, :]
        mixed = inverse = None
        for head in range(2):
            mask = head_mask(head, rows, bf16)
            scores = contract(keys * mask, queries, 1, 1)
            largest = jnp.max(scores, axis=0, keepdims=True)
            probs = jnp.exp2((scores - largest) * factor).astype(bf16)
            p_ref[head, :, start : start + n] = probs
            both = contract(probs, jnp.concatenate([values * mask, ones], 1), 0, 0)
            inv = 1.0 / both[:, 2 * HDIM :]
            part = both[:, : 2 * HDIM] * inv
            share = head_mask(head, n, f32) * inv
            mixed = part if mixed is None else mixed + part
            inverse = share if inverse is None else inverse + share
        o_ref[start : start + n, :] = mixed.astype(bf16)
        inv_ref[start : start + n, :] = inverse


def whole(count):
    return [pl.BlockSpec(memory_space=pl.ANY)] * count


def attend(qkv, first, last, before=None):
    rows, wide = qkv.shape
    width = wide // 3
    pairs = width // (2 * HDIM)
    count = last - first

    def column(offset):
        return pl.BlockSpec((rows, 2 * HDIM), lambda j: (0, offset + first + j))

    def kernel(*refs):
        attend_kernel(*refs[:3], *refs[-3:])

    given = () if before is None else tuple(before)
    return pl.pallas_call(
        kernel,
        grid=(count,),
        in_specs=[column(0), column(pairs), column(2 * pairs)] + whole(len(given)),
        out_specs=[
            column(0),
            column(0),
            pl.BlockSpec((2, rows, rows), lambda j: (first + j, 0, 0)),
        ],
        out_shape=[
            jax.ShapeDtypeStruct((rows, width), bf16),
            jax.ShapeDtypeStruct((rows, width), f32),
            jax.ShapeDtypeStruct((2 * pairs, rows, rows), bf16),
        ],
        input_output_aliases={3 + i: i for i in range(len(given))},
        compiler_params=pltpu.CompilerParams(vmem_limit_bytes=56 * 1024 * 1024),
        cost_estimate=HEAVY,
        name="attend",
    )(qkv, qkv, qkv, *given)


def attend_back_kernel(
    q_ref, k_ref, v_ref, d_ref, o_ref, inv_ref, p_ref, out_ref, sum_ref
):
    rows = q_ref.shape[0]
    scale = HDIM ** (-0.5)
    queries = q_ref[...]
    keys = k_ref[...]
    values = v_ref[...]
    grads = (d_ref[...].astype(f32) * inv_ref[...]).astype(bf16)
    product = grads.astype(f32) * o_ref[...].astype(f32)
    lane = lax.broadcasted_iota(jnp.int32, (rows, 2 * HDIM), 1)
    blocks = query_blocks(rows)
    d_queries = [None] * len(blocks)
    d_keys = d_values = None
    for head in range(2):
        mask = head_mask(head, rows, bf16)
        inner = -jnp.sum(jnp.where(lane // HDIM == head, product, 0.0), 1, keepdims=True)
        high = inner.astype(bf16)
        low = (inner - high.astype(f32)).astype(bf16)
        tail = jnp.where(lane == 0, high, jnp.where(lane == 1, low, jnp.zeros_like(low)))
        grads_wide = jnp.concatenate([grads, tail], 1)
        values_wide = jnp.concatenate([values * mask, (lane < 2).astype(bf16)], 1)
        keys_h, queries_h, grads_h = keys * mask, queries * mask, grads * mask
        for b, (start, n) in enumerate(blocks):
            d_probs = contract(values_wide, grads_wide[start : start + n, :], 1, 1)
            probs = p_ref[head, :, start : start + n]
            d_scores = probs * d_probs.astype(bf16)
            to_values = contract(probs, grads_h[start : start + n, :], 1, 0)
            to_keys = contract(d_scores, queries_h[start : start + n, :], 1, 0)
            to_queries = contract(d_scores, keys_h, 0, 0)
            d_values = to_values if d_values is None else d_values + to_values
            d_keys = to_keys if d_keys is None else d_keys + to_keys
            d_queries[b] = to_queries if d_queries[b] is None else d_queries[b] + to_queries
    d_values = d_values.astype(bf16)
    out_ref[1] = (d_keys * scale).astype(bf16)
    out_ref[2] = d_values
    sums = jnp.zeros((1, 2 * HDIM), f32)
    for b, (start, n) in enumerate(blocks):
        block = (d_queries[b] * scale).astype(bf16)
        out_ref[0, start : start + n, :] = block
        sums = sums + jnp.sum(block.astype(f32), 0, keepdims=True)
    sum_ref[0] = sums
    sum_ref[1] = jnp.sum(d_values.astype(f32), 0, keepdims=True)


def attend_back(qkv, grad, attended, inverse, probs, first, last, before=None):
    rows, wide = qkv.shape
    width = wide // 3
    pairs = width // (2 * HDIM)
    count = last - first

    def column(offset):
        return pl.BlockSpec((rows, 2 * HDIM), lambda j: (0, offset + first + j))

    def kernel(*refs):
        attend_back_kernel(*refs[:7], *refs[-2:])

    given = () if before is None else tuple(before)
    return pl.pallas_call(
        kernel,
        grid=(count,),
        in_specs=[column(0), column(pairs), column(2 * pairs)]
        + [column(0)] * 3
        + [pl.BlockSpec((2, rows, rows), lambda j: (first + j, 0, 0))]
        + whole(len(given)),
        out_specs=[
            pl.BlockSpec((3, rows, 2 * HDIM), lambda j: (0, 0, first + j)),
            pl.BlockSpec((2, 1, 2 * HDIM), lambda j: (0, 0, first + j)),
        ],
        out_shape=[
            jax.ShapeDtypeStruct((3, rows, width), bf16),
            jax.ShapeDtypeStruct((2, 1, width), f32),
        ],
        input_output_aliases={7 + i: i for i in range(len(given))},
        compiler_params=pltpu.CompilerParams(vmem_limit_bytes=56 * 1024 * 1024),
        cost_estimate=LIGHT if first == 0 else HEAVY,
        name="attend_back",
    )(qkv, qkv, qkv, grad, attended, inverse, probs, *given)


def gelu_pair(values):
    bell = jnp.exp2(values * values * (-0.5 * LOG2E))
    t = 1.0 / (1.0 + 0.23164189 * jnp.abs(values))
    poly = 0.5307027145 * t - 0.7265760135
    poly = poly * t + 0.7107068705
    poly = poly * t - 0.142248368
    poly = poly * t + 0.127414796
    tail = poly * t * bell
    area = jnp.where(values >= 0, 1.0 - tail, tail)
    return values * area, area + values * bell * 0.3989422804014327


def feed_forward_kernel(
    h_ref, dm_ref, up_ref, bias_ref, down_ref, alive_ref, last_ref, y0_ref, g0_ref,
    y_ref, g_ref, down_away, down_home, up_away, up_home, gb_ref,
    act_ref, dp_ref, y_acc, g_acc, out_ref, sems,
):
    j = pl.program_id(0)
    final = g0_ref is not None
    given = [pltpu.make_async_copy(y0_ref, y_acc, sems.at[0])]
    if final:
        given.append(pltpu.make_async_copy(g0_ref, g_acc, sems.at[1]))
    made = [
        pltpu.make_async_copy(out_ref if final else y_acc, y_ref, sems.at[2]),
        pltpu.make_async_copy(g_acc, g_ref, sems.at[3]),
    ]

    @pl.when(j == 0)
    def _():
        for copy in given:
            copy.start()
        if not final:
            g_acc[...] = jnp.zeros_like(g_acc)

    rows = h_ref.shape[0]
    up, down = up_ref[...], down_ref[...]
    bias = bias_ref[...]
    chunk = 368
    for start in range(0, rows, chunk):
        r = slice(start, min(start + chunk, rows))
        act, slope = gelu_pair(contract(h_ref[r, :], up, 1, 0) + bias)
        act = act.astype(bf16)
        act_ref[r, :] = act
        d_pre = (contract(dm_ref[r, :], down, 1, 1) * slope).astype(bf16)
        dp_ref[r, :] = d_pre
        if start == 0:

            @pl.when(j == 0)
            def _():
                for copy in given:
                    copy.wait()

        y_acc[r, :] += contract(act, down, 1, 0)
        g_acc[r, :] += contract(d_pre, up, 1, 1)

    @pl.when(j == pl.num_programs(0) - 1)
    def _():
        if final:
            out_ref[...] = (alive_ref[0] * (y_acc[...] + last_ref[...])).astype(bf16)
        for copy in made:
            copy.start()

    gb_ref[...] = jnp.sum(dp_ref[...].astype(f32), 0, keepdims=True)[None]
    first_core = lax.axis_index("rep") % 2 == 0
    for left, right, away, home in (
        (act_ref, dm_ref, down_away, down_home),
        (h_ref, dp_ref, up_away, up_home),
    ):
        grad = contract(left[...], right[...], 0, 0)
        half = grad.shape[1] // 2
        low, high = grad[:, :half], grad[:, half:]
        away[...] = jnp.where(first_core, high, low).reshape(away.shape).astype(bf16)
        home[...] = jnp.where(first_core, low, high).reshape(home.shape).astype(bf16)

    @pl.when(j == pl.num_programs(0) - 1)
    def _():
        for copy in made:
            copy.wait()


def feed_forward(links, hidden, d_out, up, bias, down, alive, last_bias, y0, g0, part):
    ns, nq = links.ns, links.nq
    rows, width = hidden.shape
    block = up.shape[1] // (2 * ns)
    rq = width // (ns * nq)
    per = width // block
    wide = dict(pipeline_mode=pl.Buffered(1))

    def full():
        return pl.BlockSpec((rows, width), lambda j: (0, 0), **wide)

    def kernel(*refs):
        refs = list(refs)
        if g0 is None:
            refs.insert(8, None)
        feed_forward_kernel(*refs)

    down_spec = pl.BlockSpec((1, block, width // 2), lambda j: (j, 0, 0))
    up_spec = pl.BlockSpec((ns, nq, 1, rq, block // 2), lambda j: (0, 0, j // per, 0, j % per))
    down_shape = jax.ShapeDtypeStruct((ns, block, width // 2), bf16)
    up_shape = jax.ShapeDtypeStruct((ns, nq, ns // per, rq, width // 2), bf16)
    sums = jax.ShapeDtypeStruct((rows, width), f32)
    given = (y0,) if g0 is None else (y0, g0)
    y, g, d_away, d_home, u_away, u_home, gb = pl.pallas_call(
        kernel,
        grid=(ns,),
        in_specs=[
            full(),
            full(),
            pl.BlockSpec((width, block), lambda j: (0, 2 * j + part)),
            pl.BlockSpec((1, block), lambda j: (0, 2 * j + part)),
            pl.BlockSpec((block, width), lambda j: (2 * j + part, 0)),
            pl.BlockSpec(memory_space=pltpu.SMEM),
            pl.BlockSpec((1, width), lambda j: (0, 0)),
        ]
        + whole(len(given)),
        out_specs=whole(2)
        + [
            down_spec,
            down_spec,
            up_spec,
            up_spec,
            pl.BlockSpec((1, 1, block), lambda j: (j, 0, 0)),
        ],
        out_shape=[
            sums if g0 is None else jax.ShapeDtypeStruct((rows, width), bf16),
            sums,
            down_shape,
            down_shape,
            up_shape,
            up_shape,
            jax.ShapeDtypeStruct((ns, 1, block), f32),
        ],
        scratch_shapes=[
            pltpu.VMEM((rows, block), bf16),
            pltpu.VMEM((rows, block), bf16),
            pltpu.VMEM((rows, width), f32),
            pltpu.VMEM((rows, width), f32),
            pltpu.VMEM((rows, width), bf16),
            pltpu.SemaphoreType.DMA((4,)),
        ],
        compiler_params=pltpu.CompilerParams(vmem_limit_bytes=50 * 1024 * 1024),
        cost_estimate=HEAVY,
        name="feed_forward",
    )(hidden, d_out, up, bias, down, alive, last_bias, *given)

    def pieces(down_grad, up_grad):
        lanes = width // 2
        return [
            down_grad.reshape(ns, nq, block // nq, lanes),
            up_grad.reshape(ns, nq, ns // per * rq, lanes),
        ]

    return y, g, pieces(d_away, u_away), pieces(d_home, u_home), gb.reshape(ns, block)


def grad_kernel(left_ref, right_ref, away_ref, home_ref):
    grad = contract(left_ref[...], right_ref[0], 0, 0)
    half = grad.shape[1] // 2
    low, high = grad[:, :half], grad[:, half:]
    first_core = lax.axis_index("rep") % 2 == 0
    away_ref[...] = jnp.where(first_core, high, low).reshape(away_ref.shape).astype(bf16)
    home_ref[...] = jnp.where(first_core, low, high).reshape(home_ref.shape).astype(bf16)


def weight_grads(links, left, rights):
    ns, nq = links.ns, links.nq
    rows, width = left.shape
    count, _, wide = rights.shape
    rq = width // (ns * nq)
    spec = pl.BlockSpec((ns, nq, 1, rq, wide // 2), lambda i: (0, 0, i, 0, 0))
    shape = jax.ShapeDtypeStruct((ns, nq, count, rq, wide // 2), bf16)
    away, home = pl.pallas_call(
        grad_kernel,
        grid=(count,),
        in_specs=[
            pl.BlockSpec((rows, width), lambda i: (0, 0)),
            pl.BlockSpec((1, rows, wide), lambda i: (i, 0, 0)),
        ],
        out_specs=[spec, spec],
        out_shape=[shape, shape],
        compiler_params=pltpu.CompilerParams(vmem_limit_bytes=48 * 1024 * 1024),
        cost_estimate=HEAVY,
        name="weight_grads",
    )(left, rights)
    flat = (ns, nq, count * rq, wide // 2)
    return [away.reshape(flat)], [home.reshape(flat)]


def row_block(rows):
    return 368 if rows % 368 == 0 else rows


def normal(values):
    centre = values - jnp.mean(values, -1, keepdims=True)
    scale = lax.rsqrt(jnp.mean(centre * centre, -1, keepdims=True) + eps)
    return centre * scale, scale


def normal_back(unit, scale, grad):
    inner = jnp.mean(grad * unit, -1, keepdims=True)
    return scale * (grad - jnp.mean(grad, -1, keepdims=True) - unit * inner)


def column_sum(values):
    return jnp.sum(values, 0, keepdims=True)


def middle_kernel(x_ref, att_ref, w_ref, bias_ref, gain_ref, shift_ref, mid_ref, h_ref):
    mid = x_ref[...].astype(f32) + contract(att_ref[...], w_ref[...], 1, 0) + bias_ref[...]
    mid_ref[...] = mid
    unit, _ = normal(mid)
    h_ref[...] = (unit * gain_ref[...] + shift_ref[...]).astype(bf16)


def middle_of(tokens, attended, weight, bias, gain, shift):
    rows, width = tokens.shape
    n = row_block(rows)
    block = pl.BlockSpec((n, width), lambda i: (i, 0))
    line = pl.BlockSpec((1, width), lambda i: (0, 0))
    return pl.pallas_call(
        middle_kernel,
        grid=(rows // n,),
        in_specs=[block, block, pl.BlockSpec(weight.shape, lambda i: (0, 0)), line, line, line],
        out_specs=[block, block],
        out_shape=[
            jax.ShapeDtypeStruct((rows, width), f32),
            jax.ShapeDtypeStruct((rows, width), bf16),
        ],
        compiler_params=pltpu.CompilerParams(vmem_limit_bytes=48 * 1024 * 1024),
        cost_estimate=HEAVY,
        name="middle",
    )(tokens, attended, weight, bias, gain, shift)


def middle_back_kernel(
    g_ref, mid_ref, dm_ref, att_ref, w_ref, gain_ref,
    d_mid_ref, d_att_ref, away_ref, home_ref, sum_ref, acc_ref,
):
    i = pl.program_id(0)

    @pl.when(i == 0)
    def _():
        acc_ref[...] = jnp.zeros_like(acc_ref)
        sum_ref[...] = jnp.zeros_like(sum_ref)

    unit, scale = normal(mid_ref[...])
    g = g_ref[...]
    d_out = dm_ref[...].astype(f32)
    d_mid = d_out + normal_back(unit, scale, g * gain_ref[...])
    d_mid_ref[...] = d_mid
    d_proj = d_mid.astype(bf16)
    d_att_ref[...] = contract(d_proj, w_ref[...], 1, 1).astype(bf16)
    acc_ref[...] += contract(att_ref[...], d_proj, 0, 0)
    sum_ref[0:1, :] += column_sum(g * unit)
    sum_ref[1:2, :] += column_sum(g)
    sum_ref[2:3, :] += column_sum(d_proj.astype(f32))
    sum_ref[3:4, :] += column_sum(d_out)

    @pl.when(i == pl.num_programs(0) - 1)
    def _():
        grad = acc_ref[...]
        half = grad.shape[1] // 2
        low, high = grad[:, :half], grad[:, half:]
        first_core = lax.axis_index("rep") % 2 == 0
        away_ref[...] = jnp.where(first_core, high, low).reshape(away_ref.shape).astype(bf16)
        home_ref[...] = jnp.where(first_core, low, high).reshape(home_ref.shape).astype(bf16)


def middle_back(links, grad, middle, d_out, attended, weight, gain):
    ns, nq = links.ns, links.nq
    rows, width = middle.shape
    n = row_block(rows)
    block = pl.BlockSpec((n, width), lambda i: (i, 0))
    pieces = (ns, nq, width // (ns * nq), width // 2)
    whole_piece = pl.BlockSpec(pieces, lambda i: (0, 0, 0, 0))
    return pl.pallas_call(
        middle_back_kernel,
        grid=(rows // n,),
        in_specs=[block] * 4
        + [
            pl.BlockSpec(weight.shape, lambda i: (0, 0)),
            pl.BlockSpec((1, width), lambda i: (0, 0)),
        ],
        out_specs=[
            block,
            block,
            whole_piece,
            whole_piece,
            pl.BlockSpec((8, width), lambda i: (0, 0)),
        ],
        out_shape=[
            jax.ShapeDtypeStruct((rows, width), f32),
            jax.ShapeDtypeStruct((rows, width), bf16),
            jax.ShapeDtypeStruct(pieces, bf16),
            jax.ShapeDtypeStruct(pieces, bf16),
            jax.ShapeDtypeStruct((8, width), f32),
        ],
        scratch_shapes=[pltpu.VMEM((width, width), f32)],
        compiler_params=pltpu.CompilerParams(vmem_limit_bytes=48 * 1024 * 1024),
        cost_estimate=HEAVY,
        name="middle_back",
    )(grad, middle, d_out, attended, weight, gain)


def entry_back_kernel(d_ref, w_ref, x_ref, d_mid_ref, gain_ref, out_ref, sum_ref):
    @pl.when(pl.program_id(0) == 0)
    def _():
        sum_ref[...] = jnp.zeros_like(sum_ref)

    width = x_ref.shape[1]
    g = contract(d_ref[0], w_ref[:, :width], 1, 1)
    for t in range(1, 3):
        g = g + contract(d_ref[t], w_ref[:, t * width : (t + 1) * width], 1, 1)
    unit, scale = normal(x_ref[...].astype(f32))
    out_ref[...] = d_mid_ref[...] + normal_back(unit, scale, g * gain_ref[...])
    sum_ref[0:1, :] += column_sum(g * unit)
    sum_ref[1:2, :] += column_sum(g)


def entry_back(grads, weight, tokens, d_mid, gain):
    rows, width = tokens.shape
    n = row_block(rows)
    block = pl.BlockSpec((n, width), lambda i: (i, 0))
    return pl.pallas_call(
        entry_back_kernel,
        grid=(rows // n,),
        in_specs=[
            pl.BlockSpec((3, n, width), lambda i: (0, i, 0)),
            pl.BlockSpec(weight.shape, lambda i: (0, 0), pipeline_mode=pl.Buffered(1)),
            block,
            block,
            pl.BlockSpec((1, width), lambda i: (0, 0)),
        ],
        out_specs=[block, pl.BlockSpec((8, width), lambda i: (0, 0))],
        out_shape=[
            jax.ShapeDtypeStruct((rows, width), f32),
            jax.ShapeDtypeStruct((8, width), f32),
        ],
        compiler_params=pltpu.CompilerParams(vmem_limit_bytes=48 * 1024 * 1024),
        cost_estimate=pl.CostEstimate(flops=6_000_000_000, transcendentals=0, bytes_accessed=1),
        name="entry_back",
    )(grads, weight, tokens, d_mid, gain)


class Links:
    def __init__(self, mesh):
        self.ns = mesh.shape["shard"]
        self.nr = mesh.shape["rep"]
        self.nq = self.nr // 2
        self.bits = self.nq.bit_length() - 1
        assert 1 << self.bits == self.nq

    def here(self):
        rep = lax.axis_index("rep")
        return lax.axis_index("shard"), rep // 2, rep % 2

    def along(self, values, step):
        return lax.ppermute(values, "shard", [(i, (i + step) % self.ns) for i in range(self.ns)])

    def chip(self, values, k):
        return lax.ppermute(values, "rep", [(i, i ^ (2 * k)) for i in range(self.nr)])

    def core(self, values):
        return lax.ppermute(values, "rep", [(i, i ^ 1) for i in range(self.nr)])


def meet(*values):
    return lax.optimization_barrier(values)


def tie(values, others):
    return lax.optimization_barrier((values, others))[0]


def piece_of(links, weights):
    _, q, c = links.here()
    parts = []
    for w in weights:
        rq, half = w.shape[0] // links.nq, w.shape[1] // 2
        parts.append(lax.dynamic_slice(w, (q * rq, c * half), (rq, half)))
    return jnp.concatenate(parts, 1)


def pack(links, weight, small, line):
    rq = weight.shape[0] // links.nq
    total = sum(v.shape[0] for v in small)
    fits = all(sum(v.shape[0] for v in part) == line for part in (small[:6], small[6:]))
    if rq % 16 or line % 128 or not fits:
        filled = jnp.concatenate(small + (jnp.zeros((-total % line,), bf16),)).reshape(-1, line)
        filler = jnp.zeros((16 - filled.shape[0], line), bf16)
        return jnp.concatenate([piece_of(links, [weight]), filled, filler])

    def kernel(w_ref, *refs):
        *vectors, out_ref, sem = refs
        rep = lax.axis_index("rep")
        q, c = rep // 2, rep % 2
        rows = pl.ds(pl.multiple_of(q * rq, rq), rq)
        copy = pltpu.make_async_copy(
            w_ref.at[rows, pl.ds(pl.multiple_of(c * line, line), line)], out_ref.at[:rq], sem
        )
        copy.start()
        lines = [[], []]
        for at, ref in enumerate(vectors):
            lines[at // 6].append(ref[...].astype(f32).reshape(1, -1))
        block = [jnp.concatenate(x, 1) for x in lines]
        row = lax.broadcasted_iota(jnp.int32, (16, line), 0)
        filled = jnp.where(row == 0, block[0], jnp.where(row == 1, block[1], 0.0))
        out_ref[rq:, :] = filled.astype(bf16)
        copy.wait()

    return pl.pallas_call(
        kernel,
        in_specs=whole(1) + [pl.BlockSpec(memory_space=pltpu.VMEM)] * len(small),
        out_specs=pl.BlockSpec(memory_space=pltpu.VMEM),
        out_shape=jax.ShapeDtypeStruct((rq + 16, line), bf16),
        scratch_shapes=[pltpu.SemaphoreType.DMA(())],
        cost_estimate=LIGHT,
        name="pack",
    )(weight, *small)


def gather_along(links, piece):
    return [links.along(piece, s) for s in range(1, links.ns)]


def lanes_of(links, values, part):
    n = values.shape[-1] // links.bits
    return values[..., part * n : (part + 1) * n]


def assemble(links, weights, got_mine, got_mate):
    ns, nq, bits = links.ns, links.nq, links.bits
    rows = [w.shape[0] for w in weights]
    cols = [w.shape[1] for w in weights]
    rq = [r // nq for r in rows]
    total = sum(cols) // 2
    lanes = total // bits
    n = len(weights)
    per_side = len(got_mine)

    def kernel(*refs):
        w_refs = refs[:n]
        sides = (refs[n : n + per_side], refs[n + per_side : n + 2 * per_side])
        out_refs = refs[n + 2 * per_side : n + 2 * per_side + n]
        sem = refs[-1]
        z = lax.axis_index("shard")
        rep = lax.axis_index("rep")
        q, c = rep // 2, rep % 2
        copies = []

        def go(src, dst):
            copy = pltpu.make_async_copy(src, dst, sem.at[len(copies)])
            copy.start()
            copies.append(copy)

        for i in range(n):
            go(w_refs[i], out_refs[i].at[pl.ds(pl.multiple_of(z * rows[i], rows[i]), rows[i]), :])
        for side, parts in enumerate(sides):
            core = c if side == 0 else 1 - c
            base = 0
            for i in range(n):
                half = cols[i] // 2

                def place(source, k, s, low, high):
                    zs = lax.rem(z + (ns - s), ns)
                    at = pl.ds(pl.multiple_of(zs * rows[i] + (q ^ k) * rq[i], rq[i]), rq[i])
                    to = pl.ds(pl.multiple_of(core * half + (low - base), 128), high - low)
                    go(source, out_refs[i].at[at, to])

                for s in range(1, ns):
                    own = parts[0].at[s - 1, :, pl.ds(base, half)]
                    place(own, 0, s, base, base + half)
                    at = 1
                    for step in range(bits):
                        for part in range(bits):
                            known = [0]
                            for t in range(step):
                                bit = 1 << ((part + t) % bits)
                                known = known + [k ^ bit for k in known]
                            known = sorted(known)
                            bit = 1 << ((part + step) % bits)
                            low = max(base, part * lanes)
                            high = min(base + half, (part + 1) * lanes)
                            if low < high:
                                cut = pl.ds(low - part * lanes, high - low)
                                for j, k in enumerate(known):
                                    source = parts[at].at[j, s - 1, :, cut]
                                    place(source, k ^ bit, s, low, high)
                            at += 1
                base += half
        for copy in copies:
            copy.wait()

    pieces = 0
    base = 0
    for i in range(n):
        half = cols[i] // 2
        for part in range(bits):
            if max(base, part * lanes) < min(base + half, (part + 1) * lanes):
                pieces += nq - 1
        pieces += 1
        base += half
    count = n + 2 * (ns - 1) * pieces
    return pl.pallas_call(
        kernel,
        out_shape=[jax.ShapeDtypeStruct((ns * r, c), bf16) for r, c in zip(rows, cols)],
        in_specs=whole(n + 2 * per_side),
        out_specs=[pl.BlockSpec(memory_space=pltpu.VMEM)] * n,
        scratch_shapes=[pltpu.SemaphoreType.DMA((count,))],
        compiler_params=pltpu.CompilerParams(vmem_limit_bytes=32 * 1024 * 1024),
        cost_estimate=LIGHT,
        name="assemble",
    )(*weights, *got_mine, *got_mate)


class Gather:
    def __init__(self, links, weights):
        self.links, self.weights = links, weights

    def start(self, own):
        self.own = own
        self.held = [{0: lanes_of(self.links, own, p)} for p in range(self.links.bits)]
        self.mine = [own]
        self.mate = [self.links.core(own)]
        self.done = 0
        return own

    def send(self):
        self.arrived = [
            self.links.chip(jnp.stack([pieces[k] for k in sorted(pieces)]), self.bit(part))
            for part, pieces in enumerate(self.held)
        ]

    def bit(self, part):
        return 1 << ((part + self.done) % self.links.bits)

    def absorb(self):
        for part, (pieces, values) in enumerate(zip(self.held, self.arrived)):
            for i, k in enumerate(sorted(pieces)):
                pieces[k ^ self.bit(part)] = values[i]
            self.mine.append(values)
            self.mate.append(self.links.core(values))
        self.done += 1

    def full(self):
        return assemble(self.links, self.weights, self.mine, self.mate)


class Scatter:
    def __init__(self, links, sent, kept):
        self.links = links
        self.rows = [s.shape[2] for s in sent]
        self.lanes = sent[0].shape[3]
        self.got = [links.core(s) for s in sent]
        self.kept = kept
        self.done = 0
        total = sum(self.rows)
        if links.bits == 2 and all(n % 32 == 0 for n in self.rows):
            first = []
            second = []
            taken = 0
            for i, n in enumerate(self.rows):
                cut = min(n, total // 2 - taken)
                if len(self.rows) == 3:
                    cut = (n, 0, n // 2)[i]
                taken += cut
                if cut:
                    first.append((i, 0, cut))
                if cut < n:
                    second.append((i, cut, n))
            self.parts = [first, second]
        else:
            self.parts = None

    def plan(self):
        if self.parts is None:
            return [(i, 0, n) for i, n in enumerate(self.rows)]
        return self.parts[0] + self.parts[1]

    def blocks(self):
        links = self.links
        ns, nq, lanes = links.ns, links.nq, self.lanes
        n = len(self.rows)
        sizes = [sum(high - low for _, low, high in part) for part in self.parts]

        def kernel(*refs):
            kept, got, outs = refs[:n], refs[n : 2 * n], refs[2 * n :]
            q = lax.axis_index("rep") // 2
            for p, part in enumerate(self.parts):
                bit = 1 << p
                for at, k in enumerate([k for k in range(nq) if not k & bit]):
                    for out, chip in ((outs[2 * p], k ^ bit), (outs[2 * p + 1], k)):
                        base = 0
                        for i, low, high in part:
                            a = kept[i][0, q ^ chip, low:high, :].astype(f32)
                            b = got[i][0, q ^ chip, low:high, :].astype(f32)
                            out[at, 0, base : base + high - low, :] = (a + b).astype(bf16)
                            base += high - low

        return pl.pallas_call(
            kernel,
            grid=(ns,),
            in_specs=[pl.BlockSpec((1, nq, r, lanes), lambda j: (j, 0, 0, 0)) for r in self.rows] * 2,
            out_specs=[
                pl.BlockSpec((nq // 2, 1, r, lanes), lambda j: (0, j, 0, 0))
                for r in sizes
                for _ in range(2)
            ],
            out_shape=[
                jax.ShapeDtypeStruct((nq // 2, ns, r, lanes), bf16) for r in sizes for _ in range(2)
            ],
            compiler_params=pltpu.CompilerParams(vmem_limit_bytes=32 * 1024 * 1024),
            cost_estimate=LIGHT,
            name="core_sums",
        )(*self.kept, *self.got)

    def prepare(self):
        links = self.links
        if self.done == 0 and self.parts is not None:
            s0, k0, s1, k1 = self.blocks()
            self.buffers = [s0, s1]
            self.stay = [[0, 2], [0, 1]]
            self.held = [{0: k0[0], 2: k0[1]}, {0: k1[0], 1: k1[1]}]
            return self.buffers
        if self.done == 0:
            _, q, _ = links.here()
            total = sum(self.rows)
            size = total // links.bits
            self.held = []
            both = [a.astype(f32) + b.astype(f32) for a, b in zip(self.kept, self.got)]
            both = jnp.concatenate(both, 2).astype(bf16)
            for p in range(links.bits):
                high = (p + 1) * size if p < links.bits - 1 else total
                cut = both[:, :, p * size : high]
                self.held.append(
                    {k: lax.dynamic_index_in_dim(cut, q ^ k, 1, False) for k in range(links.nq)}
                )
        self.buffers = []
        self.stay = []
        for part, pieces in enumerate(self.held):
            bit = 1 << ((part + self.done) % links.bits)
            stay = [k for k in sorted(pieces) if not k & bit]
            self.stay.append(stay)
            self.buffers.append(jnp.stack([pieces[k ^ bit] for k in stay]))
        return self.buffers

    def send(self):
        self.arrived = [
            self.links.chip(buffer, 1 << ((part + self.done) % self.links.bits))
            for part, buffer in enumerate(self.buffers)
        ]

    def absorb(self):
        last = self.done == self.links.bits - 1 and self.parts is not None
        out = []
        for pieces, got, stay in zip(self.held, self.arrived, self.stay):
            if last:
                out.append((pieces[0], got[0]))
                continue
            out.append(
                {
                    k: (pieces[k].astype(f32) + got[i].astype(f32)).astype(bf16)
                    for i, k in enumerate(stay)
                }
            )
        self.held = out
        self.done += 1

    def join(self, other):
        n = len(self.rows)
        self.held = [
            {k: jnp.concatenate([mine[k], theirs[k]], 1) for k in mine}
            for mine, theirs in zip(self.held, other.held)
        ]
        self.rows = self.rows + other.rows
        self.parts = [
            mine + [(i + n, low, high) for i, low, high in theirs]
            for mine, theirs in zip(self.parts, other.parts)
        ]

    def prepare_along(self, lines=None):
        links = self.links
        ns = links.ns
        if self.parts is not None:
            lanes = self.lanes
            total = sum(self.rows)
            more = 0 if lines is None else lines.shape[1]

            def kernel(a0, b0, a1, b1, *refs):
                outs = refs[-ns:]
                z = lax.axis_index("shard")
                for s, out in enumerate(outs):
                    at = lax.rem(z + s, ns)
                    base = 0
                    for a, b in ((a0, b0), (a1, b1)):
                        n = a.shape[1]
                        out[base : base + n, :] = (a[at].astype(f32) + b[at].astype(f32)).astype(bf16)
                        base += n
                    if more:
                        out[base : base + more, :] = refs[0][at].astype(bf16)

            pairs = [x for pair in self.held for x in pair]
            if more:
                pairs.append(lines)
            self.buffers = pl.pallas_call(
                kernel,
                in_specs=[pl.BlockSpec(memory_space=pltpu.VMEM)] * len(pairs),
                out_specs=[pl.BlockSpec(memory_space=pltpu.VMEM)] * ns,
                out_shape=[jax.ShapeDtypeStruct((total + more, lanes), bf16)] * ns,
                compiler_params=pltpu.CompilerParams(vmem_limit_bytes=32 * 1024 * 1024),
                cost_estimate=LIGHT,
                name="chip_sums",
            )(*pairs)
            return self.buffers
        z, _, _ = links.here()
        total = jnp.concatenate([p[0] for p in self.held], 1)
        self.buffers = [
            lax.dynamic_index_in_dim(total, (z + s) % ns, 0, False) for s in range(ns)
        ]
        return self.buffers

    def send_along(self):
        self.arrived = [
            self.links.along(self.buffers[s], s) for s in range(1, self.links.ns)
        ]

    def settle(self):
        final = self.buffers[0].astype(f32)
        for x in self.arrived:
            final = final + x.astype(f32)
        total = sum(self.rows)
        self.final = final[:total].astype(bf16)
        return final[total:]

    def owned(self):
        links = self.links
        _, q, c = links.here()
        rows = slice(self.base, self.base + sum(self.rows))
        mine = jnp.stack([v[rows] for v in self.mine])
        mate = jnp.stack([v[rows] for v in self.mate])
        both = jnp.stack([jnp.where(c == 0, mine, mate), jnp.where(c == 0, mate, mine)])
        ordered = [lax.dynamic_index_in_dim(both, q ^ j, 1) for j in range(links.nq)]
        full = jnp.concatenate(ordered, 1).astype(f32)
        outs = []
        base = 0
        for n in self.rows:
            outs.append(full[:, :, base : base + n])
            base += n
        return outs


class Spread:
    def __init__(self, links, scatters):
        self.links, self.scatters = links, scatters
        finals = [s.final for s in scatters]
        self.final = jnp.concatenate(finals) if len(finals) > 1 else finals[0]
        self.others = [links.chip(self.final, k) for k in range(1, links.nq)]

    def pair(self):
        mine = [self.final] + self.others
        self.mate = [self.links.core(v) for v in mine]
        base = 0
        for s in self.scatters:
            s.mine, s.mate, s.base = mine, self.mate, base
            base += sum(s.rows)


def owned_by_kernel(links, scatters, shapes, place):
    sides = scatters[0].mine + scatters[0].mate
    nq = links.nq

    def kernel(*refs):
        ins, outs = refs[: len(sides)], refs[len(sides) :]
        rep = lax.axis_index("rep")
        q, first_core = rep // 2, rep % 2 == 0
        for at, scatter in enumerate(scatters):
            for k in range(nq):
                mine, mate = ins[k], ins[nq + k]
                chip = q ^ k
                base = scatter.base
                for i, low, high in scatter.plan():
                    for lo, hi, left, right, out, factor, offset, zero, one in place(at, i):
                        a, b = max(lo, low), min(hi, high)
                        if a >= b:
                            continue
                        r = slice(base + a - low, base + b - low)
                        x, y = mine[r, left:right].astype(f32), mate[r, left:right].astype(f32)
                        row = pl.multiple_of(chip * factor + (offset + a - lo), 8)
                        rows = pl.ds(row, b - a)
                        wide = right - left
                        outs[out][rows, zero : zero + wide] = jnp.where(first_core, x, y)
                        outs[out][rows, one : one + wide] = jnp.where(first_core, y, x)
                    base += high - low

    return pl.pallas_call(
        kernel,
        in_specs=[pl.BlockSpec(memory_space=pltpu.VMEM)] * len(sides),
        out_specs=[pl.BlockSpec(memory_space=pltpu.VMEM)] * len(shapes),
        out_shape=[jax.ShapeDtypeStruct(s, f32) for s in shapes],
        compiler_params=pltpu.CompilerParams(vmem_limit_bytes=48 * 1024 * 1024),
        cost_estimate=LIGHT,
        name="owned",
    )(*sides)


def owned_feed_forward(links, scatter_1, scatter_2, w_up, w_down, w_out):
    lanes = scatter_1.lanes
    block = w_down.shape[0] // 2
    if scatter_1.parts is None or scatter_2.parts is None:
        down_first, up_first = scatter_1.owned()
        down_second, up_second, o_wout = scatter_2.owned()
        o_wdown = jnp.concatenate([side_by_side(down_first, 1), side_by_side(down_second, 1)])
        return o_wdown, up_columns(links, up_first, up_second), side_by_side(o_wout, 1)
    down_rows, up_rows = scatter_1.rows
    rq = w_up.shape[0] // links.nq
    half = block // 2

    def place(at, i):
        if i == 0:
            return [(0, down_rows, 0, lanes, 0, down_rows, at * block, 0, lanes)]
        if i == 2:
            return [(0, rq, 0, lanes, 2, rq, 0, 0, lanes)]
        out = []
        per = lanes // half
        for g in range(up_rows // rq):
            for p in range(per):
                column = (g * per + p) * 2 * block + at * block
                out.append(
                    (g * rq, (g + 1) * rq, p * half, (p + 1) * half, 1, rq, 0, column, column + half)
                )
        return out

    return owned_by_kernel(
        links, [scatter_1, scatter_2], [w_down.shape, w_up.shape, w_out.shape], place
    )


def owned_qkv(links, scatter, w_qkv):
    if scatter.parts is None:
        (grad,) = scatter.owned()
        return side_by_side(grad, 3)
    lanes = scatter.lanes
    rq = w_qkv.shape[0] // links.nq

    def place(at, i):
        return [
            (t * rq, (t + 1) * rq, 0, lanes, 0, rq, 0, 2 * t * lanes, (2 * t + 1) * lanes)
            for t in range(3)
        ]

    return owned_by_kernel(links, [scatter], [w_qkv.shape], place)[0]


def up_columns(links, first, second):
    cores, chips, _, lanes = first.shape
    both = jnp.stack([first, second])
    groups = first.shape[2] * chips * links.ns // (2 * lanes)
    rows = first.shape[2] // groups
    per = links.ns // groups
    both = both.reshape(2, cores, chips, groups, rows, per, lanes // per)
    return both.transpose(2, 4, 3, 5, 0, 1, 6).reshape(chips * rows, -1)


def side_by_side(grad, groups):
    cores, chips, rows, lanes = grad.shape
    grad = grad.reshape(cores, chips, groups, rows // groups, lanes)
    return grad.transpose(1, 3, 2, 0, 4).reshape(chips * rows // groups, groups * cores * lanes)


def total_over_rep(links, lines):
    lines = lines + links.core(lines)
    crossed = [links.chip(lines, k) for k in range(1, links.nq)]
    for x in crossed:
        lines = lines + x
    return lines


def total_over_shard(links, lines):
    z, _, _ = links.here()
    moved = [
        links.along(lax.dynamic_index_in_dim(lines, (z + s) % links.ns, 0, False), s)
        for s in range(1, links.ns)
    ]
    line = lax.dynamic_index_in_dim(lines, z, 0, False)
    for x in moved:
        line = line + x
    return line


def body(
    links,
    inputs,
    counts,
    ln1_gain,
    ln1_shift,
    w_qkv,
    qv_bias,
    w_out,
    out_bias,
    ln2_gain,
    ln2_shift,
    w_up,
    up_bias,
    w_down,
    down_bias,
    cotangent,
):
    ns = links.ns
    slots = inputs.shape[1]
    seq_len = inputs.shape[2]
    width = inputs.shape[3]
    n_rows = slots * seq_len
    z = lax.axis_index("shard")

    small = (ln1_gain, ln1_shift, out_bias, ln2_gain, ln2_shift, down_bias, qv_bias, up_bias)
    sizes = [v.shape[0] for v in small]
    line = w_qkv.shape[1] // 2
    n_lines = -(-sum(sizes) // line)

    gather_a, gather_b, gather_c = (
        Gather(links, [w_qkv]),
        Gather(links, [w_out, w_up]),
        Gather(links, [w_down]),
    )
    n = w_qkv.shape[0] // links.nq
    packed_a = pack(links, w_qkv, small, line)
    got = gather_along(links, packed_a)
    got_small = [g[n : n + n_lines] for g in got]
    own_a = gather_a.start(jnp.stack([g[:n] for g in got]))
    got_b = gather_along(links, tie(piece_of(links, [w_out, w_up]), own_a))
    while gather_a.done < links.bits:
        gather_a.send()
        gather_a.absorb()
    gather_a.mine, got_b = meet(gather_a.mine, got_b)
    (full_qkv,) = gather_a.full()
    got_c = gather_along(links, tie(piece_of(links, [w_down]), got_b))
    gather_b.start(jnp.stack(got_b))
    gather_b.send()
    all_small = jnp.stack([packed_a[n : n + n_lines]] + got_small).reshape(ns, -1)
    all_small = jnp.concatenate(
        [lax.dynamic_index_in_dim(all_small, (z - j) % ns, 0) for j in range(ns)]
    )
    full_small = []
    base = 0
    for n in sizes:
        full_small.append(all_small[:, base : base + n].reshape(-1).astype(f32))
        base += n
    full_g1, full_s1, full_bout, full_g2, full_s2, full_bdown, bias_f, full_bup = full_small
    first_slot = z * slots
    alive = (jnp.arange(slots, dtype=jnp.int32) + first_slot < counts[0]).astype(f32)
    assert slots == 1
    d_out_b = jnp.where(alive[0] > 0, cotangent, jnp.zeros_like(cotangent)).reshape(n_rows, width)
    tokens_b = inputs.reshape(n_rows, width)
    hidden_one_b = layer_norm(tokens_b.astype(f32), full_g1, full_s1).astype(bf16)
    projected = matmul(hidden_one_b, full_qkv)
    none = jnp.zeros((width,), f32)
    qkv_bias = jnp.concatenate([bias_f[:width], none, bias_f[width:]])
    qkv_b = (projected + qkv_bias).astype(bf16)
    pairs = width // (2 * HDIM)
    cuts = (0, pairs * 3 // 8, pairs * 5 // 8, pairs)
    qkv_b, gather_b.arrived = meet(qkv_b, gather_b.arrived)
    gather_b.absorb()
    while gather_b.done < links.bits - 1:
        gather_b.send()
        gather_b.absorb()
    gather_b.send()
    kept = attend(qkv_b, cuts[0], cuts[1])
    kept, gather_b.arrived, got_c = meet(kept, gather_b.arrived, got_c)
    gather_b.absorb()
    gather_c.start(jnp.stack(got_c))
    gather_c.send()
    kept = attend(qkv_b, cuts[1], cuts[2], kept)
    kept, gather_c.arrived = meet(kept, gather_c.arrived)
    gather_c.absorb()
    while gather_c.done < links.bits - 1:
        gather_c.send()
        gather_c.absorb()
    gather_c.send()
    kept = attend(qkv_b, cuts[2], cuts[3], kept)
    kept, gather_c.arrived = meet(kept, gather_c.arrived)
    gather_c.absorb()
    attended_b, inverse, probs_b = kept
    full_wout, full_wup = gather_b.full()
    gain_two = full_g2[None]
    middle, hidden_two_b = middle_of(
        tokens_b, attended_b, full_wout, full_bout[None], gain_two, full_s2[None]
    )
    middle, gather_c.mate = meet(middle, gather_c.mate)
    (full_wdown,) = gather_c.full()
    bias_up = full_bup[None]
    last_bias = full_bdown[None]
    y, g, away, home, gb_first = feed_forward(
        links, hidden_two_b, d_out_b, full_wup, bias_up, full_wdown, alive, last_bias, middle, None, 0
    )
    scatter_1 = Scatter(links, away, home)
    output, g, away, home, gb_second = feed_forward(
        links, hidden_two_b, d_out_b, full_wup, bias_up, full_wdown, alive, last_bias, y, g, 1
    )
    output = output.reshape(inputs.shape)
    grad_bup = jnp.concatenate([gb_first, gb_second], 1)
    g, scatter_1.kept = meet(g, scatter_1.kept)
    scatter_2 = Scatter(links, away, home)
    early = scatter_1.parts is not None
    if early:
        scatter_2.kept, scatter_1.buffers = meet(scatter_2.kept, scatter_1.prepare())
        g, scatter_1.buffers, scatter_2.buffers = meet(
            g, scatter_1.buffers, scatter_2.prepare()
        )
        scatter_2.send()
    else:
        g, scatter_1.buffers = meet(g, scatter_1.prepare())
    scatter_1.send()
    d_mid, d_att_b, out_away, out_home, sums = middle_back(
        links, g, middle, d_out_b, attended_b, full_wout, gain_two
    )
    grad_g2, grad_s2, grad_bout, grad_bdown = (sums[i] for i in range(4))
    if early:
        d_att_b, out_away, out_home = meet(d_att_b, out_away, out_home)
        scatter_o = Scatter(links, [out_away], [out_home])
    else:
        scatter_2 = Scatter(links, away + [out_away], home + [out_home])
        d_att_b, scatter_2.buffers = meet(d_att_b, scatter_2.prepare())
        scatter_2.send()
    thirds = (0, pairs // 2, pairs * 3 // 4, pairs)

    def back(part, before=None):
        low, high = thirds[part], thirds[part + 1]
        return attend_back(
            qkv_b, d_att_b, attended_b, inverse, probs_b, low, high, before
        )

    grads = back(0)
    grads, scatter_1.arrived, scatter_2.arrived = meet(
        grads, scatter_1.arrived, scatter_2.arrived
    )
    scatter_1.absorb()
    scatter_2.absorb()
    for _ in range(links.bits - 2):
        scatter_1.prepare()
        scatter_1.send()
        scatter_1.absorb()
        scatter_2.prepare()
        scatter_2.send()
        scatter_2.absorb()
    if early:
        grads, scatter_1.buffers, scatter_2.held, scatter_o.buffers = meet(
            grads, scatter_1.prepare(), scatter_2.held, scatter_o.prepare()
        )
        scatter_o.send()
    else:
        grads, scatter_1.buffers, scatter_2.buffers = meet(
            grads, scatter_1.prepare(), scatter_2.prepare()
        )
    scatter_1.send()
    grads = back(1, grads)
    if early:
        grads, scatter_1.arrived, scatter_o.arrived = meet(
            grads, scatter_1.arrived, scatter_o.arrived
        )
        scatter_o.absorb()
        scatter_2.join(scatter_o)
        scatter_2.prepare()
    else:
        grads, scatter_1.arrived = meet(grads, scatter_1.arrived)
    scatter_1.absorb()
    grads, scatter_1.buffers, scatter_2.buffers = meet(
        grads, scatter_1.prepare_along(), scatter_2.buffers
    )
    scatter_2.send()
    scatter_1.send_along()
    grads = back(2, grads)
    grads, scatter_2.arrived = meet(grads, scatter_2.arrived)
    scatter_2.absorb()
    grads, scatter_2.buffers = meet(grads, scatter_2.prepare_along())
    scatter_2.send_along()
    d_qkv, qv_sums = grads
    qkv_away, qkv_home = weight_grads(links, hidden_one_b, d_qkv)
    qkv_away, qkv_home, scatter_1.arrived = meet(qkv_away, qkv_home, scatter_1.arrived)
    scatter_3 = Scatter(links, qkv_away, qkv_home)
    scatter_1.settle()
    d_qkv, scatter_3.buffers = meet(d_qkv, scatter_3.prepare())
    scatter_3.send()
    input_grad, entry_sums = entry_back(d_qkv, full_qkv, tokens_b, d_mid, full_g1[None])
    for _ in range(links.bits - 2):
        scatter_3.absorb()
        scatter_3.prepare()
        scatter_3.send()
    input_grad, entry_sums, scatter_3.arrived, scatter_2.arrived = meet(
        input_grad, entry_sums, scatter_3.arrived, scatter_2.arrived
    )
    scatter_3.absorb()
    scatter_3.prepare()
    scatter_3.send()
    scatter_2.settle()
    input_grad = input_grad.reshape(inputs.shape)
    grad_g1, grad_s1 = entry_sums[0], entry_sums[1]
    grad_qvb = qv_sums.reshape(-1)
    small_grads = (grad_g1, grad_s1, grad_bout, grad_g2, grad_s2, grad_bdown, grad_qvb, grad_bup)
    joined = jnp.concatenate([g.reshape(ns, -1) for g in small_grads], 1)
    n_small = joined.shape[1]
    ride = scatter_3.parts is not None and n_small % scatter_3.lanes == 0
    if ride:
        joined = joined.reshape(ns, -1, scatter_3.lanes)
        joined = jnp.pad(joined, ((0, 0), (0, -joined.shape[1] % 8), (0, 0)))
    joined = total_over_rep(links, joined)
    scatter_3.arrived, scatter_1.final, scatter_2.final = meet(
        scatter_3.arrived, scatter_1.final, scatter_2.final
    )
    scatter_3.absorb()
    if ride:
        scatter_3.prepare_along(joined)
    else:
        scatter_3.prepare_along()
        joined = total_over_shard(links, joined)
    scatter_3.send_along()
    spread_12 = Spread(links, [scatter_1, scatter_2])
    scatter_3.arrived, spread_12.others = meet(scatter_3.arrived, spread_12.others)
    arrived_lines = scatter_3.settle()
    spread_3 = Spread(links, [scatter_3])
    spread_12.pair()
    o_wdown, o_wup, o_wout = owned_feed_forward(links, scatter_1, scatter_2, w_up, w_down, w_out)
    if ride:
        joined = arrived_lines.reshape(-1)[:n_small]
    joined, o_wdown, o_wup, o_wout, spread_3.others = meet(
        joined, o_wdown, o_wup, o_wout, spread_3.others
    )
    spread_3.pair()
    o_qkv = owned_qkv(links, scatter_3, w_qkv)
    owned = []
    base = 0
    for n in sizes:
        owned.append(joined[base : base + n])
        base += n
    o_g1, o_s1, o_bout, o_g2, o_s2, o_bdown, o_qvb, o_bup = owned
    return (
        output,
        input_grad,
        o_g1,
        o_s1,
        o_qkv,
        o_qvb,
        o_wout,
        o_bout,
        o_g2,
        o_s2,
        o_wup,
        o_bup,
        o_wdown,
        o_bdown,
    )


def solution(mesh):
    tokens = P("rep", "shard", None, None)
    vector = P("shard")
    matrix = P("shard", None)
    return jax.shard_map(
        functools.partial(body, Links(mesh)),
        mesh=mesh,
        in_specs=(
            tokens,
            P("rep"),
            vector,
            vector,
            matrix,
            vector,
            matrix,
            vector,
            vector,
            vector,
            matrix,
            vector,
            matrix,
            vector,
            tokens,
        ),
        out_specs=(
            tokens,
            tokens,
            vector,
            vector,
            matrix,
            vector,
            matrix,
            vector,
            vector,
            vector,
            matrix,
            vector,
            matrix,
            vector,
        ),
        check_vma=False,
    )
```

```python
import functools

import jax
import jax.numpy as jnp
from jax import lax
from jax.experimental import pallas as pl
from jax.experimental.pallas import tpu as pltpu
from jax.sharding import PartitionSpec as P

HDIM = 64

eps = 1e-06
bf16 = jnp.bfloat16
LIGHT = pl.CostEstimate(flops=1, transcendentals=0, bytes_accessed=1)
HEAVY = pl.CostEstimate(flops=20_000_000_000, transcendentals=0, bytes_accessed=10_000_000)
f32 = jnp.float32


def layer_norm(values, gain, shift):
    centre = values - jnp.mean(values, -1, keepdims=True)
    spread = jnp.mean(centre * centre, -1, keepdims=True)
    return centre * lax.rsqrt(spread + eps) * gain + shift


def matmul(left, right):
    return jnp.dot(left, right, preferred_element_type=f32)


LOG2E = 1.4426950408889634


def contract(left, right, left_dim, right_dim):
    return lax.dot_general(
        left, right, (((left_dim,), (right_dim,)), ((), ())), preferred_element_type=f32
    )


def query_blocks(rows, tile=256):
    return [(i, min(tile, rows - i)) for i in range(0, rows, tile)]


def head_mask(head, rows, dtype):
    lane = lax.broadcasted_iota(jnp.int32, (rows, 2 * HDIM), 1)
    return (lane // HDIM == head).astype(dtype)


def attend_kernel(q_ref, k_ref, v_ref, o_ref, inv_ref, p_ref):
    rows = q_ref.shape[0]
    factor = HDIM ** (-0.5) * LOG2E
    keys = k_ref[...]
    values = v_ref[...]
    ones = jnp.ones(values.shape, bf16)
    for start, n in query_blocks(rows):
        queries = q_ref[start : start + n, :]
        mixed = inverse = None
        for head in range(2):
            mask = head_mask(head, rows, bf16)
            scores = contract(keys * mask, queries, 1, 1)
            largest = jnp.max(scores, axis=0, keepdims=True)
            probs = jnp.exp2((scores - largest) * factor).astype(bf16)
            p_ref[head, :, start : start + n] = probs
            both = contract(probs, jnp.concatenate([values * mask, ones], 1), 0, 0)
            inv = 1.0 / both[:, 2 * HDIM :]
            part = both[:, : 2 * HDIM] * inv
            share = head_mask(head, n, f32) * inv
            mixed = part if mixed is None else mixed + part
            inverse = share if inverse is None else inverse + share
        o_ref[start : start + n, :] = mixed.astype(bf16)
        inv_ref[start : start + n, :] = inverse


def whole(count):
    return [pl.BlockSpec(memory_space=pl.ANY)] * count


def attend(qkv, first, last, before=None):
    rows, wide = qkv.shape
    width = wide // 3
    pairs = width // (2 * HDIM)
    count = last - first

    def column(offset):
        return pl.BlockSpec((rows, 2 * HDIM), lambda j: (0, offset + first + j))

    def kernel(*refs):
        attend_kernel(*refs[:3], *refs[-3:])

    given = () if before is None else tuple(before)
    return pl.pallas_call(
        kernel,
        grid=(count,),
        in_specs=[column(0), column(pairs), column(2 * pairs)] + whole(len(given)),
        out_specs=[
            column(0),
            column(0),
            pl.BlockSpec((2, rows, rows), lambda j: (first + j, 0, 0)),
        ],
        out_shape=[
            jax.ShapeDtypeStruct((rows, width), bf16),
            jax.ShapeDtypeStruct((rows, width), f32),
            jax.ShapeDtypeStruct((2 * pairs, rows, rows), bf16),
        ],
        input_output_aliases={3 + i: i for i in range(len(given))},
        compiler_params=pltpu.CompilerParams(vmem_limit_bytes=56 * 1024 * 1024),
        cost_estimate=HEAVY,
        name="attend",
    )(qkv, qkv, qkv, *given)


def attend_back_kernel(
    q_ref, k_ref, v_ref, d_ref, o_ref, inv_ref, p_ref, out_ref, sum_ref
):
    rows = q_ref.shape[0]
    scale = HDIM ** (-0.5)
    queries = q_ref[...]
    keys = k_ref[...]
    values = v_ref[...]
    grads = (d_ref[...].astype(f32) * inv_ref[...]).astype(bf16)
    product = grads.astype(f32) * o_ref[...].astype(f32)
    lane = lax.broadcasted_iota(jnp.int32, (rows, 2 * HDIM), 1)
    blocks = query_blocks(rows)
    d_queries = [None] * len(blocks)
    d_keys = d_values = None
    for head in range(2):
        mask = head_mask(head, rows, bf16)
        inner = -jnp.sum(jnp.where(lane // HDIM == head, product, 0.0), 1, keepdims=True)
        high = inner.astype(bf16)
        low = (inner - high.astype(f32)).astype(bf16)
        tail = jnp.where(lane == 0, high, jnp.where(lane == 1, low, jnp.zeros_like(low)))
        grads_wide = jnp.concatenate([grads, tail], 1)
        values_wide = jnp.concatenate([values * mask, (lane < 2).astype(bf16)], 1)
        keys_h, queries_h, grads_h = keys * mask, queries * mask, grads * mask
        for b, (start, n) in enumerate(blocks):
            d_probs = contract(values_wide, grads_wide[start : start + n, :], 1, 1)
            probs = p_ref[head, :, start : start + n]
            d_scores = probs * d_probs.astype(bf16)
            to_values = contract(probs, grads_h[start : start + n, :], 1, 0)
            to_keys = contract(d_scores, queries_h[start : start + n, :], 1, 0)
            to_queries = contract(d_scores, keys_h, 0, 0)
            d_values = to_values if d_values is None else d_values + to_values
            d_keys = to_keys if d_keys is None else d_keys + to_keys
            d_queries[b] = to_queries if d_queries[b] is None else d_queries[b] + to_queries
    d_values = d_values.astype(bf16)
    out_ref[1] = (d_keys * scale).astype(bf16)
    out_ref[2] = d_values
    sums = jnp.zeros((1, 2 * HDIM), f32)
    for b, (start, n) in enumerate(blocks):
        block = (d_queries[b] * scale).astype(bf16)
        out_ref[0, start : start + n, :] = block
        sums = sums + jnp.sum(block.astype(f32), 0, keepdims=True)
    sum_ref[0] = sums
    sum_ref[1] = jnp.sum(d_values.astype(f32), 0, keepdims=True)


def attend_back(qkv, grad, attended, inverse, probs, first, last, before=None):
    rows, wide = qkv.shape
    width = wide // 3
    pairs = width // (2 * HDIM)
    count = last - first

    def column(offset):
        return pl.BlockSpec((rows, 2 * HDIM), lambda j: (0, offset + first + j))

    def kernel(*refs):
        attend_back_kernel(*refs[:7], *refs[-2:])

    given = () if before is None else tuple(before)
    return pl.pallas_call(
        kernel,
        grid=(count,),
        in_specs=[column(0), column(pairs), column(2 * pairs)]
        + [column(0)] * 3
        + [pl.BlockSpec((2, rows, rows), lambda j: (first + j, 0, 0))]
        + whole(len(given)),
        out_specs=[
            pl.BlockSpec((3, rows, 2 * HDIM), lambda j: (0, 0, first + j)),
            pl.BlockSpec((2, 1, 2 * HDIM), lambda j: (0, 0, first + j)),
        ],
        out_shape=[
            jax.ShapeDtypeStruct((3, rows, width), bf16),
            jax.ShapeDtypeStruct((2, 1, width), f32),
        ],
        input_output_aliases={7 + i: i for i in range(len(given))},
        compiler_params=pltpu.CompilerParams(vmem_limit_bytes=56 * 1024 * 1024),
        cost_estimate=LIGHT if first == 0 else HEAVY,
        name="attend_back",
    )(qkv, qkv, qkv, grad, attended, inverse, probs, *given)


def gelu_pair(values):
    bell = jnp.exp2(values * values * (-0.5 * LOG2E))
    t = 1.0 / (1.0 + 0.23164189 * jnp.abs(values))
    poly = 0.5307027145 * t - 0.7265760135
    poly = poly * t + 0.7107068705
    poly = poly * t - 0.142248368
    poly = poly * t + 0.127414796
    tail = poly * t * bell
    area = jnp.where(values >= 0, 1.0 - tail, tail)
    return values * area, area + values * bell * 0.3989422804014327


def feed_forward_kernel(
    h_ref, dm_ref, up_ref, bias_ref, down_ref, alive_ref, last_ref, y0_ref, g0_ref,
    y_ref, g_ref, down_away, down_home, up_away, up_home, gb_ref,
    act_ref, dp_ref, y_acc, g_acc, out_ref, sems,
):
    j = pl.program_id(0)
    final = g0_ref is not None
    given = [pltpu.make_async_copy(y0_ref, y_acc, sems.at[0])]
    if final:
        given.append(pltpu.make_async_copy(g0_ref, g_acc, sems.at[1]))
    made = [
        pltpu.make_async_copy(out_ref if final else y_acc, y_ref, sems.at[2]),
        pltpu.make_async_copy(g_acc, g_ref, sems.at[3]),
    ]

    @pl.when(j == 0)
    def _():
        for copy in given:
            copy.start()
        if not final:
            g_acc[...] = jnp.zeros_like(g_acc)

    rows = h_ref.shape[0]
    up, down = up_ref[...], down_ref[...]
    bias = bias_ref[...]
    chunk = 368
    for start in range(0, rows, chunk):
        r = slice(start, min(start + chunk, rows))
        act, slope = gelu_pair(contract(h_ref[r, :], up, 1, 0) + bias)
        act = act.astype(bf16)
        act_ref[r, :] = act
        d_pre = (contract(dm_ref[r, :], down, 1, 1) * slope).astype(bf16)
        dp_ref[r, :] = d_pre
        if start == 0:

            @pl.when(j == 0)
            def _():
                for copy in given:
                    copy.wait()

        y_acc[r, :] += contract(act, down, 1, 0)
        g_acc[r, :] += contract(d_pre, up, 1, 1)

    @pl.when(j == pl.num_programs(0) - 1)
    def _():
        if final:
            out_ref[...] = (alive_ref[0] * (y_acc[...] + last_ref[...])).astype(bf16)
        for copy in made:
            copy.start()

    gb_ref[...] = jnp.sum(dp_ref[...].astype(f32), 0, keepdims=True)[None]
    first_core = lax.axis_index("rep") % 2 == 0
    for left, right, away, home in (
        (act_ref, dm_ref, down_away, down_home),
        (h_ref, dp_ref, up_away, up_home),
    ):
        grad = contract(left[...], right[...], 0, 0)
        half = grad.shape[1] // 2
        low, high = grad[:, :half], grad[:, half:]
        away[...] = jnp.where(first_core, high, low).reshape(away.shape).astype(bf16)
        home[...] = jnp.where(first_core, low, high).reshape(home.shape).astype(bf16)

    @pl.when(j == pl.num_programs(0) - 1)
    def _():
        for copy in made:
            copy.wait()


def feed_forward(links, hidden, d_out, up, bias, down, alive, last_bias, y0, g0, part):
    ns, nq = links.ns, links.nq
    rows, width = hidden.shape
    block = up.shape[1] // (2 * ns)
    rq = width // (ns * nq)
    per = width // block
    wide = dict(pipeline_mode=pl.Buffered(1))

    def full():
        return pl.BlockSpec((rows, width), lambda j: (0, 0), **wide)

    def kernel(*refs):
        refs = list(refs)
        if g0 is None:
            refs.insert(8, None)
        feed_forward_kernel(*refs)

    down_spec = pl.BlockSpec((1, block, width // 2), lambda j: (j, 0, 0))
    up_spec = pl.BlockSpec((ns, nq, 1, rq, block // 2), lambda j: (0, 0, j // per, 0, j % per))
    down_shape = jax.ShapeDtypeStruct((ns, block, width // 2), bf16)
    up_shape = jax.ShapeDtypeStruct((ns, nq, ns // per, rq, width // 2), bf16)
    sums = jax.ShapeDtypeStruct((rows, width), f32)
    given = (y0,) if g0 is None else (y0, g0)
    y, g, d_away, d_home, u_away, u_home, gb = pl.pallas_call(
        kernel,
        grid=(ns,),
        in_specs=[
            full(),
            full(),
            pl.BlockSpec((width, block), lambda j: (0, 2 * j + part)),
            pl.BlockSpec((1, block), lambda j: (0, 2 * j + part)),
            pl.BlockSpec((block, width), lambda j: (2 * j + part, 0)),
            pl.BlockSpec(memory_space=pltpu.SMEM),
            pl.BlockSpec((1, width), lambda j: (0, 0)),
        ]
        + whole(len(given)),
        out_specs=whole(2)
        + [
            down_spec,
            down_spec,
            up_spec,
            up_spec,
            pl.BlockSpec((1, 1, block), lambda j: (j, 0, 0)),
        ],
        out_shape=[
            sums if g0 is None else jax.ShapeDtypeStruct((rows, width), bf16),
            sums,
            down_shape,
            down_shape,
            up_shape,
            up_shape,
            jax.ShapeDtypeStruct((ns, 1, block), f32),
        ],
        scratch_shapes=[
            pltpu.VMEM((rows, block), bf16),
            pltpu.VMEM((rows, block), bf16),
            pltpu.VMEM((rows, width), f32),
            pltpu.VMEM((rows, width), f32),
            pltpu.VMEM((rows, width), bf16),
            pltpu.SemaphoreType.DMA((4,)),
        ],
        compiler_params=pltpu.CompilerParams(vmem_limit_bytes=50 * 1024 * 1024),
        cost_estimate=HEAVY,
        name="feed_forward",
    )(hidden, d_out, up, bias, down, alive, last_bias, *given)

    def pieces(down_grad, up_grad):
        lanes = width // 2
        return [
            down_grad.reshape(ns, nq, block // nq, lanes),
            up_grad.reshape(ns, nq, ns // per * rq, lanes),
        ]

    return y, g, pieces(d_away, u_away), pieces(d_home, u_home), gb.reshape(ns, block)


def grad_kernel(left_ref, right_ref, away_ref, home_ref):
    grad = contract(left_ref[...], right_ref[0], 0, 0)
    half = grad.shape[1] // 2
    low, high = grad[:, :half], grad[:, half:]
    first_core = lax.axis_index("rep") % 2 == 0
    away_ref[...] = jnp.where(first_core, high, low).reshape(away_ref.shape).astype(bf16)
    home_ref[...] = jnp.where(first_core, low, high).reshape(home_ref.shape).astype(bf16)


def weight_grads(links, left, rights, first, count):
    ns, nq = links.ns, links.nq
    rows, width = left.shape
    wide = rights.shape[2]
    rq = width // (ns * nq)
    spec = pl.BlockSpec((ns, nq, 1, rq, wide // 2), lambda i: (0, 0, i, 0, 0))
    shape = jax.ShapeDtypeStruct((ns, nq, count, rq, wide // 2), bf16)
    away, home = pl.pallas_call(
        grad_kernel,
        grid=(count,),
        in_specs=[
            pl.BlockSpec((rows, width), lambda i: (0, 0)),
            pl.BlockSpec((1, rows, wide), lambda i: (first + i, 0, 0)),
        ],
        out_specs=[spec, spec],
        out_shape=[shape, shape],
        compiler_params=pltpu.CompilerParams(vmem_limit_bytes=48 * 1024 * 1024),
        cost_estimate=HEAVY,
        name="weight_grads",
    )(left, rights)
    flat = (ns, nq, count * rq, wide // 2)
    return away.reshape(flat), home.reshape(flat)


def row_block(rows):
    return 368 if rows % 368 == 0 else rows


def normal(values):
    centre = values - jnp.mean(values, -1, keepdims=True)
    scale = lax.rsqrt(jnp.mean(centre * centre, -1, keepdims=True) + eps)
    return centre * scale, scale


def normal_back(unit, scale, grad):
    inner = jnp.mean(grad * unit, -1, keepdims=True)
    return scale * (grad - jnp.mean(grad, -1, keepdims=True) - unit * inner)


def column_sum(values):
    return jnp.sum(values, 0, keepdims=True)


def middle_kernel(x_ref, att_ref, w_ref, bias_ref, gain_ref, shift_ref, mid_ref, h_ref):
    mid = x_ref[...].astype(f32) + contract(att_ref[...], w_ref[...], 1, 0) + bias_ref[...]
    mid_ref[...] = mid
    unit, _ = normal(mid)
    h_ref[...] = (unit * gain_ref[...] + shift_ref[...]).astype(bf16)


def middle_of(tokens, attended, weight, bias, gain, shift):
    rows, width = tokens.shape
    n = row_block(rows)
    block = pl.BlockSpec((n, width), lambda i: (i, 0))
    line = pl.BlockSpec((1, width), lambda i: (0, 0))
    return pl.pallas_call(
        middle_kernel,
        grid=(rows // n,),
        in_specs=[block, block, pl.BlockSpec(weight.shape, lambda i: (0, 0)), line, line, line],
        out_specs=[block, block],
        out_shape=[
            jax.ShapeDtypeStruct((rows, width), f32),
            jax.ShapeDtypeStruct((rows, width), bf16),
        ],
        compiler_params=pltpu.CompilerParams(vmem_limit_bytes=48 * 1024 * 1024),
        cost_estimate=HEAVY,
        name="middle",
    )(tokens, attended, weight, bias, gain, shift)


def middle_back_kernel(
    g_ref, mid_ref, dm_ref, att_ref, w_ref, gain_ref,
    d_mid_ref, d_att_ref, away_ref, home_ref, sum_ref, acc_ref,
):
    i = pl.program_id(0)

    @pl.when(i == 0)
    def _():
        acc_ref[...] = jnp.zeros_like(acc_ref)
        sum_ref[...] = jnp.zeros_like(sum_ref)

    unit, scale = normal(mid_ref[...])
    g = g_ref[...]
    d_out = dm_ref[...].astype(f32)
    d_mid = d_out + normal_back(unit, scale, g * gain_ref[...])
    d_mid_ref[...] = d_mid
    d_proj = d_mid.astype(bf16)
    d_att_ref[...] = contract(d_proj, w_ref[...], 1, 1).astype(bf16)
    acc_ref[...] += contract(att_ref[...], d_proj, 0, 0)
    sum_ref[0:1, :] += column_sum(g * unit)
    sum_ref[1:2, :] += column_sum(g)
    sum_ref[2:3, :] += column_sum(d_proj.astype(f32))
    sum_ref[3:4, :] += column_sum(d_out)

    @pl.when(i == pl.num_programs(0) - 1)
    def _():
        grad = acc_ref[...]
        half = grad.shape[1] // 2
        low, high = grad[:, :half], grad[:, half:]
        first_core = lax.axis_index("rep") % 2 == 0
        away_ref[...] = jnp.where(first_core, high, low).reshape(away_ref.shape).astype(bf16)
        home_ref[...] = jnp.where(first_core, low, high).reshape(home_ref.shape).astype(bf16)


def middle_back(links, grad, middle, d_out, attended, weight, gain):
    ns, nq = links.ns, links.nq
    rows, width = middle.shape
    n = row_block(rows)
    block = pl.BlockSpec((n, width), lambda i: (i, 0))
    pieces = (ns, nq, width // (ns * nq), width // 2)
    whole_piece = pl.BlockSpec(pieces, lambda i: (0, 0, 0, 0))
    return pl.pallas_call(
        middle_back_kernel,
        grid=(rows // n,),
        in_specs=[block] * 4
        + [
            pl.BlockSpec(weight.shape, lambda i: (0, 0)),
            pl.BlockSpec((1, width), lambda i: (0, 0)),
        ],
        out_specs=[
            block,
            block,
            whole_piece,
            whole_piece,
            pl.BlockSpec((8, width), lambda i: (0, 0)),
        ],
        out_shape=[
            jax.ShapeDtypeStruct((rows, width), f32),
            jax.ShapeDtypeStruct((rows, width), bf16),
            jax.ShapeDtypeStruct(pieces, bf16),
            jax.ShapeDtypeStruct(pieces, bf16),
            jax.ShapeDtypeStruct((8, width), f32),
        ],
        scratch_shapes=[pltpu.VMEM((width, width), f32)],
        compiler_params=pltpu.CompilerParams(vmem_limit_bytes=48 * 1024 * 1024),
        cost_estimate=HEAVY,
        name="middle_back",
    )(grad, middle, d_out, attended, weight, gain)


def entry_back_kernel(d_ref, w_ref, x_ref, d_mid_ref, gain_ref, out_ref, sum_ref):
    @pl.when(pl.program_id(0) == 0)
    def _():
        sum_ref[...] = jnp.zeros_like(sum_ref)

    width = x_ref.shape[1]
    g = contract(d_ref[0], w_ref[:, :width], 1, 1)
    for t in range(1, 3):
        g = g + contract(d_ref[t], w_ref[:, t * width : (t + 1) * width], 1, 1)
    unit, scale = normal(x_ref[...].astype(f32))
    out_ref[...] = d_mid_ref[...] + normal_back(unit, scale, g * gain_ref[...])
    sum_ref[0:1, :] += column_sum(g * unit)
    sum_ref[1:2, :] += column_sum(g)


def entry_back(grads, weight, tokens, d_mid, gain):
    rows, width = tokens.shape
    n = row_block(rows)
    block = pl.BlockSpec((n, width), lambda i: (i, 0))
    return pl.pallas_call(
        entry_back_kernel,
        grid=(rows // n,),
        in_specs=[
            pl.BlockSpec((3, n, width), lambda i: (0, i, 0)),
            pl.BlockSpec(weight.shape, lambda i: (0, 0), pipeline_mode=pl.Buffered(1)),
            block,
            block,
            pl.BlockSpec((1, width), lambda i: (0, 0)),
        ],
        out_specs=[block, pl.BlockSpec((8, width), lambda i: (0, 0))],
        out_shape=[
            jax.ShapeDtypeStruct((rows, width), f32),
            jax.ShapeDtypeStruct((8, width), f32),
        ],
        compiler_params=pltpu.CompilerParams(vmem_limit_bytes=48 * 1024 * 1024),
        cost_estimate=pl.CostEstimate(flops=6_000_000_000, transcendentals=0, bytes_accessed=1),
        name="entry_back",
    )(grads, weight, tokens, d_mid, gain)


class Links:
    def __init__(self, mesh):
        self.ns = mesh.shape["shard"]
        self.nr = mesh.shape["rep"]
        self.nq = self.nr // 2
        self.bits = self.nq.bit_length() - 1
        assert 1 << self.bits == self.nq

    def here(self):
        rep = lax.axis_index("rep")
        return lax.axis_index("shard"), rep // 2, rep % 2

    def along(self, values, step):
        return lax.ppermute(values, "shard", [(i, (i + step) % self.ns) for i in range(self.ns)])

    def chip(self, values, k):
        return lax.ppermute(values, "rep", [(i, i ^ (2 * k)) for i in range(self.nr)])

    def core(self, values):
        return lax.ppermute(values, "rep", [(i, i ^ 1) for i in range(self.nr)])


def meet(*values):
    return lax.optimization_barrier(values)


def tie(values, others):
    return lax.optimization_barrier((values, others))[0]


def piece_of(links, weights):
    _, q, c = links.here()
    parts = []
    for w in weights:
        rq, half = w.shape[0] // links.nq, w.shape[1] // 2
        parts.append(lax.dynamic_slice(w, (q * rq, c * half), (rq, half)))
    return jnp.concatenate(parts, 1)


def pack(links, weight, small, line):
    rq = weight.shape[0] // links.nq
    total = sum(v.shape[0] for v in small)
    fits = all(sum(v.shape[0] for v in part) == line for part in (small[:6], small[6:]))
    if rq % 16 or line % 128 or not fits:
        filled = jnp.concatenate(small + (jnp.zeros((-total % line,), bf16),)).reshape(-1, line)
        filler = jnp.zeros((16 - filled.shape[0], line), bf16)
        return jnp.concatenate([piece_of(links, [weight]), filled, filler])

    def kernel(w_ref, *refs):
        *vectors, out_ref, sem = refs
        rep = lax.axis_index("rep")
        q, c = rep // 2, rep % 2
        rows = pl.ds(pl.multiple_of(q * rq, rq), rq)
        copy = pltpu.make_async_copy(
            w_ref.at[rows, pl.ds(pl.multiple_of(c * line, line), line)], out_ref.at[:rq], sem
        )
        copy.start()
        lines = [[], []]
        for at, ref in enumerate(vectors):
            lines[at // 6].append(ref[...].astype(f32).reshape(1, -1))
        block = [jnp.concatenate(x, 1) for x in lines]
        row = lax.broadcasted_iota(jnp.int32, (16, line), 0)
        filled = jnp.where(row == 0, block[0], jnp.where(row == 1, block[1], 0.0))
        out_ref[rq:, :] = filled.astype(bf16)
        copy.wait()

    return pl.pallas_call(
        kernel,
        in_specs=whole(1) + [pl.BlockSpec(memory_space=pltpu.VMEM)] * len(small),
        out_specs=pl.BlockSpec(memory_space=pltpu.VMEM),
        out_shape=jax.ShapeDtypeStruct((rq + 16, line), bf16),
        scratch_shapes=[pltpu.SemaphoreType.DMA(())],
        cost_estimate=LIGHT,
        name="pack",
    )(weight, *small)


def gather_along(links, piece):
    return [links.along(piece, s) for s in range(1, links.ns)]


def lanes_of(links, values, part):
    n = values.shape[-1] // links.bits
    return values[..., part * n : (part + 1) * n]


def assemble(links, weights, got_mine, got_mate, through):
    ns, nq, bits = links.ns, links.nq, links.bits
    rows = [w.shape[0] for w in weights]
    cols = [w.shape[1] for w in weights]
    rq = [r // nq for r in rows]
    total = sum(cols) // 2
    lanes = total // bits
    n = len(weights)
    per_side = len(got_mine)

    def kernel(*refs):
        w_refs = refs[:n]
        sides = (refs[n : n + per_side], refs[n + per_side : n + 2 * per_side])
        final_refs = refs[n + 2 * per_side : n + 2 * per_side + n]
        out_refs = refs[n + 2 * per_side + n :][:n] if through else final_refs
        sem = refs[-1]
        z = lax.axis_index("shard")
        rep = lax.axis_index("rep")
        q, c = rep // 2, rep % 2
        copies = []
        by_step = [[] for _ in range(ns)]

        def go(src, dst, s=0):
            copy = pltpu.make_async_copy(src, dst, sem.at[len(copies)])
            copy.start()
            copies.append(copy)
            by_step[s].append(copy)

        for i in range(n):
            go(w_refs[i], out_refs[i].at[pl.ds(pl.multiple_of(z * rows[i], rows[i]), rows[i]), :])
        for side, parts in enumerate(sides):
            core = c if side == 0 else 1 - c
            base = 0
            for i in range(n):
                half = cols[i] // 2

                def place(source, k, s, low, high):
                    zs = lax.rem(z + (ns - s), ns)
                    at = pl.ds(pl.multiple_of(zs * rows[i] + (q ^ k) * rq[i], rq[i]), rq[i])
                    to = pl.ds(pl.multiple_of(core * half + (low - base), 128), high - low)
                    go(source, out_refs[i].at[at, to], s)

                for s in range(1, ns):
                    own = parts[0].at[s - 1, :, pl.ds(base, half)]
                    place(own, 0, s, base, base + half)
                    at = 1
                    for step in range(bits):
                        for part in range(bits):
                            known = [0]
                            for t in range(step):
                                bit = 1 << ((part + t) % bits)
                                known = known + [k ^ bit for k in known]
                            known = sorted(known)
                            bit = 1 << ((part + step) % bits)
                            low = max(base, part * lanes)
                            high = min(base + half, (part + 1) * lanes)
                            if low < high:
                                cut = pl.ds(low - part * lanes, high - low)
                                for j, k in enumerate(known):
                                    source = parts[at].at[j, s - 1, :, cut]
                                    place(source, k ^ bit, s, low, high)
                            at += 1
                base += half
        onward = []
        for s in range(ns):
            for copy in by_step[s]:
                copy.wait()
            if through:
                zs = lax.rem(z + (ns - s), ns)
                for i in range(n):
                    at = pl.ds(pl.multiple_of(zs * rows[i], rows[i]), rows[i])
                    move = pltpu.make_async_copy(
                        out_refs[i].at[at, :],
                        final_refs[i].at[at, :],
                        sem.at[len(copies) + len(onward)],
                    )
                    move.start()
                    onward.append(move)
        for move in onward:
            move.wait()

    pieces = 0
    base = 0
    for i in range(n):
        half = cols[i] // 2
        for part in range(bits):
            if max(base, part * lanes) < min(base + half, (part + 1) * lanes):
                pieces += nq - 1
        pieces += 1
        base += half
    count = n + 2 * (ns - 1) * pieces
    return pl.pallas_call(
        kernel,
        out_shape=[jax.ShapeDtypeStruct((ns * r, c), bf16) for r, c in zip(rows, cols)],
        in_specs=whole(n + 2 * per_side),
        out_specs=[
            pl.BlockSpec(memory_space=pltpu.MemorySpace.HBM if through else pltpu.VMEM)
        ]
        * n,
        scratch_shapes=[
            pltpu.VMEM((ns * r, c), bf16) for r, c in zip(rows, cols) if through
        ]
        + [pltpu.SemaphoreType.DMA((count + ns * n,))],
        compiler_params=pltpu.CompilerParams(vmem_limit_bytes=32 * 1024 * 1024),
        cost_estimate=LIGHT,
        name="assemble",
    )(*weights, *got_mine, *got_mate)


class Gather:
    def __init__(self, links, weights):
        self.links, self.weights = links, weights

    def start(self, own):
        self.own = own
        self.held = [{0: lanes_of(self.links, own, p)} for p in range(self.links.bits)]
        self.mine = [own]
        self.mate = [self.links.core(own)]
        self.done = 0
        return own

    def send(self):
        self.arrived = [
            self.links.chip(jnp.stack([pieces[k] for k in sorted(pieces)]), self.bit(part))
            for part, pieces in enumerate(self.held)
        ]

    def bit(self, part):
        return 1 << ((part + self.done) % self.links.bits)

    def absorb(self):
        for part, (pieces, values) in enumerate(zip(self.held, self.arrived)):
            for i, k in enumerate(sorted(pieces)):
                pieces[k ^ self.bit(part)] = values[i]
            self.mine.append(values)
            self.mate.append(self.links.core(values))
        self.done += 1

    def full(self, through=True):
        return assemble(self.links, self.weights, self.mine, self.mate, through)


class Scatter:
    def __init__(self, links, sent, kept):
        self.links = links
        self.rows = [s.shape[2] for s in sent]
        self.lanes = sent[0].shape[3]
        self.got = [links.core(s) for s in sent]
        self.kept = kept
        self.done = 0
        total = sum(self.rows)
        if links.bits == 2 and all(n % 32 == 0 for n in self.rows):
            first = []
            second = []
            taken = 0
            for i, n in enumerate(self.rows):
                cut = min(n, total // 2 - taken)
                if len(self.rows) == 3:
                    cut = (n, 0, n // 2)[i]
                taken += cut
                if cut:
                    first.append((i, 0, cut))
                if cut < n:
                    second.append((i, cut, n))
            self.parts = [first, second]
        else:
            self.parts = None

    def plan(self):
        if self.parts is None:
            return [(i, 0, n) for i, n in enumerate(self.rows)]
        return self.parts[0] + self.parts[1]

    def blocks(self):
        links = self.links
        ns, nq, lanes = links.ns, links.nq, self.lanes
        n = len(self.rows)
        sizes = [sum(high - low for _, low, high in part) for part in self.parts]

        def kernel(*refs):
            kept, got, outs = refs[:n], refs[n : 2 * n], refs[2 * n :]
            q = lax.axis_index("rep") // 2
            for p, part in enumerate(self.parts):
                bit = 1 << p
                for at, k in enumerate([k for k in range(nq) if not k & bit]):
                    for out, chip in ((outs[2 * p], k ^ bit), (outs[2 * p + 1], k)):
                        base = 0
                        for i, low, high in part:
                            a = kept[i][0, q ^ chip, low:high, :].astype(f32)
                            b = got[i][0, q ^ chip, low:high, :].astype(f32)
                            out[at, 0, base : base + high - low, :] = (a + b).astype(bf16)
                            base += high - low

        return pl.pallas_call(
            kernel,
            grid=(ns,),
            in_specs=[pl.BlockSpec((1, nq, r, lanes), lambda j: (j, 0, 0, 0)) for r in self.rows] * 2,
            out_specs=[
                pl.BlockSpec((nq // 2, 1, r, lanes), lambda j: (0, j, 0, 0))
                for r in sizes
                for _ in range(2)
            ],
            out_shape=[
                jax.ShapeDtypeStruct((nq // 2, ns, r, lanes), bf16) for r in sizes for _ in range(2)
            ],
            compiler_params=pltpu.CompilerParams(vmem_limit_bytes=32 * 1024 * 1024),
            cost_estimate=LIGHT,
            name="core_sums",
        )(*self.kept, *self.got)

    def prepare(self):
        links = self.links
        if self.done == 0 and self.parts is not None:
            s0, k0, s1, k1 = self.blocks()
            self.buffers = [s0, s1]
            self.stay = [[0, 2], [0, 1]]
            self.held = [{0: k0[0], 2: k0[1]}, {0: k1[0], 1: k1[1]}]
            return self.buffers
        if self.done == 0:
            _, q, _ = links.here()
            total = sum(self.rows)
            size = total // links.bits
            self.held = []
            both = [a.astype(f32) + b.astype(f32) for a, b in zip(self.kept, self.got)]
            both = jnp.concatenate(both, 2).astype(bf16)
            for p in range(links.bits):
                high = (p + 1) * size if p < links.bits - 1 else total
                cut = both[:, :, p * size : high]
                self.held.append(
                    {k: lax.dynamic_index_in_dim(cut, q ^ k, 1, False) for k in range(links.nq)}
                )
        self.buffers = []
        self.stay = []
        for part, pieces in enumerate(self.held):
            bit = 1 << ((part + self.done) % links.bits)
            stay = [k for k in sorted(pieces) if not k & bit]
            self.stay.append(stay)
            self.buffers.append(jnp.stack([pieces[k ^ bit] for k in stay]))
        return self.buffers

    def send(self):
        self.arrived = [
            self.links.chip(buffer, 1 << ((part + self.done) % self.links.bits))
            for part, buffer in enumerate(self.buffers)
        ]

    def absorb(self):
        last = self.done == self.links.bits - 1 and self.parts is not None
        out = []
        for pieces, got, stay in zip(self.held, self.arrived, self.stay):
            if last:
                out.append((pieces[0], got[0]))
                continue
            out.append(
                {
                    k: (pieces[k].astype(f32) + got[i].astype(f32)).astype(bf16)
                    for i, k in enumerate(stay)
                }
            )
        self.held = out
        self.done += 1

    def join(self, other):
        n = len(self.rows)
        self.held = [
            {k: jnp.concatenate([mine[k], theirs[k]], 1) for k in mine}
            for mine, theirs in zip(self.held, other.held)
        ]
        self.rows = self.rows + other.rows
        self.parts = [
            mine + [(i + n, low, high) for i, low, high in theirs]
            for mine, theirs in zip(self.parts, other.parts)
        ]

    def prepare_along(self, lines=None):
        links = self.links
        ns = links.ns
        if self.parts is not None:
            lanes = self.lanes
            total = sum(self.rows)
            more = 0 if lines is None else lines.shape[1]

            def kernel(a0, b0, a1, b1, *refs):
                outs = refs[-ns:]
                z = lax.axis_index("shard")
                for s, out in enumerate(outs):
                    at = lax.rem(z + s, ns)
                    base = 0
                    for a, b in ((a0, b0), (a1, b1)):
                        n = a.shape[1]
                        out[base : base + n, :] = (a[at].astype(f32) + b[at].astype(f32)).astype(bf16)
                        base += n
                    if more:
                        out[base : base + more, :] = refs[0][at].astype(bf16)

            pairs = [x for pair in self.held for x in pair]
            if more:
                pairs.append(lines)
            self.buffers = pl.pallas_call(
                kernel,
                in_specs=[pl.BlockSpec(memory_space=pltpu.VMEM)] * len(pairs),
                out_specs=[pl.BlockSpec(memory_space=pltpu.VMEM)] * ns,
                out_shape=[jax.ShapeDtypeStruct((total + more, lanes), bf16)] * ns,
                compiler_params=pltpu.CompilerParams(vmem_limit_bytes=32 * 1024 * 1024),
                cost_estimate=LIGHT,
                name="chip_sums",
            )(*pairs)
            return self.buffers
        z, _, _ = links.here()
        total = jnp.concatenate([p[0] for p in self.held], 1)
        self.buffers = [
            lax.dynamic_index_in_dim(total, (z + s) % ns, 0, False) for s in range(ns)
        ]
        return self.buffers

    def send_along(self):
        self.arrived = [
            self.links.along(self.buffers[s], s) for s in range(1, self.links.ns)
        ]

    def settle(self):
        final = self.buffers[0].astype(f32)
        for x in self.arrived:
            final = final + x.astype(f32)
        total = sum(self.rows)
        self.final = final[:total].astype(bf16)
        return final[total:]

    def owned(self):
        links = self.links
        _, q, c = links.here()
        rows = slice(self.base, self.base + sum(self.rows))
        mine = jnp.stack([v[rows] for v in self.mine])
        mate = jnp.stack([v[rows] for v in self.mate])
        both = jnp.stack([jnp.where(c == 0, mine, mate), jnp.where(c == 0, mate, mine)])
        ordered = [lax.dynamic_index_in_dim(both, q ^ j, 1) for j in range(links.nq)]
        full = jnp.concatenate(ordered, 1).astype(f32)
        outs = []
        base = 0
        for n in self.rows:
            outs.append(full[:, :, base : base + n])
            base += n
        return outs


class Spread:
    def __init__(self, links, scatters):
        self.links, self.scatters = links, scatters
        finals = [s.final for s in scatters]
        self.final = jnp.concatenate(finals) if len(finals) > 1 else finals[0]
        self.others = [links.chip(self.final, k) for k in range(1, links.nq)]

    def pair(self):
        mine = [self.final] + self.others
        self.mate = [self.links.core(v) for v in mine]
        base = 0
        for s in self.scatters:
            s.mine, s.mate, s.base = mine, self.mate, base
            base += sum(s.rows)


def owned_by_kernel(links, scatters, shapes, place):
    sides = scatters[0].mine + scatters[0].mate
    nq = links.nq

    def kernel(*refs):
        ins, outs = refs[: len(sides)], refs[len(sides) :]
        rep = lax.axis_index("rep")
        q, first_core = rep // 2, rep % 2 == 0
        for at, scatter in enumerate(scatters):
            for k in range(nq):
                mine, mate = ins[k], ins[nq + k]
                chip = q ^ k
                base = scatter.base
                for i, low, high in scatter.plan():
                    for lo, hi, left, right, out, factor, offset, zero, one in place(at, i):
                        a, b = max(lo, low), min(hi, high)
                        if a >= b:
                            continue
                        r = slice(base + a - low, base + b - low)
                        x, y = mine[r, left:right].astype(f32), mate[r, left:right].astype(f32)
                        row = pl.multiple_of(chip * factor + (offset + a - lo), 8)
                        rows = pl.ds(row, b - a)
                        wide = right - left
                        outs[out][rows, zero : zero + wide] = jnp.where(first_core, x, y)
                        outs[out][rows, one : one + wide] = jnp.where(first_core, y, x)
                    base += high - low

    return pl.pallas_call(
        kernel,
        in_specs=[pl.BlockSpec(memory_space=pltpu.VMEM)] * len(sides),
        out_specs=[pl.BlockSpec(memory_space=pltpu.VMEM)] * len(shapes),
        out_shape=[jax.ShapeDtypeStruct(s, f32) for s in shapes],
        compiler_params=pltpu.CompilerParams(vmem_limit_bytes=48 * 1024 * 1024),
        cost_estimate=LIGHT,
        name="owned",
    )(*sides)


def owned_feed_forward(links, scatter_1, scatter_2, w_up, w_down, w_out):
    lanes = scatter_1.lanes
    block = w_down.shape[0] // 2
    if scatter_1.parts is None or scatter_2.parts is None:
        down_first, up_first = scatter_1.owned()
        down_second, up_second, o_wout = scatter_2.owned()
        o_wdown = jnp.concatenate([side_by_side(down_first, 1), side_by_side(down_second, 1)])
        return o_wdown, up_columns(links, up_first, up_second), side_by_side(o_wout, 1)
    down_rows, up_rows = scatter_1.rows
    rq = w_up.shape[0] // links.nq
    half = block // 2

    def place(at, i):
        if i == 0:
            return [(0, down_rows, 0, lanes, 0, down_rows, at * block, 0, lanes)]
        if i == 2:
            return [(0, rq, 0, lanes, 2, rq, 0, 0, lanes)]
        out = []
        per = lanes // half
        for g in range(up_rows // rq):
            for p in range(per):
                column = (g * per + p) * 2 * block + at * block
                out.append(
                    (g * rq, (g + 1) * rq, p * half, (p + 1) * half, 1, rq, 0, column, column + half)
                )
        return out

    return owned_by_kernel(
        links, [scatter_1, scatter_2], [w_down.shape, w_up.shape, w_out.shape], place
    )


def owned_qkv(links, scatter, w_qkv):
    if scatter.parts is None:
        return side_by_side(jnp.concatenate(scatter.owned(), 2), 3)
    lanes = scatter.lanes
    rq = w_qkv.shape[0] // links.nq

    def place(at, i):
        return [
            (n * rq, (n + 1) * rq, 0, lanes, 0, rq, 0, 2 * t * lanes, (2 * t + 1) * lanes)
            for n, t in enumerate(range(3))
        ]

    return owned_by_kernel(links, [scatter], [w_qkv.shape], place)[0]


def up_columns(links, first, second):
    cores, chips, _, lanes = first.shape
    both = jnp.stack([first, second])
    groups = first.shape[2] * chips * links.ns // (2 * lanes)
    rows = first.shape[2] // groups
    per = links.ns // groups
    both = both.reshape(2, cores, chips, groups, rows, per, lanes // per)
    return both.transpose(2, 4, 3, 5, 0, 1, 6).reshape(chips * rows, -1)


def side_by_side(grad, groups):
    cores, chips, rows, lanes = grad.shape
    grad = grad.reshape(cores, chips, groups, rows // groups, lanes)
    return grad.transpose(1, 3, 2, 0, 4).reshape(chips * rows // groups, groups * cores * lanes)


def total_over_rep(links, lines):
    lines = lines + links.core(lines)
    crossed = [links.chip(lines, k) for k in range(1, links.nq)]
    for x in crossed:
        lines = lines + x
    return lines


def total_over_shard(links, lines):
    z, _, _ = links.here()
    moved = [
        links.along(lax.dynamic_index_in_dim(lines, (z + s) % links.ns, 0, False), s)
        for s in range(1, links.ns)
    ]
    line = lax.dynamic_index_in_dim(lines, z, 0, False)
    for x in moved:
        line = line + x
    return line


def body(
    links,
    inputs,
    counts,
    ln1_gain,
    ln1_shift,
    w_qkv,
    qv_bias,
    w_out,
    out_bias,
    ln2_gain,
    ln2_shift,
    w_up,
    up_bias,
    w_down,
    down_bias,
    cotangent,
):
    ns = links.ns
    slots = inputs.shape[1]
    seq_len = inputs.shape[2]
    width = inputs.shape[3]
    n_rows = slots * seq_len
    z = lax.axis_index("shard")

    small = (ln1_gain, ln1_shift, out_bias, ln2_gain, ln2_shift, down_bias, qv_bias, up_bias)
    sizes = [v.shape[0] for v in small]
    line = w_qkv.shape[1] // 2
    n_lines = -(-sum(sizes) // line)

    gather_a, gather_b, gather_c = (
        Gather(links, [w_qkv]),
        Gather(links, [w_out, w_up]),
        Gather(links, [w_down]),
    )
    n = w_qkv.shape[0] // links.nq
    packed_a = pack(links, w_qkv, small, line)
    got = gather_along(links, packed_a)
    got_small = [g[n : n + n_lines] for g in got]
    own_a = gather_a.start(jnp.stack([g[:n] for g in got]))
    got_b = gather_along(links, tie(piece_of(links, [w_out, w_up]), own_a))
    while gather_a.done < links.bits:
        gather_a.send()
        gather_a.absorb()
    gather_a.mine, got_b = meet(gather_a.mine, got_b)
    (full_qkv,) = gather_a.full(False)
    got_c = gather_along(links, tie(piece_of(links, [w_down]), got_b))
    gather_b.start(jnp.stack(got_b))
    gather_b.send()
    all_small = jnp.stack([packed_a[n : n + n_lines]] + got_small).reshape(ns, -1)
    all_small = jnp.concatenate(
        [lax.dynamic_index_in_dim(all_small, (z - j) % ns, 0) for j in range(ns)]
    )
    full_small = []
    base = 0
    for n in sizes:
        full_small.append(all_small[:, base : base + n].reshape(-1).astype(f32))
        base += n
    full_g1, full_s1, full_bout, full_g2, full_s2, full_bdown, bias_f, full_bup = full_small
    first_slot = z * slots
    alive = (jnp.arange(slots, dtype=jnp.int32) + first_slot < counts[0]).astype(f32)
    assert slots == 1
    d_out_b = jnp.where(alive[0] > 0, cotangent, jnp.zeros_like(cotangent)).reshape(n_rows, width)
    tokens_b = inputs.reshape(n_rows, width)
    hidden_one_b = layer_norm(tokens_b.astype(f32), full_g1, full_s1).astype(bf16)
    projected = matmul(hidden_one_b, full_qkv)
    none = jnp.zeros((width,), f32)
    qkv_bias = jnp.concatenate([bias_f[:width], none, bias_f[width:]])
    qkv_b = (projected + qkv_bias).astype(bf16)
    pairs = width // (2 * HDIM)
    cuts = (0, pairs * 3 // 8, pairs * 5 // 8, pairs)
    qkv_b, gather_b.arrived = meet(qkv_b, gather_b.arrived)
    gather_b.absorb()
    while gather_b.done < links.bits - 1:
        gather_b.send()
        gather_b.absorb()
    gather_b.send()
    kept = attend(qkv_b, cuts[0], cuts[1])
    kept, gather_b.arrived, got_c = meet(kept, gather_b.arrived, got_c)
    gather_b.absorb()
    gather_c.start(jnp.stack(got_c))
    gather_c.send()
    kept = attend(qkv_b, cuts[1], cuts[2], kept)
    kept, gather_c.arrived = meet(kept, gather_c.arrived)
    gather_c.absorb()
    while gather_c.done < links.bits - 1:
        gather_c.send()
        gather_c.absorb()
    gather_c.send()
    kept = attend(qkv_b, cuts[2], cuts[3], kept)
    kept, gather_c.arrived = meet(kept, gather_c.arrived)
    gather_c.absorb()
    attended_b, inverse, probs_b = kept
    full_wout, full_wup = gather_b.full()
    gain_two = full_g2[None]
    middle, hidden_two_b = middle_of(
        tokens_b, attended_b, full_wout, full_bout[None], gain_two, full_s2[None]
    )
    middle, gather_c.mate = meet(middle, gather_c.mate)
    (full_wdown,) = gather_c.full()
    bias_up = full_bup[None]
    last_bias = full_bdown[None]
    y, g, away, home, gb_first = feed_forward(
        links, hidden_two_b, d_out_b, full_wup, bias_up, full_wdown, alive, last_bias, middle, None, 0
    )
    scatter_1 = Scatter(links, away, home)
    output, g, away, home, gb_second = feed_forward(
        links, hidden_two_b, d_out_b, full_wup, bias_up, full_wdown, alive, last_bias, y, g, 1
    )
    output = output.reshape(inputs.shape)
    grad_bup = jnp.concatenate([gb_first, gb_second], 1)
    g, scatter_1.kept = meet(g, scatter_1.kept)
    scatter_2 = Scatter(links, away, home)
    early = scatter_1.parts is not None
    if early:
        scatter_2.kept, scatter_1.buffers = meet(scatter_2.kept, scatter_1.prepare())
        g, scatter_1.buffers, scatter_2.buffers = meet(
            g, scatter_1.buffers, scatter_2.prepare()
        )
        scatter_2.send()
    else:
        g, scatter_1.buffers = meet(g, scatter_1.prepare())
    scatter_1.send()
    d_mid, d_att_b, out_away, out_home, sums = middle_back(
        links, g, middle, d_out_b, attended_b, full_wout, gain_two
    )
    grad_g2, grad_s2, grad_bout, grad_bdown = (sums[i] for i in range(4))
    if early:
        d_att_b, out_away, out_home = meet(d_att_b, out_away, out_home)
        scatter_o = Scatter(links, [out_away], [out_home])
    else:
        scatter_2 = Scatter(links, away + [out_away], home + [out_home])
        d_att_b, scatter_2.buffers = meet(d_att_b, scatter_2.prepare())
        scatter_2.send()
    thirds = (0, pairs // 2, pairs * 3 // 4, pairs)

    def back(part, before=None):
        low, high = thirds[part], thirds[part + 1]
        return attend_back(
            qkv_b, d_att_b, attended_b, inverse, probs_b, low, high, before
        )

    grads = back(0)
    grads, scatter_1.arrived, scatter_2.arrived = meet(
        grads, scatter_1.arrived, scatter_2.arrived
    )
    scatter_1.absorb()
    scatter_2.absorb()
    for _ in range(links.bits - 2):
        scatter_1.prepare()
        scatter_1.send()
        scatter_1.absorb()
        scatter_2.prepare()
        scatter_2.send()
        scatter_2.absorb()
    if early:
        grads, scatter_1.buffers, scatter_2.held, scatter_o.buffers = meet(
            grads, scatter_1.prepare(), scatter_2.held, scatter_o.prepare()
        )
        scatter_o.send()
    else:
        grads, scatter_1.buffers, scatter_2.buffers = meet(
            grads, scatter_1.prepare(), scatter_2.prepare()
        )
    scatter_1.send()
    grads = back(1, grads)
    if early:
        grads, scatter_1.arrived, scatter_o.arrived = meet(
            grads, scatter_1.arrived, scatter_o.arrived
        )
        scatter_o.absorb()
        scatter_2.join(scatter_o)
        scatter_2.prepare()
    else:
        grads, scatter_1.arrived = meet(grads, scatter_1.arrived)
    scatter_1.absorb()
    grads, scatter_1.buffers, scatter_2.buffers = meet(
        grads, scatter_1.prepare_along(), scatter_2.buffers
    )
    scatter_2.send()
    scatter_1.send_along()
    grads = back(2, grads)
    grads, scatter_2.arrived = meet(grads, scatter_2.arrived)
    scatter_2.absorb()
    grads, scatter_2.buffers = meet(grads, scatter_2.prepare_along())
    scatter_2.send_along()
    d_qkv, qv_sums = grads
    qkv_away, qkv_home = weight_grads(links, hidden_one_b, d_qkv, 0, 3)
    qkv_away, qkv_home, scatter_1.arrived = meet(qkv_away, qkv_home, scatter_1.arrived)
    scatter_3 = Scatter(links, [qkv_away], [qkv_home])
    scatter_1.settle()
    d_qkv, scatter_3.buffers = meet(d_qkv, scatter_3.prepare())
    scatter_3.send()
    input_grad, entry_sums = entry_back(d_qkv, full_qkv, tokens_b, d_mid, full_g1[None])
    for _ in range(links.bits - 2):
        scatter_3.absorb()
        scatter_3.prepare()
        scatter_3.send()
    input_grad, entry_sums, scatter_3.arrived, scatter_2.arrived = meet(
        input_grad, entry_sums, scatter_3.arrived, scatter_2.arrived
    )
    scatter_3.absorb()
    scatter_3.prepare()
    scatter_3.send()
    scatter_2.settle()
    input_grad = input_grad.reshape(inputs.shape)
    grad_g1, grad_s1 = entry_sums[0], entry_sums[1]
    grad_qvb = qv_sums.reshape(-1)
    small_grads = (grad_g1, grad_s1, grad_bout, grad_g2, grad_s2, grad_bdown, grad_qvb, grad_bup)
    joined = jnp.concatenate([g.reshape(ns, -1) for g in small_grads], 1)
    n_small = joined.shape[1]
    ride = scatter_3.parts is not None and n_small % scatter_3.lanes == 0
    if ride:
        joined = joined.reshape(ns, -1, scatter_3.lanes)
        joined = jnp.pad(joined, ((0, 0), (0, -joined.shape[1] % 8), (0, 0)))
    joined = total_over_rep(links, joined)
    scatter_3.arrived, scatter_1.final, scatter_2.final = meet(
        scatter_3.arrived, scatter_1.final, scatter_2.final
    )
    scatter_3.absorb()
    if ride:
        scatter_3.prepare_along(joined)
    else:
        scatter_3.prepare_along()
        joined = total_over_shard(links, joined)
    scatter_3.send_along()
    spread_12 = Spread(links, [scatter_1, scatter_2])
    scatter_3.arrived, spread_12.others = meet(scatter_3.arrived, spread_12.others)
    arrived_lines = scatter_3.settle()
    spread_3 = Spread(links, [scatter_3])
    spread_12.pair()
    o_wdown, o_wup, o_wout = owned_feed_forward(links, scatter_1, scatter_2, w_up, w_down, w_out)
    if ride:
        joined = arrived_lines.reshape(-1)[:n_small]
    owned = []
    base = 0
    for n in sizes:
        owned.append(joined[base : base + n])
        base += n
    owned, o_wdown, o_wup, o_wout, spread_3.others = meet(
        owned, o_wdown, o_wup, o_wout, spread_3.others
    )
    spread_3.pair()
    o_qkv = owned_qkv(links, scatter_3, w_qkv)
    o_g1, o_s1, o_bout, o_g2, o_s2, o_bdown, o_qvb, o_bup = owned
    return (
        output,
        input_grad,
        o_g1,
        o_s1,
        o_qkv,
        o_qvb,
        o_wout,
        o_bout,
        o_g2,
        o_s2,
        o_wup,
        o_bup,
        o_wdown,
        o_bdown,
    )


def solution(mesh):
    tokens = P("rep", "shard", None, None)
    vector = P("shard")
    matrix = P("shard", None)
    return jax.shard_map(
        functools.partial(body, Links(mesh)),
        mesh=mesh,
        in_specs=(
            tokens,
            P("rep"),
            vector,
            vector,
            matrix,
            vector,
            matrix,
            vector,
            vector,
            vector,
            matrix,
            vector,
            matrix,
            vector,
            tokens,
        ),
        out_specs=(
            tokens,
            tokens,
            vector,
            vector,
            matrix,
            vector,
            matrix,
            vector,
            vector,
            vector,
            matrix,
            vector,
            matrix,
            vector,
        ),
        check_vma=False,
    )
```
